256 devices in a mesh: req: 32 (over y, x, core), head: 8 (over z).
Axes of the slice: x: 4, y: 4, z: 8, core: 2. Of those that a mesh axis runs over, the one named last changes fastest.
Arguments:
- tokens: bfloat16 [4096, 1536], P(('req', 'head')), may hold values from -6 to 6
- pre_gain: float32 [1536], replicated, may hold values from 0.1 to 1.9
- inner_weight: bfloat16 [1536, 2, 3072], P(None, None, 'head')
- shared_weight: bfloat16 [1536, 304], replicated, may hold values from -0.15625 to 0.15625
- conv_inner: float32 [4, 3072], P(None, 'head'), may hold values from -0.5 to 0.5
- conv_inner_bias: float32 [3072], P('head'), may hold values from -0.5 to 0.5
- conv_shared: float32 [4, 256], replicated, may hold values from -0.5 to 0.5
- conv_shared_bias: float32 [256], replicated, may hold values from -0.5 to 0.5
- step_bias: float32 [48], P('head'), may hold values from -4 to 0
- decay_log: float32 [48], P('head'), may hold values from 0 to 2.77
- skip_gain: float32 [48], P('head'), may hold values from 0.5 to 1.5
- gate_gain: float32 [3072], P('head'), may hold values from 0.1 to 1.9
- out_weight: bfloat16 [3072, 1536], P('head'), may hold values from -0.109375 to 0.109375
- states: bfloat16 [1024, 48, 64, 128], P('req', 'head'), may hold values from -1.1953125 to 1.1953125
- edge_inner: bfloat16 [1024, 3, 3072], P('req', None, 'head'), may hold values from -6 to 6
- edge_shared: bfloat16 [1024, 3, 256], P('req'), may hold values from -6 to 6
- counts: int32 [1024], P('req'), may hold values from 1 to 4, as said below
- mig_ids: int32 [32], replicated, may hold values from 0 to 1023, as said below
- mig_dest: int32 [32], replicated, may hold values from 0 to 1023, as said below
- reorder: int32 [1024], replicated, may hold values from 0 to 1023, as said below
Outputs:
- hidden_out: bfloat16 [4096, 1536], P(('req', 'head'))
- states_out: bfloat16 [1024, 48, 64, 128], P('req', 'head')
- edge_inner_out: bfloat16 [1024, 3, 3072], P('req', None, 'head')
- edge_shared_out: bfloat16 [1024, 3, 256], P('req')
The draws below stay inside these ranges and needn't reach their ends.
Inputs may be any that keep to these rules, and one draw needn't show every extreme that they name: counts: each slot's token rows are r * 4 to r * 4 + 3 of tokens; the first counts[r] of them are real. mig_ids: distinct old slots listed by owner: entry i is one of the slots i * 32 to (i + 1) * 32 - 1, those held by index i of req. mig_dest: a reordering of the slots in mig_ids. reorder: a permutation of all slots. The 32 new slots j with j // 32 = d take at most 1 values reorder[j] of any one block of 32 slots, and exactly 1 of some block.
All inputs are finite; a program needn't handle non-finite values.
Results may differ from the reference program's by a relative error of at most 0.013.
Values may be sent and summed in bfloat16 or wider, within the bound.
A program may use at most 128 MiB of HBM per device.

```python
import math
import jax
import jax.numpy as jnp
from jax import lax

D = 1536
HEADS = 48
HEAD_DIM = 64
STATE = 128
CONV = 4
TMAX = 4
REQ_DEV = 32
MIG_DEV = 1
INNER = 3072
REQUESTS = 1024


def draw_inner_weight(key, part):
    columns = jnp.arange(HEADS * HEAD_DIM, dtype=jnp.float32) / (HEADS * HEAD_DIM)
    values = jax.random.normal(key, (D, 2, HEADS * HEAD_DIM), jnp.float32)
    factor = jnp.exp(math.log(3.0) * (columns - 0.5))
    return (values * factor * (1.0 / math.sqrt(D))).astype(jnp.bfloat16)


def migration_lists(key):
    folded = jax.random.fold_in(key, 17)
    first_key, second_key = jax.random.split(folded)
    groups = REQUESTS // REQ_DEV

    def choose_local(member):
        return jax.random.permutation(member, REQ_DEV)[:MIG_DEV]
    chosen = jax.vmap(choose_local)(jax.random.split(first_key, groups))
    listed = (jnp.arange(groups, dtype=jnp.int32)[:, None] * REQ_DEV + chosen.astype(jnp.int32)).reshape(-1)
    shuffled = listed[jax.random.permutation(second_key, groups * MIG_DEV)]
    return (listed.astype(jnp.int32), shuffled.astype(jnp.int32))


def draw_mig_ids(key, part):
    return migration_lists(key)[0]


def draw_mig_dest(key, part):
    return migration_lists(key)[1]


def draw_reorder(key, part):
    groups = REQUESTS // REQ_DEV
    first_key, second_key = jax.random.split(jax.random.fold_in(key, 3))

    def local_order(member):
        return jax.random.permutation(member, REQ_DEV).astype(jnp.int32)
    picked = jax.vmap(local_order)(jax.random.split(first_key, groups))
    placed = jax.vmap(local_order)(jax.random.split(second_key, groups))
    owners = jnp.arange(groups, dtype=jnp.int32)[:, None]
    if REQ_DEV < groups:
        spacing = groups // REQ_DEV
        offsets = jnp.where(picked == 0, groups - 1, picked * spacing).astype(jnp.int32)
    else:
        offsets = (picked % groups).astype(jnp.int32)
    source_owner = (owners + offsets) % groups
    source_local = placed[source_owner, picked]
    return (source_owner * REQ_DEV + source_local).reshape(-1).astype(jnp.int32)


def draw_counts(key, part):
    first_key, second_key, third_key = jax.random.split(jax.random.fold_in(key, 5), 3)
    levels = jax.random.randint(first_key, (REQUESTS,), 0, 16)
    result = 1 + (levels >= 8).astype(jnp.int32) + (levels >= 12).astype(jnp.int32) + (levels >= 14).astype(jnp.int32)
    longest_at = jax.random.randint(second_key, (), 0, REQUESTS)
    shortest_at = (longest_at + 1 + jax.random.randint(third_key, (), 0, REQUESTS - 1)) % REQUESTS
    result = result.at[longest_at].set(TMAX).at[shortest_at].set(1)
    return result.astype(jnp.int32)


def shard_levels(key, shape, cuts, low, largest):
    gain = 1.0
    for axis_at, blocks in cuts:
        draws = jax.random.uniform(jax.random.fold_in(jax.random.fold_in(key, 6), axis_at), (blocks,), jnp.float32, low / len(cuts), largest / len(cuts))
        gain = gain * jnp.repeat(jnp.exp(draws), shape[axis_at] // blocks).reshape((-1,) + (1,) * (len(shape) - 1 - axis_at))
    return gain


def scatter_about(stream_key, shape, scale, most, cuts=(), held_as=jnp.bfloat16):
    values = jax.random.normal(stream_key, shape, jnp.float32) * scale
    if len(cuts) > 0:
        values = shard_levels(stream_key, shape, cuts, -0.22, 0.18) * values
    return jnp.clip(values, min=-most, max=most).astype(held_as)


def setup_inputs(seed: int = 0) -> dict:
    keys = jax.random.split(jax.random.key(seed), 21)
    return {
        "tokens": scatter_about(keys[0], (REQUESTS * TMAX, D), 1.0, 6.0, ((0, 256),)),
        "pre_gain": jnp.clip(1.0 + 0.18 * jax.random.normal(keys[1], (D,), jnp.float32), 0.1, 1.9),
        "inner_weight": draw_inner_weight(jax.random.fold_in(keys[20], 71), 0),
        "shared_weight": scatter_about(keys[3], (D, 2 * STATE + HEADS), D ** -0.5, 0.15625),
        "conv_inner": jnp.clip(jax.random.uniform(keys[4], (CONV, INNER), jnp.float32, -0.5, 0.5) * shard_levels(keys[4], (CONV, INNER), ((1, 8),), -0.4, 0.0), -0.5, 0.5),
        "conv_inner_bias": jnp.clip(jax.random.uniform(keys[5], (INNER,), jnp.float32, -0.5, 0.5) * shard_levels(keys[5], (INNER,), ((0, 8),), -0.4, 0.0), -0.5, 0.5),
        "conv_shared": jnp.clip(jax.random.uniform(keys[6], (CONV, 2 * STATE), jnp.float32, -0.5, 0.5), -0.5, 0.5),
        "conv_shared_bias": jnp.clip(jax.random.uniform(keys[7], (2 * STATE,), jnp.float32, -0.5, 0.5), -0.5, 0.5),
        "step_bias": jnp.clip(-4.0 + 4.0 * jax.random.uniform(keys[8], (HEADS,), jnp.float32) ** shard_levels(keys[8], (HEADS,), ((0, 8),), -0.2, 0.2), -4.0, 0.0),
        "decay_log": jnp.clip(2.77 * jax.random.uniform(keys[9], (HEADS,), jnp.float32) ** shard_levels(keys[9], (HEADS,), ((0, 8),), -0.2, 0.2), 0.0, 2.77),
        "skip_gain": jnp.clip(0.5 + 1.0 * jax.random.uniform(keys[10], (HEADS,), jnp.float32) ** shard_levels(keys[10], (HEADS,), ((0, 8),), -0.2, 0.2), 0.5, 1.5),
        "gate_gain": jnp.clip(1.0 + 0.18 * jax.random.normal(keys[11], (INNER,), jnp.float32), 0.1, 1.9),
        "out_weight": scatter_about(keys[12], (INNER, D), INNER ** -0.5, 0.109375, ((0, 8),)),
        "states": scatter_about(keys[13], (REQUESTS, HEADS, HEAD_DIM, STATE), 0.2, 1.1953125, ((0, 32), (1, 8))),
        "edge_inner": scatter_about(keys[14], (REQUESTS, CONV - 1, INNER), 1.0, 6.0, ((0, 32), (2, 8))),
        "edge_shared": scatter_about(keys[15], (REQUESTS, CONV - 1, 2 * STATE), 1.0, 6.0, ((0, 32),)),
        "counts": draw_counts(jax.random.fold_in(keys[20], 71), 0),
        "mig_ids": draw_mig_ids(jax.random.fold_in(keys[20], 71), 0),
        "mig_dest": draw_mig_dest(jax.random.fold_in(keys[20], 71), 0),
        "reorder": draw_reorder(jax.random.fold_in(keys[20], 71), 0),
    }


EPS = 1e-05

def advance(carried, step_now, inputs_now, entry_now, readout_now, decay, skip_gain):
    factor = jnp.exp(step_now * decay)
    carried = carried * factor[:, :, None, None] + (step_now[:, :, None] * inputs_now)[:, :, :, None] * entry_now[:, None, None, :]
    produced = jnp.einsum('khpn,kn->khp', carried, readout_now, precision=lax.Precision.HIGHEST)
    return (carried, produced + skip_gain[None, :, None] * inputs_now)

def depthwise(edge, fresh, weight, offset_bias):
    sequence = jnp.concatenate([edge, fresh], axis=1).astype(jnp.float32)
    window = fresh.shape[1]
    summed = sequence[:, 0:window] * weight[0]
    for offset in range(1, weight.shape[0]):
        summed = summed + sequence[:, offset:offset + window] * weight[offset]
    return jax.nn.silu(summed + offset_bias)

def new_edge(edge, fresh, counts):
    sequence = jnp.concatenate([edge, fresh], axis=1)
    keep_rows = edge.shape[1]
    result = edge
    for length in range(1, fresh.shape[1] + 1):
        result = jnp.where((counts == length)[:, None, None], sequence[:, length:length + keep_rows], result)
    return result

def reference(tokens, pre_gain, inner_weight, shared_weight, conv_inner, conv_inner_bias, conv_shared, conv_shared_bias, step_bias, decay_log, skip_gain, gate_gain, out_weight, states, edge_inner, edge_shared, counts, mig_ids, mig_dest, reorder):
    all_slots = jnp.arange(REQUESTS, dtype=jnp.int32)
    source = all_slots.at[mig_dest].set(mig_ids)
    anchor = source[reorder]
    moved_states = states[anchor]
    moved_inner = edge_inner[anchor]
    moved_shared = edge_shared[anchor]
    rows_in = tokens.astype(jnp.float32)
    normed = (rows_in * lax.rsqrt(lax.optimization_barrier(jnp.mean(rows_in * rows_in, axis=-1, keepdims=True)) + EPS) * pre_gain).astype(jnp.bfloat16)
    gate_part = jnp.dot(normed, inner_weight[:, 0, :], preferred_element_type=jnp.float32).astype(jnp.bfloat16)
    value_part = jnp.dot(normed, inner_weight[:, 1, :], preferred_element_type=jnp.float32).astype(jnp.bfloat16)
    shared_part = jnp.dot(normed, shared_weight, preferred_element_type=jnp.float32).astype(jnp.bfloat16)
    gate_part = gate_part.reshape(REQUESTS, TMAX, INNER)
    value_part = value_part.reshape(REQUESTS, TMAX, INNER)
    shared_part = shared_part.reshape(REQUESTS, TMAX, 2 * STATE + HEADS)
    fresh_shared = shared_part[:, :, :2 * STATE]
    edge_inner_out = new_edge(moved_inner, value_part, counts)
    edge_shared_out = new_edge(moved_shared, fresh_shared, counts)
    mixed_inner = depthwise(moved_inner, value_part, conv_inner, conv_inner_bias)
    mixed_shared = depthwise(moved_shared, fresh_shared, conv_shared, conv_shared_bias)
    valid = jnp.arange(TMAX)[None, :] < counts[:, None]
    step_size = jax.nn.softplus(shared_part[:, :, 2 * STATE:].astype(jnp.float32) + step_bias)
    step_size = jnp.where(valid[:, :, None], step_size, 0.0)
    decay = -jnp.exp(decay_log)
    inputs = mixed_inner.reshape(REQUESTS, TMAX, HEADS, HEAD_DIM)

    def run_block(block):
        carried, step_block, input_block, shared_block = block
        carried = carried.astype(jnp.float32)
        collected = []
        for position in range(TMAX):
            carried, produced = advance(carried, step_block[:, position], input_block[:, position], shared_block[:, position, :STATE], shared_block[:, position, STATE:], decay, skip_gain)
            collected.append(produced)
        return (carried.astype(jnp.bfloat16), jnp.stack(collected, axis=1))
    block_count = REQUESTS // REQ_DEV

    def split_blocks(array):
        return array.reshape((block_count, REQ_DEV) + array.shape[1:])
    final_states, outputs = lax.map(run_block, (split_blocks(moved_states), split_blocks(step_size), split_blocks(inputs), split_blocks(mixed_shared)))
    final_states = final_states.reshape(states.shape)
    outputs = outputs.reshape(REQUESTS, TMAX, INNER)
    gated = outputs * jax.nn.silu(gate_part.astype(jnp.float32))
    square_sum = lax.optimization_barrier(jnp.sum(gated * gated, axis=-1, keepdims=True))
    scaled = gated * lax.rsqrt(square_sum / INNER + EPS) * gate_gain
    scaled = jnp.where(valid[:, :, None], scaled, 0.0).astype(jnp.bfloat16).reshape(REQUESTS * TMAX, INNER)
    mixer = jnp.dot(scaled, out_weight, preferred_element_type=jnp.float32)
    hidden_out = (rows_in + mixer).astype(jnp.bfloat16)
    return (hidden_out, final_states, edge_inner_out, edge_shared_out)
```

```python
import jax
import jax.numpy as jnp
from jax import lax
from jax.sharding import PartitionSpec as P

EPS = 1e-05
HIGH = lax.Precision.HIGHEST


def depthwise(edge, fresh, weight, offset_bias):
    sequence = jnp.concatenate([edge, fresh], axis=1).astype(jnp.float32)
    window = fresh.shape[1]
    summed = sequence[:, 0:window] * weight[0]
    for offset in range(1, weight.shape[0]):
        summed = summed + sequence[:, offset : offset + window] * weight[offset]
    return jax.nn.silu(summed + offset_bias)


def new_edge(edge, fresh, counts):
    sequence = jnp.concatenate([edge, fresh], axis=1)
    keep_rows = edge.shape[1]
    result = edge
    for length in range(1, fresh.shape[1] + 1):
        result = jnp.where(
            (counts == length)[:, None, None], sequence[:, length : length + keep_rows], result
        )
    return result


def rank_rows(partner, position, capacity):
    matching = partner[:, None] == partner[None, :]
    earlier = position[None, :] < position[:, None]
    ranking = jnp.sum(jnp.logical_and(matching, earlier), axis=1)
    return partner * capacity + ranking


def route_rows(anchor, first_slot, slot_count, all_slots, capacity):
    inverse = jnp.zeros(all_slots.shape, jnp.int32).at[anchor].set(all_slots)
    targets = lax.dynamic_slice_in_dim(inverse, first_slot, slot_count)
    send_rows = rank_rows(targets // slot_count, targets % slot_count, capacity)
    sources = lax.dynamic_slice_in_dim(anchor, first_slot, slot_count)
    recv_rows = rank_rows(sources // slot_count, jnp.arange(slot_count, dtype=jnp.int32), capacity)
    return (send_rows, recv_rows)


def migrate(item, mig_dest, slot_count, groups, device):
    length = item.shape[0]
    piece = -(-length // groups)
    padded = jnp.pad(item, (0, piece * groups - length)).reshape(groups, piece)
    first = lax.all_to_all(padded, "req", 0, 0, tiled=True)
    dest_dev = mig_dest // slot_count
    order = jnp.zeros((groups,), jnp.int32).at[dest_dev].set(jnp.arange(groups, dtype=jnp.int32))
    second = lax.all_to_all(first[order], "req", 0, 0, tiled=True)
    arrived = second.reshape(-1)[:length]
    target_local = mig_dest[order[device]] - device * slot_count
    return arrived, target_local


def local(
    tokens,
    pre_gain,
    inner_weight,
    shared_weight,
    conv_inner,
    conv_inner_bias,
    conv_shared,
    conv_shared_bias,
    step_bias,
    decay_log,
    skip_gain,
    gate_gain,
    out_weight,
    states,
    edge_inner,
    edge_shared,
    counts,
    mig_ids,
    mig_dest,
    reorder,
):
    slot_count, heads_here, head_dim, state_dim = states.shape
    inner_here = heads_here * head_dim
    lanes = state_dim
    groups = lax.axis_size("req")
    device = lax.axis_index("req")
    first_slot = device * slot_count
    stride = (slot_count + groups - 1) // groups
    all_slots = jnp.arange(slot_count * groups, dtype=jnp.int32)

    rows_in = tokens.astype(jnp.float32)
    normed = (
        rows_in * lax.rsqrt(jnp.mean(rows_in * rows_in, axis=-1, keepdims=True) + EPS) * pre_gain
    ).astype(jnp.bfloat16)
    inner_flat = inner_weight.reshape(inner_weight.shape[0], 2 * inner_here)
    piece_rows = lax.all_gather(normed, "head", axis=0, tiled=True)
    inner_rows = jnp.dot(piece_rows, inner_flat, preferred_element_type=jnp.float32).astype(
        jnp.bfloat16
    )
    shared_rows = jnp.dot(piece_rows, shared_weight, preferred_element_type=jnp.float32).astype(
        jnp.bfloat16
    )

    state_rows = heads_here * head_dim * state_dim // lanes
    inner_edge_rows = edge_inner.shape[1] * edge_inner.shape[2] // lanes
    shared_edge_rows = edge_shared.shape[1] * edge_shared.shape[2] // lanes
    packed = jnp.concatenate(
        [
            states.reshape(slot_count, state_rows, lanes),
            edge_inner.reshape(slot_count, inner_edge_rows, lanes),
            edge_shared.reshape(slot_count, shared_edge_rows, lanes),
        ],
        axis=1,
    )
    row_total = packed.shape[1]

    moving = mig_ids.shape[0] // groups
    own_id = mig_ids[device * moving]
    mig_local = own_id - first_slot
    item = lax.dynamic_index_in_dim(packed, mig_local, 0, keepdims=False).reshape(-1)
    arrived, target_local = migrate(item, mig_dest, slot_count, groups, device)
    arrived = arrived.reshape(row_total, lanes)

    send_rows, recv_rows = route_rows(reorder, first_slot, slot_count, all_slots, stride)
    buffer_rows = groups * stride
    send_idx = (
        jnp.zeros((buffer_rows,), jnp.int32).at[send_rows].set(jnp.arange(slot_count, dtype=jnp.int32))
    )
    send_buf = jnp.where(
        (send_idx == target_local)[:, None, None], arrived[None], packed[send_idx]
    )
    received = lax.all_to_all(send_buf, "req", 0, 0, tiled=True)
    moved = received[recv_rows]
    moved_states = moved[:, :state_rows].reshape(slot_count, heads_here, head_dim, state_dim)
    moved_inner = moved[:, state_rows : state_rows + inner_edge_rows].reshape(edge_inner.shape)
    moved_shared = moved[:, state_rows + inner_edge_rows :].reshape(edge_shared.shape)

    window = inner_rows.shape[0] // slot_count
    inner_rows = inner_rows.reshape(slot_count, window, 2 * inner_here)
    shared_rows = shared_rows.reshape(slot_count, window, shared_rows.shape[1])
    gate_part = inner_rows[:, :, :inner_here]
    value_part = inner_rows[:, :, inner_here:]
    fresh_shared = shared_rows[:, :, : 2 * state_dim]
    head_index = lax.axis_index("head")
    step_raw = lax.dynamic_slice_in_dim(
        shared_rows[:, :, 2 * state_dim :], head_index * heads_here, heads_here, axis=2
    )
    edge_inner_out = new_edge(moved_inner, value_part, counts)
    edge_shared_out = new_edge(moved_shared, fresh_shared, counts)
    mixed_inner = depthwise(moved_inner, value_part, conv_inner, conv_inner_bias)
    mixed_shared = depthwise(moved_shared, fresh_shared, conv_shared, conv_shared_bias)
    valid = jnp.arange(window)[None, :] < counts[:, None]
    step_size = jax.nn.softplus(step_raw.astype(jnp.float32) + step_bias)
    step_size = jnp.where(valid[:, :, None], step_size, 0.0)
    decay = -jnp.exp(decay_log)
    inputs = mixed_inner.reshape(slot_count, window, heads_here, head_dim)
    entries = mixed_shared[:, :, :state_dim]
    readouts = mixed_shared[:, :, state_dim:]

    factor = jnp.exp(step_size * decay)
    cum = [factor[:, 0]]
    for t in range(1, window):
        cum.append(cum[-1] * factor[:, t])
    cumulative = jnp.stack(cum, axis=1)
    span = {}
    for t in range(window):
        span[(t, t)] = jnp.ones_like(factor[:, 0])
        for s in range(t - 1, -1, -1):
            span[(t, s)] = span[(t, s + 1)] * factor[:, s + 1]
    held = moved_states.astype(jnp.float32)
    from_state = jnp.einsum("rhpn,rtn->rthp", held, readouts, precision=HIGH)
    overlap = jnp.einsum("rtn,rsn->rts", readouts, entries, precision=HIGH)
    weighted = step_size[:, :, :, None] * inputs
    produced = []
    for t in range(window):
        acc = cumulative[:, t, :, None] * from_state[:, t]
        for s in range(t + 1):
            coef = span[(t, s)] * overlap[:, t, s, None]
            acc = acc + coef[:, :, None] * weighted[:, s]
        produced.append(acc + skip_gain[None, :, None] * inputs[:, t])
    outputs = jnp.stack(produced, axis=1)
    last = window - 1
    pushed = jnp.stack([span[(last, s)] for s in range(window)], axis=1)[:, :, :, None] * weighted
    update = jnp.einsum("rshp,rsn->rhpn", pushed, entries, precision=HIGH)
    final = cumulative[:, last, :, None, None] * held + update
    states_out = final.astype(jnp.bfloat16)

    outputs = outputs.reshape(slot_count, window, inner_here)
    gated = outputs * jax.nn.silu(gate_part.astype(jnp.float32))
    square_part = jnp.sum(gated * gated, axis=-1).reshape(slot_count * window, 1)
    pre_scaled = (
        jnp.where(valid[:, :, None], gated * gate_gain, 0.0)
        .astype(jnp.bfloat16)
        .reshape(slot_count * window, inner_here)
    )
    partial = jnp.dot(pre_scaled, out_weight, preferred_element_type=jnp.float32)
    extra = jnp.broadcast_to(square_part, (partial.shape[0], 128))
    combined = jnp.concatenate([partial, extra], axis=1)
    reduced = lax.psum_scatter(combined, "head", scatter_dimension=0, tiled=True)
    full_inner = inner_here * lax.axis_size("head")
    scale = lax.rsqrt(reduced[:, -1:] / full_inner + EPS)
    hidden_out = (rows_in + reduced[:, : partial.shape[1]] * scale).astype(jnp.bfloat16)
    return (hidden_out, states_out, edge_inner_out, edge_shared_out)


def solution(mesh):
    placed = (
        P(("req", "head"), None),
        P(),
        P(None, None, "head"),
        P(),
        P(None, "head"),
        P("head"),
        P(),
        P(),
        P("head"),
        P("head"),
        P("head"),
        P("head"),
        P("head", None),
        P("req", "head", None, None),
        P("req", None, "head"),
        P("req", None, None),
        P("req"),
        P(),
        P(),
        P(),
    )
    return jax.shard_map(
        local,
        mesh=mesh,
        in_specs=placed,
        out_specs=(
            P(("req", "head"), None),
            P("req", "head", None, None),
            P("req", None, "head"),
            P("req", None, None),
        ),
        check_vma=False,
    )
```

```python
import functools

import jax
import jax.numpy as jnp
from jax import lax
from jax.sharding import PartitionSpec as P
from jax.experimental import pallas as pl
from jax.experimental.pallas import tpu as pltpu

EPS = 1e-05
HIGH = lax.Precision.HIGHEST


def depthwise(edge, fresh, weight, offset_bias):
    sequence = jnp.concatenate([edge, fresh], axis=1).astype(jnp.float32)
    window = fresh.shape[1]
    summed = sequence[:, 0:window] * weight[0]
    for offset in range(1, weight.shape[0]):
        summed = summed + sequence[:, offset : offset + window] * weight[offset]
    return jax.nn.silu(summed + offset_bias)


def new_edge(edge, fresh, counts):
    sequence = jnp.concatenate([edge, fresh], axis=1)
    keep_rows = edge.shape[1]
    result = edge
    for length in range(1, fresh.shape[1] + 1):
        result = jnp.where(
            (counts == length)[:, None, None], sequence[:, length : length + keep_rows], result
        )
    return result


def rank_rows(partner, position, capacity):
    matching = partner[:, None] == partner[None, :]
    earlier = position[None, :] < position[:, None]
    ranking = jnp.sum(jnp.logical_and(matching, earlier), axis=1)
    return partner * capacity + ranking


def invert(values, size):
    hits = values[None, :] == jnp.arange(size, dtype=jnp.int32)[:, None]
    return jnp.sum(jnp.where(hits, jnp.arange(values.shape[0], dtype=jnp.int32)[None, :], 0), axis=1)


def route_rows(anchor, first_slot, slot_count, all_slots, capacity):
    mine = first_slot + jnp.arange(slot_count, dtype=jnp.int32)
    hits = anchor[None, :] == mine[:, None]
    targets = jnp.sum(jnp.where(hits, all_slots[None, :], 0), axis=1)
    send_rows = rank_rows(targets // slot_count, targets % slot_count, capacity)
    sources = lax.dynamic_slice_in_dim(anchor, first_slot, slot_count)
    recv_rows = rank_rows(sources // slot_count, jnp.arange(slot_count, dtype=jnp.int32), capacity)
    return (send_rows, recv_rows)


def recurrence_kernel(rows_ref, *refs, group, window):
    held_refs = refs[:group]
    mix_ref, weight_ref, read_ref, out_ref = refs[group:]
    for q in range(group):
        held = held_refs[q][0].astype(jnp.float32)
        mix = mix_ref[q]
        read_ref[q] = lax.dot_general(
            mix, held, (((1,), (1,)), ((), ())), precision=HIGH,
            preferred_element_type=jnp.float32,
        )
        weight = weight_ref[q]
        acc = weight[:, window : window + 1] * held
        for s in range(window):
            acc = acc + weight[:, s : s + 1] * mix[window + s : window + s + 1, :]
        out_ref[q] = acc.astype(out_ref.dtype)


def recurrence(received, rows, mix, weight, state_rows, group=4):
    slot_count, _, lanes = received.shape
    window = mix.shape[1] // 2
    held_specs = [
        pl.BlockSpec((1, state_rows, lanes), lambda i, r, q=q: (r[i * group + q], 0, 0))
        for q in range(group)
    ]
    grid_spec = pltpu.PrefetchScalarGridSpec(
        num_scalar_prefetch=1,
        grid=(slot_count // group,),
        in_specs=held_specs
        + [
            pl.BlockSpec((group, 2 * window, lanes), lambda i, r: (i, 0, 0)),
            pl.BlockSpec((group, state_rows, 2 * window), lambda i, r: (i, 0, 0)),
        ],
        out_specs=[
            pl.BlockSpec((group, 2 * window, state_rows), lambda i, r: (i, 0, 0)),
            pl.BlockSpec((group, state_rows, lanes), lambda i, r: (i, 0, 0)),
        ],
    )
    return pl.pallas_call(
        functools.partial(recurrence_kernel, group=group, window=window),
        grid_spec=grid_spec,
        out_shape=[
            jax.ShapeDtypeStruct((slot_count, 2 * window, state_rows), jnp.float32),
            jax.ShapeDtypeStruct((slot_count, state_rows, lanes), jnp.bfloat16),
        ],
    )(rows, *([received] * group), mix, weight)


def migrate(item, mig_dest, slot_count, groups, device):
    length = item.shape[0]
    piece = -(-length // groups)
    padded = jnp.pad(item, (0, piece * groups - length)).reshape(groups, piece)
    first = lax.all_to_all(padded, "req", 0, 0, tiled=True)
    dest_dev = mig_dest // slot_count
    order = invert(dest_dev, groups)
    second = lax.all_to_all(first[order], "req", 0, 0, tiled=True)
    arrived = second.reshape(-1)[:length]
    target_local = mig_dest[order[device]] - device * slot_count
    return arrived, target_local


def local(
    tokens,
    pre_gain,
    inner_weight,
    shared_weight,
    conv_inner,
    conv_inner_bias,
    conv_shared,
    conv_shared_bias,
    step_bias,
    decay_log,
    skip_gain,
    gate_gain,
    out_weight,
    states,
    edge_inner,
    edge_shared,
    counts,
    mig_ids,
    mig_dest,
    reorder,
):
    slot_count, heads_here, head_dim, state_dim = states.shape
    inner_here = heads_here * head_dim
    lanes = state_dim
    groups = lax.axis_size("req")
    device = lax.axis_index("req")
    first_slot = device * slot_count
    stride = (slot_count + groups - 1) // groups
    all_slots = jnp.arange(slot_count * groups, dtype=jnp.int32)

    rows_in = tokens.astype(jnp.float32)
    normed = (
        rows_in * lax.rsqrt(jnp.mean(rows_in * rows_in, axis=-1, keepdims=True) + EPS) * pre_gain
    ).astype(jnp.bfloat16)
    inner_flat = inner_weight.reshape(inner_weight.shape[0], 2 * inner_here)
    piece_rows = lax.all_gather(normed, "head", axis=0, tiled=True)
    inner_rows = jnp.dot(piece_rows, inner_flat, preferred_element_type=jnp.float32).astype(
        jnp.bfloat16
    )
    shared_rows = jnp.dot(piece_rows, shared_weight, preferred_element_type=jnp.float32).astype(
        jnp.bfloat16
    )

    state_rows = heads_here * head_dim * state_dim // lanes
    inner_edge_rows = edge_inner.shape[1] * edge_inner.shape[2] // lanes
    shared_edge_rows = edge_shared.shape[1] * edge_shared.shape[2] // lanes
    packed = jnp.concatenate(
        [
            states.reshape(slot_count, state_rows, lanes),
            edge_inner.reshape(slot_count, inner_edge_rows, lanes),
            edge_shared.reshape(slot_count, shared_edge_rows, lanes),
        ],
        axis=1,
    )
    row_total = packed.shape[1]

    moving = mig_ids.shape[0] // groups
    own_id = mig_ids[device * moving]
    mig_local = own_id - first_slot
    item = lax.dynamic_index_in_dim(packed, mig_local, 0, keepdims=False).reshape(-1)
    arrived, target_local = migrate(item, mig_dest, slot_count, groups, device)
    arrived = arrived.reshape(row_total, lanes)

    send_rows, recv_rows = route_rows(reorder, first_slot, slot_count, all_slots, stride)
    buffer_rows = groups * stride
    send_idx = invert(send_rows, buffer_rows)
    send_buf = jnp.where(
        (send_idx == target_local)[:, None, None], arrived[None], packed[send_idx]
    )
    received = lax.all_to_all(send_buf, "req", 0, 0, tiled=True)
    moved = received[:, state_rows:][recv_rows]
    moved_inner = moved[:, :inner_edge_rows].reshape(edge_inner.shape)
    moved_shared = moved[:, inner_edge_rows:].reshape(edge_shared.shape)

    window = inner_rows.shape[0] // slot_count
    inner_rows = inner_rows.reshape(slot_count, window, 2 * inner_here)
    shared_rows = shared_rows.reshape(slot_count, window, shared_rows.shape[1])
    gate_part = inner_rows[:, :, :inner_here]
    value_part = inner_rows[:, :, inner_here:]
    fresh_shared = shared_rows[:, :, : 2 * state_dim]
    head_index = lax.axis_index("head")
    step_raw = lax.dynamic_slice_in_dim(
        shared_rows[:, :, 2 * state_dim :], head_index * heads_here, heads_here, axis=2
    )
    edge_inner_out = new_edge(moved_inner, value_part, counts)
    edge_shared_out = new_edge(moved_shared, fresh_shared, counts)
    mixed_inner = depthwise(moved_inner, value_part, conv_inner, conv_inner_bias)
    mixed_shared = depthwise(moved_shared, fresh_shared, conv_shared, conv_shared_bias)
    valid = jnp.arange(window)[None, :] < counts[:, None]
    step_size = jax.nn.softplus(step_raw.astype(jnp.float32) + step_bias)
    step_size = jnp.where(valid[:, :, None], step_size, 0.0)
    decay = -jnp.exp(decay_log)
    inputs = mixed_inner.reshape(slot_count, window, heads_here, head_dim)
    entries = mixed_shared[:, :, :state_dim]
    readouts = mixed_shared[:, :, state_dim:]

    factor = jnp.exp(step_size * decay)
    cum = [factor[:, 0]]
    for t in range(1, window):
        cum.append(cum[-1] * factor[:, t])
    cumulative = jnp.stack(cum, axis=1)
    span = {}
    for t in range(window):
        span[(t, t)] = jnp.ones_like(factor[:, 0])
        for s in range(t - 1, -1, -1):
            span[(t, s)] = span[(t, s + 1)] * factor[:, s + 1]
    weighted = step_size[:, :, :, None] * inputs
    last = window - 1
    pushed = jnp.stack([span[(last, s)] for s in range(window)], axis=1)[:, :, :, None] * weighted
    carry = jnp.broadcast_to(
        cumulative[:, last, :, None], (slot_count, heads_here, head_dim)
    ).reshape(slot_count, 1, inner_here)
    weight = jnp.concatenate(
        [
            pushed.reshape(slot_count, window, inner_here),
            carry,
            jnp.zeros((slot_count, window - 1, inner_here), jnp.float32),
        ],
        axis=1,
    ).transpose(0, 2, 1)
    mix = jnp.concatenate([readouts, entries], axis=1)
    read, states_out = recurrence(received, recv_rows, mix, weight, state_rows)
    states_out = states_out.reshape(states.shape)
    from_state = read[:, :window].reshape(slot_count, window, heads_here, head_dim)
    overlap = jnp.einsum("rtn,rsn->rts", readouts, entries, precision=HIGH)
    produced = []
    for t in range(window):
        acc = cumulative[:, t, :, None] * from_state[:, t]
        for s in range(t + 1):
            coef = span[(t, s)] * overlap[:, t, s, None]
            acc = acc + coef[:, :, None] * weighted[:, s]
        produced.append(acc + skip_gain[None, :, None] * inputs[:, t])
    outputs = jnp.stack(produced, axis=1)

    outputs = outputs.reshape(slot_count, window, inner_here)
    gated = outputs * jax.nn.silu(gate_part.astype(jnp.float32))
    square_part = jnp.sum(gated * gated, axis=-1).reshape(slot_count * window, 1)
    pre_scaled = (
        jnp.where(valid[:, :, None], gated * gate_gain, 0.0)
        .astype(jnp.bfloat16)
        .reshape(slot_count * window, inner_here)
    )
    partial = jnp.dot(pre_scaled, out_weight, preferred_element_type=jnp.float32)
    extra = jnp.broadcast_to(square_part, (partial.shape[0], 128))
    combined = jnp.concatenate([partial, extra], axis=1)
    reduced = lax.psum_scatter(combined, "head", scatter_dimension=0, tiled=True)
    full_inner = inner_here * lax.axis_size("head")
    scale = lax.rsqrt(reduced[:, -1:] / full_inner + EPS)
    hidden_out = (rows_in + reduced[:, : partial.shape[1]] * scale).astype(jnp.bfloat16)
    return (hidden_out, states_out, edge_inner_out, edge_shared_out)


def solution(mesh):
    placed = (
        P(("req", "head"), None),
        P(),
        P(None, None, "head"),
        P(),
        P(None, "head"),
        P("head"),
        P(),
        P(),
        P("head"),
        P("head"),
        P("head"),
        P("head"),
        P("head", None),
        P("req", "head", None, None),
        P("req", None, "head"),
        P("req", None, None),
        P("req"),
        P(),
        P(),
        P(),
    )
    return jax.shard_map(
        local,
        mesh=mesh,
        in_specs=placed,
        out_specs=(
            P(("req", "head"), None),
            P("req", "head", None, None),
            P("req", None, "head"),
            P("req", None, None),
        ),
        check_vma=False,
    )
```

```python
import functools

import jax
import jax.numpy as jnp
from jax import lax
from jax.sharding import PartitionSpec as P
from jax.experimental import pallas as pl
from jax.experimental.pallas import tpu as pltpu

EPS = 1e-05
HIGH = lax.Precision.HIGHEST


def depthwise(edge, fresh, weight, offset_bias):
    sequence = jnp.concatenate([edge, fresh], axis=1).astype(jnp.float32)
    window = fresh.shape[1]
    summed = sequence[:, 0:window] * weight[0]
    for offset in range(1, weight.shape[0]):
        summed = summed + sequence[:, offset : offset + window] * weight[offset]
    return jax.nn.silu(summed + offset_bias)


def new_edge(edge, fresh, counts):
    sequence = jnp.concatenate([edge, fresh], axis=1)
    keep_rows = edge.shape[1]
    result = edge
    for length in range(1, fresh.shape[1] + 1):
        result = jnp.where(
            (counts == length)[:, None, None], sequence[:, length : length + keep_rows], result
        )
    return result


def rank_rows(partner, position, capacity):
    matching = partner[:, None] == partner[None, :]
    earlier = position[None, :] < position[:, None]
    ranking = jnp.sum(jnp.logical_and(matching, earlier), axis=1)
    return partner * capacity + ranking


def invert(values, size):
    hits = values[None, :] == jnp.arange(size, dtype=jnp.int32)[:, None]
    return jnp.sum(jnp.where(hits, jnp.arange(values.shape[0], dtype=jnp.int32)[None, :], 0), axis=1)


def route_rows(anchor, first_slot, slot_count, all_slots, capacity):
    mine = first_slot + jnp.arange(slot_count, dtype=jnp.int32)
    hits = anchor[None, :] == mine[:, None]
    targets = jnp.sum(jnp.where(hits, all_slots[None, :], 0), axis=1)
    send_rows = rank_rows(targets // slot_count, targets % slot_count, capacity)
    sources = lax.dynamic_slice_in_dim(anchor, first_slot, slot_count)
    recv_rows = rank_rows(sources // slot_count, jnp.arange(slot_count, dtype=jnp.int32), capacity)
    return (send_rows, recv_rows)


def recurrence_kernel(rows_ref, *refs, group, window, heads):
    held_refs = refs[:group]
    mix_ref, weight_ref, read_ref, out_ref = refs[group:]
    for q in range(group):
        held = held_refs[q][0].astype(jnp.float32)
        mix = mix_ref[q]
        read_ref[q] = lax.dot_general(
            mix[: 2 * window], held, (((1,), (1,)), ((), ())), precision=HIGH,
            preferred_element_type=jnp.float32,
        )
        pushed = lax.dot_general(
            weight_ref[q], mix[window : 3 * window], (((0,), (0,)), ((), ())),
            precision=HIGH, preferred_element_type=jnp.float32,
        )
        rows = held.shape[0] // heads
        carry = mix[2 * window : 2 * window + 1]
        for h in range(heads):
            part = slice(h * rows, (h + 1) * rows)
            out_ref[q, part] = (carry[:, h : h + 1] * held[part] + pushed[part]).astype(
                out_ref.dtype
            )


def recurrence(received, rows, mix, weight, state_rows, heads, group=4):
    slot_count, _, lanes = received.shape
    window = mix.shape[1] // 4
    held_specs = [
        pl.BlockSpec((1, state_rows, lanes), lambda i, r, q=q: (r[i * group + q], 0, 0))
        for q in range(group)
    ]
    grid_spec = pltpu.PrefetchScalarGridSpec(
        num_scalar_prefetch=1,
        grid=(slot_count // group,),
        in_specs=held_specs
        + [
            pl.BlockSpec((group, 4 * window, lanes), lambda i, r: (i, 0, 0)),
            pl.BlockSpec((group, 2 * window, state_rows), lambda i, r: (i, 0, 0)),
        ],
        out_specs=[
            pl.BlockSpec((group, 2 * window, state_rows), lambda i, r: (i, 0, 0)),
            pl.BlockSpec((group, state_rows, lanes), lambda i, r: (i, 0, 0)),
        ],
    )
    return pl.pallas_call(
        functools.partial(recurrence_kernel, group=group, window=window, heads=heads),
        grid_spec=grid_spec,
        out_shape=[
            jax.ShapeDtypeStruct((slot_count, 2 * window, state_rows), jnp.float32),
            jax.ShapeDtypeStruct((slot_count, state_rows, lanes), jnp.bfloat16),
        ],
    )(rows, *([received] * group), mix, weight)


def migrate(item, mig_dest, slot_count, groups, device):
    length = item.shape[0]
    piece = -(-length // groups)
    padded = jnp.pad(item, (0, piece * groups - length)).reshape(groups, piece)
    first = lax.all_to_all(padded, "req", 0, 0, tiled=True)
    dest_dev = mig_dest // slot_count
    order = invert(dest_dev, groups)
    second = lax.all_to_all(first[order], "req", 0, 0, tiled=True)
    arrived = second.reshape(-1)[:length]
    target_local = mig_dest[order[device]] - device * slot_count
    return arrived, target_local


def local(
    tokens,
    pre_gain,
    inner_weight,
    shared_weight,
    conv_inner,
    conv_inner_bias,
    conv_shared,
    conv_shared_bias,
    step_bias,
    decay_log,
    skip_gain,
    gate_gain,
    out_weight,
    states,
    edge_inner,
    edge_shared,
    counts,
    mig_ids,
    mig_dest,
    reorder,
):
    slot_count, heads_here, head_dim, state_dim = states.shape
    inner_here = heads_here * head_dim
    lanes = state_dim
    groups = lax.axis_size("req")
    device = lax.axis_index("req")
    first_slot = device * slot_count
    stride = (slot_count + groups - 1) // groups
    all_slots = jnp.arange(slot_count * groups, dtype=jnp.int32)

    rows_in = tokens.astype(jnp.float32)
    normed = (
        rows_in * lax.rsqrt(jnp.mean(rows_in * rows_in, axis=-1, keepdims=True) + EPS) * pre_gain
    ).astype(jnp.bfloat16)
    inner_flat = inner_weight.reshape(inner_weight.shape[0], 2 * inner_here)
    piece_rows = lax.all_gather(normed, "head", axis=0, tiled=True)
    inner_rows = jnp.dot(piece_rows, inner_flat, preferred_element_type=jnp.float32).astype(
        jnp.bfloat16
    )
    shared_rows = jnp.dot(piece_rows, shared_weight, preferred_element_type=jnp.float32).astype(
        jnp.bfloat16
    )

    state_rows = heads_here * head_dim * state_dim // lanes
    inner_edge_rows = edge_inner.shape[1] * edge_inner.shape[2] // lanes
    shared_edge_rows = edge_shared.shape[1] * edge_shared.shape[2] // lanes
    packed = jnp.concatenate(
        [
            states.reshape(slot_count, state_rows, lanes),
            edge_inner.reshape(slot_count, inner_edge_rows, lanes),
            edge_shared.reshape(slot_count, shared_edge_rows, lanes),
        ],
        axis=1,
    )
    row_total = packed.shape[1]

    moving = mig_ids.shape[0] // groups
    own_id = mig_ids[device * moving]
    mig_local = own_id - first_slot
    item = lax.dynamic_index_in_dim(packed, mig_local, 0, keepdims=False).reshape(-1)
    arrived, target_local = migrate(item, mig_dest, slot_count, groups, device)
    arrived = arrived.reshape(row_total, lanes)

    send_rows, recv_rows = route_rows(reorder, first_slot, slot_count, all_slots, stride)
    buffer_rows = groups * stride
    send_idx = invert(send_rows, buffer_rows)
    send_buf = jnp.where(
        (send_idx == target_local)[:, None, None], arrived[None], packed[send_idx]
    )
    received = lax.all_to_all(send_buf, "req", 0, 0, tiled=True)
    moved = received[:, state_rows:][recv_rows]
    moved_inner = moved[:, :inner_edge_rows].reshape(edge_inner.shape)
    moved_shared = moved[:, inner_edge_rows:].reshape(edge_shared.shape)

    window = inner_rows.shape[0] // slot_count
    inner_rows = inner_rows.reshape(slot_count, window, 2 * inner_here)
    shared_rows = shared_rows.reshape(slot_count, window, shared_rows.shape[1])
    gate_part = inner_rows[:, :, :inner_here]
    value_part = inner_rows[:, :, inner_here:]
    fresh_shared = shared_rows[:, :, : 2 * state_dim]
    head_index = lax.axis_index("head")
    step_raw = lax.dynamic_slice_in_dim(
        shared_rows[:, :, 2 * state_dim :], head_index * heads_here, heads_here, axis=2
    )
    edge_inner_out = new_edge(moved_inner, value_part, counts)
    edge_shared_out = new_edge(moved_shared, fresh_shared, counts)
    mixed_inner = depthwise(moved_inner, value_part, conv_inner, conv_inner_bias)
    mixed_shared = depthwise(moved_shared, fresh_shared, conv_shared, conv_shared_bias)
    valid = jnp.arange(window)[None, :] < counts[:, None]
    step_size = jax.nn.softplus(step_raw.astype(jnp.float32) + step_bias)
    step_size = jnp.where(valid[:, :, None], step_size, 0.0)
    decay = -jnp.exp(decay_log)
    entries = mixed_shared[:, :, :state_dim]
    readouts = mixed_shared[:, :, state_dim:]

    factor = jnp.exp(step_size * decay)
    cum = [factor[:, 0]]
    for t in range(1, window):
        cum.append(cum[-1] * factor[:, t])
    span = {}
    for t in range(window):
        span[(t, t)] = jnp.ones_like(factor[:, 0])
        for s in range(t - 1, -1, -1):
            span[(t, s)] = span[(t, s + 1)] * factor[:, s + 1]

    def per_head(v):
        return jnp.repeat(v, head_dim, axis=-1)

    flat_inputs = mixed_inner.reshape(slot_count, window, inner_here)
    weighted = per_head(step_size) * flat_inputs
    last = window - 1
    pushed = jnp.stack([per_head(span[(last, s)]) * weighted[:, s] for s in range(window)], axis=1)
    weight = jnp.concatenate([pushed, jnp.zeros_like(pushed)], axis=1)
    carry = jnp.pad(cum[last], ((0, 0), (0, state_dim - heads_here)))[:, None, :]
    mix = jnp.concatenate(
        [readouts, entries, carry, jnp.zeros((slot_count, 2 * window - 1, state_dim), jnp.float32)],
        axis=1,
    )
    read, states_out = recurrence(received, recv_rows, mix, weight, state_rows, heads_here)
    states_out = states_out.reshape(states.shape)
    overlap = jnp.einsum("rtn,rsn->rts", readouts, entries, precision=HIGH)
    skip_wide = jnp.repeat(skip_gain, head_dim)
    produced = []
    for t in range(window):
        acc = per_head(cum[t]) * read[:, t]
        for s in range(t + 1):
            acc = acc + per_head(span[(t, s)] * overlap[:, t, s, None]) * weighted[:, s]
        produced.append(acc + skip_wide * flat_inputs[:, t])
    outputs = jnp.stack(produced, axis=1)

    gated = outputs * jax.nn.silu(gate_part.astype(jnp.float32))
    square_part = jnp.sum(gated * gated, axis=-1).reshape(slot_count * window, 1)
    pre_scaled = (
        jnp.where(valid[:, :, None], gated * gate_gain, 0.0)
        .astype(jnp.bfloat16)
        .reshape(slot_count * window, inner_here)
    )
    partial = jnp.dot(pre_scaled, out_weight, preferred_element_type=jnp.float32)
    extra = jnp.broadcast_to(square_part, (partial.shape[0], 128))
    combined = jnp.concatenate([partial, extra], axis=1)
    reduced = lax.psum_scatter(combined, "head", scatter_dimension=0, tiled=True)
    full_inner = inner_here * lax.axis_size("head")
    scale = lax.rsqrt(reduced[:, -1:] / full_inner + EPS)
    hidden_out = (rows_in + reduced[:, : partial.shape[1]] * scale).astype(jnp.bfloat16)
    return (hidden_out, states_out, edge_inner_out, edge_shared_out)


def solution(mesh):
    placed = (
        P(("req", "head"), None),
        P(),
        P(None, None, "head"),
        P(),
        P(None, "head"),
        P("head"),
        P(),
        P(),
        P("head"),
        P("head"),
        P("head"),
        P("head"),
        P("head", None),
        P("req", "head", None, None),
        P("req", None, "head"),
        P("req", None, None),
        P("req"),
        P(),
        P(),
        P(),
    )
    return jax.shard_map(
        local,
        mesh=mesh,
        in_specs=placed,
        out_specs=(
            P(("req", "head"), None),
            P("req", "head", None, None),
            P("req", None, "head"),
            P("req", None, None),
        ),
        check_vma=False,
    )
```

```python
import functools

import jax
import jax.numpy as jnp
from jax import lax
from jax.sharding import PartitionSpec as P
from jax.experimental import pallas as pl
from jax.experimental.pallas import tpu as pltpu

EPS = 1e-05
HIGH = lax.Precision.HIGHEST


def depthwise(edge, fresh, weight, offset_bias):
    sequence = jnp.concatenate([edge, fresh], axis=1).astype(jnp.float32)
    window = fresh.shape[1]
    summed = sequence[:, 0:window] * weight[0]
    for offset in range(1, weight.shape[0]):
        summed = summed + sequence[:, offset : offset + window] * weight[offset]
    return jax.nn.silu(summed + offset_bias)


def new_edge(edge, fresh, counts):
    sequence = jnp.concatenate([edge, fresh], axis=1)
    keep_rows = edge.shape[1]
    result = edge
    for length in range(1, fresh.shape[1] + 1):
        result = jnp.where(
            (counts == length)[:, None, None], sequence[:, length : length + keep_rows], result
        )
    return result


def rank_rows(partner, position, capacity):
    matching = partner[:, None] == partner[None, :]
    earlier = position[None, :] < position[:, None]
    ranking = jnp.sum(jnp.logical_and(matching, earlier), axis=1)
    return partner * capacity + ranking


def invert(values, size):
    hits = values[None, :] == jnp.arange(size, dtype=jnp.int32)[:, None]
    return jnp.sum(jnp.where(hits, jnp.arange(values.shape[0], dtype=jnp.int32)[None, :], 0), axis=1)


def route_rows(anchor, first_slot, slot_count, all_slots, capacity):
    mine = first_slot + jnp.arange(slot_count, dtype=jnp.int32)
    hits = anchor[None, :] == mine[:, None]
    targets = jnp.sum(jnp.where(hits, all_slots[None, :], 0), axis=1)
    send_rows = rank_rows(targets // slot_count, targets % slot_count, capacity)
    sources = lax.dynamic_slice_in_dim(anchor, first_slot, slot_count)
    recv_rows = rank_rows(sources // slot_count, jnp.arange(slot_count, dtype=jnp.int32), capacity)
    return (send_rows, recv_rows)


def recurrence_kernel(rows_ref, *refs, group, window, heads):
    held_refs = refs[:group]
    mix_ref, weight_ref, read_ref, out_ref = refs[group:]
    nt = (((1,), (1,)), ((), ()))
    tn = (((0,), (0,)), ((), ()))
    for q in range(group):
        held_low = held_refs[q][0]
        mix = mix_ref[q]
        read = None
        rest = mix[: 2 * window]
        for _ in range(3):
            part = rest.astype(jnp.bfloat16)
            rest = rest - part.astype(jnp.float32)
            term = lax.dot_general(part, held_low, nt, preferred_element_type=jnp.float32)
            read = term if read is None else read + term
        read_ref[q] = read
        weight = weight_ref[q]
        entry = mix[window : 3 * window]
        w_hi = weight.astype(jnp.bfloat16)
        w_lo = (weight - w_hi.astype(jnp.float32)).astype(jnp.bfloat16)
        e_hi = entry.astype(jnp.bfloat16)
        e_lo = (entry - e_hi.astype(jnp.float32)).astype(jnp.bfloat16)
        pushed = (
            lax.dot_general(w_hi, e_hi, tn, preferred_element_type=jnp.float32)
            + lax.dot_general(w_hi, e_lo, tn, preferred_element_type=jnp.float32)
            + lax.dot_general(w_lo, e_hi, tn, preferred_element_type=jnp.float32)
        )
        held = held_low.astype(jnp.float32)
        rows = held.shape[0] // heads
        carry = mix[2 * window : 2 * window + 1]
        for h in range(heads):
            part = slice(h * rows, (h + 1) * rows)
            out_ref[q, part] = (carry[:, h : h + 1] * held[part] + pushed[part]).astype(
                out_ref.dtype
            )


def recurrence(received, rows, mix, weight, state_rows, heads, group=4):
    slot_count, _, lanes = received.shape
    window = mix.shape[1] // 4
    held_specs = [
        pl.BlockSpec((1, state_rows, lanes), lambda i, r, q=q: (r[i * group + q], 0, 0))
        for q in range(group)
    ]
    grid_spec = pltpu.PrefetchScalarGridSpec(
        num_scalar_prefetch=1,
        grid=(slot_count // group,),
        in_specs=held_specs
        + [
            pl.BlockSpec((group, 4 * window, lanes), lambda i, r: (i, 0, 0)),
            pl.BlockSpec((group, 2 * window, state_rows), lambda i, r: (i, 0, 0)),
        ],
        out_specs=[
            pl.BlockSpec((group, 2 * window, state_rows), lambda i, r: (i, 0, 0)),
            pl.BlockSpec((group, state_rows, lanes), lambda i, r: (i, 0, 0)),
        ],
    )
    return pl.pallas_call(
        functools.partial(recurrence_kernel, group=group, window=window, heads=heads),
        grid_spec=grid_spec,
        out_shape=[
            jax.ShapeDtypeStruct((slot_count, 2 * window, state_rows), jnp.float32),
            jax.ShapeDtypeStruct((slot_count, state_rows, lanes), jnp.bfloat16),
        ],
    )(rows, *([received] * group), mix, weight)


def migrate(item, mig_dest, slot_count, groups, device):
    length = item.shape[0]
    piece = -(-length // groups)
    padded = jnp.pad(item, (0, piece * groups - length)).reshape(groups, piece)
    first = lax.all_to_all(padded, "req", 0, 0, tiled=True)
    dest_dev = mig_dest // slot_count
    order = invert(dest_dev, groups)
    pick = (order[:, None] == jnp.arange(groups, dtype=jnp.int32)[None, :]).astype(first.dtype)
    routed = jnp.dot(pick, first, preferred_element_type=jnp.float32).astype(first.dtype)
    second = lax.all_to_all(routed, "req", 0, 0, tiled=True)
    arrived = second.reshape(-1)[:length]
    target_local = mig_dest[order[device]] - device * slot_count
    return arrived, target_local


def local(
    tokens,
    pre_gain,
    inner_weight,
    shared_weight,
    conv_inner,
    conv_inner_bias,
    conv_shared,
    conv_shared_bias,
    step_bias,
    decay_log,
    skip_gain,
    gate_gain,
    out_weight,
    states,
    edge_inner,
    edge_shared,
    counts,
    mig_ids,
    mig_dest,
    reorder,
):
    slot_count, heads_here, head_dim, state_dim = states.shape
    inner_here = heads_here * head_dim
    lanes = state_dim
    groups = lax.axis_size("req")
    device = lax.axis_index("req")
    first_slot = device * slot_count
    stride = (slot_count + groups - 1) // groups
    all_slots = jnp.arange(slot_count * groups, dtype=jnp.int32)

    rows_in = tokens.astype(jnp.float32)
    normed = (
        rows_in * lax.rsqrt(jnp.mean(rows_in * rows_in, axis=-1, keepdims=True) + EPS) * pre_gain
    ).astype(jnp.bfloat16)
    inner_flat = inner_weight.reshape(inner_weight.shape[0], 2 * inner_here)
    piece_rows = lax.all_gather(normed, "head", axis=0, tiled=True)
    inner_rows = jnp.dot(piece_rows, inner_flat, preferred_element_type=jnp.float32).astype(
        jnp.bfloat16
    )
    shared_rows = jnp.dot(piece_rows, shared_weight, preferred_element_type=jnp.float32).astype(
        jnp.bfloat16
    )

    state_rows = heads_here * head_dim * state_dim // lanes
    inner_edge_rows = edge_inner.shape[1] * edge_inner.shape[2] // lanes
    shared_edge_rows = edge_shared.shape[1] * edge_shared.shape[2] // lanes
    packed = jnp.concatenate(
        [
            states.reshape(slot_count, state_rows, lanes),
            edge_inner.reshape(slot_count, inner_edge_rows, lanes),
            edge_shared.reshape(slot_count, shared_edge_rows, lanes),
        ],
        axis=1,
    )
    row_total = packed.shape[1]

    moving = mig_ids.shape[0] // groups
    own_id = mig_ids[device * moving]
    mig_local = own_id - first_slot
    item = jnp.concatenate(
        [
            lax.dynamic_index_in_dim(part, mig_local, 0, keepdims=False).reshape(-1)
            for part in (states, edge_inner, edge_shared)
        ]
    )
    arrived, target_local = migrate(item, mig_dest, slot_count, groups, device)
    arrived = arrived.reshape(row_total, lanes)

    send_rows, recv_rows = route_rows(reorder, first_slot, slot_count, all_slots, stride)
    buffer_rows = groups * stride
    send_idx = invert(send_rows, buffer_rows)
    send_buf = jnp.where(
        (send_idx == target_local)[:, None, None], arrived[None], packed[send_idx]
    )
    received = lax.all_to_all(send_buf, "req", 0, 0, tiled=True)
    moved = received[:, state_rows:][recv_rows]
    moved_inner = moved[:, :inner_edge_rows].reshape(edge_inner.shape)
    moved_shared = moved[:, inner_edge_rows:].reshape(edge_shared.shape)

    window = inner_rows.shape[0] // slot_count
    inner_rows = inner_rows.reshape(slot_count, window, 2 * inner_here)
    shared_rows = shared_rows.reshape(slot_count, window, shared_rows.shape[1])
    gate_part = inner_rows[:, :, :inner_here]
    value_part = inner_rows[:, :, inner_here:]
    fresh_shared = shared_rows[:, :, : 2 * state_dim]
    head_index = lax.axis_index("head")
    step_raw = lax.dynamic_slice_in_dim(
        shared_rows[:, :, 2 * state_dim :], head_index * heads_here, heads_here, axis=2
    )
    edge_inner_out = new_edge(moved_inner, value_part, counts)
    edge_shared_out = new_edge(moved_shared, fresh_shared, counts)
    mixed_inner = depthwise(moved_inner, value_part, conv_inner, conv_inner_bias)
    mixed_shared = depthwise(moved_shared, fresh_shared, conv_shared, conv_shared_bias)
    valid = jnp.arange(window)[None, :] < counts[:, None]
    step_size = jax.nn.softplus(step_raw.astype(jnp.float32) + step_bias)
    step_size = jnp.where(valid[:, :, None], step_size, 0.0)
    decay = -jnp.exp(decay_log)
    entries = mixed_shared[:, :, :state_dim]
    readouts = mixed_shared[:, :, state_dim:]

    factor = jnp.exp(step_size * decay)
    cum = [factor[:, 0]]
    for t in range(1, window):
        cum.append(cum[-1] * factor[:, t])
    span = {}
    for t in range(window):
        span[(t, t)] = jnp.ones_like(factor[:, 0])
        for s in range(t - 1, -1, -1):
            span[(t, s)] = span[(t, s + 1)] * factor[:, s + 1]

    def per_head(v):
        return jnp.repeat(v, head_dim, axis=-1)

    flat_inputs = mixed_inner.reshape(slot_count, window, inner_here)
    weighted = per_head(step_size) * flat_inputs
    last = window - 1
    pushed = jnp.stack([per_head(span[(last, s)]) * weighted[:, s] for s in range(window)], axis=1)
    weight = jnp.concatenate([pushed, jnp.zeros_like(pushed)], axis=1)
    carry = jnp.pad(cum[last], ((0, 0), (0, state_dim - heads_here)))[:, None, :]
    mix = jnp.concatenate(
        [readouts, entries, carry, jnp.zeros((slot_count, 2 * window - 1, state_dim), jnp.float32)],
        axis=1,
    )
    read, states_out = recurrence(received, recv_rows, mix, weight, state_rows, heads_here)
    states_out = states_out.reshape(states.shape)
    overlap = jnp.einsum("rtn,rsn->rts", readouts, entries, precision=HIGH)
    skip_wide = jnp.repeat(skip_gain, head_dim)
    produced = []
    for t in range(window):
        acc = per_head(cum[t]) * read[:, t]
        for s in range(t + 1):
            acc = acc + per_head(span[(t, s)] * overlap[:, t, s, None]) * weighted[:, s]
        produced.append(acc + skip_wide * flat_inputs[:, t])
    outputs = jnp.stack(produced, axis=1)

    gated = outputs * jax.nn.silu(gate_part.astype(jnp.float32))
    square_part = jnp.sum(gated * gated, axis=-1).reshape(slot_count * window, 1)
    pre_scaled = (
        jnp.where(valid[:, :, None], gated * gate_gain, 0.0)
        .astype(jnp.bfloat16)
        .reshape(slot_count * window, inner_here)
    )
    partial = jnp.dot(pre_scaled, out_weight, preferred_element_type=jnp.float32)
    extra = jnp.broadcast_to(square_part, (partial.shape[0], 128))
    combined = jnp.concatenate([partial, extra], axis=1)
    reduced = lax.psum_scatter(combined, "head", scatter_dimension=0, tiled=True)
    full_inner = inner_here * lax.axis_size("head")
    scale = lax.rsqrt(reduced[:, -1:] / full_inner + EPS)
    hidden_out = (rows_in + reduced[:, : partial.shape[1]] * scale).astype(jnp.bfloat16)
    return (hidden_out, states_out, edge_inner_out, edge_shared_out)


def solution(mesh):
    placed = (
        P(("req", "head"), None),
        P(),
        P(None, None, "head"),
        P(),
        P(None, "head"),
        P("head"),
        P(),
        P(),
        P("head"),
        P("head"),
        P("head"),
        P("head"),
        P("head", None),
        P("req", "head", None, None),
        P("req", None, "head"),
        P("req", None, None),
        P("req"),
        P(),
        P(),
        P(),
    )
    return jax.shard_map(
        local,
        mesh=mesh,
        in_specs=placed,
        out_specs=(
            P(("req", "head"), None),
            P("req", "head", None, None),
            P("req", None, "head"),
            P("req", None, None),
        ),
        check_vma=False,
    )
```

```python
import functools

import jax
import jax.numpy as jnp
from jax import lax
from jax.sharding import PartitionSpec as P
from jax.experimental import pallas as pl
from jax.experimental.pallas import tpu as pltpu

EPS = 1e-05
HIGH = lax.Precision.HIGHEST


def depthwise(edge, fresh, weight, offset_bias):
    sequence = jnp.concatenate([edge, fresh], axis=1).astype(jnp.float32)
    window = fresh.shape[1]
    summed = sequence[:, 0:window] * weight[0]
    for offset in range(1, weight.shape[0]):
        summed = summed + sequence[:, offset : offset + window] * weight[offset]
    return jax.nn.silu(summed + offset_bias)


def new_edge(edge, fresh, counts):
    sequence = jnp.concatenate([edge, fresh], axis=1)
    keep_rows = edge.shape[1]
    result = edge
    for length in range(1, fresh.shape[1] + 1):
        result = jnp.where(
            (counts == length)[:, None, None], sequence[:, length : length + keep_rows], result
        )
    return result


def rank_rows(partner, position, capacity):
    matching = partner[:, None] == partner[None, :]
    earlier = position[None, :] < position[:, None]
    ranking = jnp.sum(jnp.logical_and(matching, earlier), axis=1)
    return partner * capacity + ranking


def invert(values, size):
    hits = values[None, :] == jnp.arange(size, dtype=jnp.int32)[:, None]
    return jnp.sum(jnp.where(hits, jnp.arange(values.shape[0], dtype=jnp.int32)[None, :], 0), axis=1)


def route_rows(anchor, first_slot, slot_count, all_slots, capacity):
    mine = first_slot + jnp.arange(slot_count, dtype=jnp.int32)
    hits = anchor[None, :] == mine[:, None]
    targets = jnp.sum(jnp.where(hits, all_slots[None, :], 0), axis=1)
    send_rows = rank_rows(targets // slot_count, targets % slot_count, capacity)
    sources = lax.dynamic_slice_in_dim(anchor, first_slot, slot_count)
    recv_rows = rank_rows(sources // slot_count, jnp.arange(slot_count, dtype=jnp.int32), capacity)
    return (send_rows, recv_rows)


def recurrence_kernel(rows_ref, *refs, group, window, heads):
    held_refs = refs[:group]
    mix_ref, weight_ref, read_ref, out_ref = refs[group:]
    nt = (((1,), (1,)), ((), ()))
    tn = (((0,), (0,)), ((), ()))
    for q in range(group):
        held_low = held_refs[q][0]
        mix = mix_ref[q]
        read = None
        rest = mix[: 2 * window]
        for _ in range(3):
            part = rest.astype(jnp.bfloat16)
            rest = rest - part.astype(jnp.float32)
            term = lax.dot_general(part, held_low, nt, preferred_element_type=jnp.float32)
            read = term if read is None else read + term
        read_ref[q] = read
        weight = weight_ref[q]
        entry = mix[window : 3 * window]
        w_hi = weight.astype(jnp.bfloat16)
        w_lo = (weight - w_hi.astype(jnp.float32)).astype(jnp.bfloat16)
        e_hi = entry.astype(jnp.bfloat16)
        e_lo = (entry - e_hi.astype(jnp.float32)).astype(jnp.bfloat16)
        pushed = (
            lax.dot_general(w_hi, e_hi, tn, preferred_element_type=jnp.float32)
            + lax.dot_general(w_hi, e_lo, tn, preferred_element_type=jnp.float32)
            + lax.dot_general(w_lo, e_hi, tn, preferred_element_type=jnp.float32)
        )
        held = held_low.astype(jnp.float32)
        rows = held.shape[0] // heads
        carry = mix[2 * window : 2 * window + 1]
        for h in range(heads):
            part = slice(h * rows, (h + 1) * rows)
            out_ref[q, part] = (carry[:, h : h + 1] * held[part] + pushed[part]).astype(
                out_ref.dtype
            )


def recurrence(received, rows, mix, weight, state_rows, heads, group=4):
    slot_count, _, lanes = received.shape
    window = mix.shape[1] // 4
    held_specs = [
        pl.BlockSpec((1, state_rows, lanes), lambda i, r, q=q: (r[i * group + q], 0, 0))
        for q in range(group)
    ]
    grid_spec = pltpu.PrefetchScalarGridSpec(
        num_scalar_prefetch=1,
        grid=(slot_count // group,),
        in_specs=held_specs
        + [
            pl.BlockSpec((group, 4 * window, lanes), lambda i, r: (i, 0, 0)),
            pl.BlockSpec((group, 2 * window, state_rows), lambda i, r: (i, 0, 0)),
        ],
        out_specs=[
            pl.BlockSpec((group, 2 * window, state_rows), lambda i, r: (i, 0, 0)),
            pl.BlockSpec((group, state_rows, lanes), lambda i, r: (i, 0, 0)),
        ],
    )
    return pl.pallas_call(
        functools.partial(recurrence_kernel, group=group, window=window, heads=heads),
        grid_spec=grid_spec,
        out_shape=[
            jax.ShapeDtypeStruct((slot_count, 2 * window, state_rows), jnp.float32),
            jax.ShapeDtypeStruct((slot_count, state_rows, lanes), jnp.bfloat16),
        ],
    )(rows, *([received] * group), mix, weight)

MESH = pl.DeviceIdType.MESH


def scatter_sum_kernel(x_ref, out_ref, slots, send_sem, recv_sem, *, n, rows):
    me = lax.axis_index("head")
    group = lax.axis_index("req")
    barrier = pltpu.get_barrier_semaphore()
    for k in range(1, n):
        pl.semaphore_signal(
            barrier, inc=1, device_id=(group, lax.rem(me + k, n)), device_id_type=MESH
        )
    pl.semaphore_wait(barrier, n - 1)
    copies = []
    for k in range(1, n):
        peer = lax.rem(me + k, n)
        start = pl.multiple_of(peer * rows, rows)
        copy = pltpu.make_async_remote_copy(
            src_ref=x_ref.at[pl.ds(start, rows)],
            dst_ref=slots.at[k - 1],
            send_sem=send_sem.at[k - 1],
            recv_sem=recv_sem.at[k - 1],
            device_id=(group, peer),
            device_id_type=MESH,
        )
        copy.start()
        copies.append(copy)
    own = pl.multiple_of(me * rows, rows)
    total = x_ref[pl.ds(own, rows)].astype(jnp.float32)
    for k, copy in enumerate(copies):
        copy.wait()
        total = total + slots[k].astype(jnp.float32)
    out_ref[...] = total


def scatter_sum(x, n):
    rows = x.shape[0] // n
    return pl.pallas_call(
        functools.partial(scatter_sum_kernel, n=n, rows=rows),
        out_shape=jax.ShapeDtypeStruct((rows, x.shape[1]), jnp.float32),
        in_specs=[pl.BlockSpec(memory_space=pltpu.VMEM)],
        out_specs=pl.BlockSpec(memory_space=pltpu.VMEM),
        scratch_shapes=[
            pltpu.VMEM((n - 1, rows, x.shape[1]), x.dtype),
            pltpu.SemaphoreType.DMA((n - 1,)),
            pltpu.SemaphoreType.DMA((n - 1,)),
        ],
        compiler_params=pltpu.CompilerParams(collective_id=0, has_side_effects=True),
    )(x)


def migrate(item, mig_dest, slot_count, groups, device):
    length = item.shape[0]
    piece = -(-length // groups)
    padded = jnp.pad(item, (0, piece * groups - length)).reshape(groups, piece)
    first = lax.all_to_all(padded, "req", 0, 0, tiled=True)
    dest_dev = mig_dest // slot_count
    order = invert(dest_dev, groups)
    pick = (order[:, None] == jnp.arange(groups, dtype=jnp.int32)[None, :]).astype(first.dtype)
    routed = jnp.dot(pick, first, preferred_element_type=jnp.float32).astype(first.dtype)
    second = lax.all_to_all(routed, "req", 0, 0, tiled=True)
    arrived = second.reshape(-1)[:length]
    target_local = mig_dest[order[device]] - device * slot_count
    return arrived, target_local


def local(
    tokens,
    pre_gain,
    inner_weight,
    shared_weight,
    conv_inner,
    conv_inner_bias,
    conv_shared,
    conv_shared_bias,
    step_bias,
    decay_log,
    skip_gain,
    gate_gain,
    out_weight,
    states,
    edge_inner,
    edge_shared,
    counts,
    mig_ids,
    mig_dest,
    reorder,
):
    slot_count, heads_here, head_dim, state_dim = states.shape
    inner_here = heads_here * head_dim
    lanes = state_dim
    groups = lax.axis_size("req")
    device = lax.axis_index("req")
    first_slot = device * slot_count
    stride = (slot_count + groups - 1) // groups
    all_slots = jnp.arange(slot_count * groups, dtype=jnp.int32)

    rows_in = tokens.astype(jnp.float32)
    normed = (
        rows_in * lax.rsqrt(jnp.mean(rows_in * rows_in, axis=-1, keepdims=True) + EPS) * pre_gain
    ).astype(jnp.bfloat16)
    inner_flat = inner_weight.reshape(inner_weight.shape[0], 2 * inner_here)
    piece_rows = lax.all_gather(normed, "head", axis=0, tiled=True)
    inner_rows = jnp.dot(piece_rows, inner_flat, preferred_element_type=jnp.float32).astype(
        jnp.bfloat16
    )
    shared_rows = jnp.dot(piece_rows, shared_weight, preferred_element_type=jnp.float32).astype(
        jnp.bfloat16
    )

    state_rows = heads_here * head_dim * state_dim // lanes
    inner_edge_rows = edge_inner.shape[1] * edge_inner.shape[2] // lanes
    shared_edge_rows = edge_shared.shape[1] * edge_shared.shape[2] // lanes
    packed = jnp.concatenate(
        [
            states.reshape(slot_count, state_rows, lanes),
            edge_inner.reshape(slot_count, inner_edge_rows, lanes),
            edge_shared.reshape(slot_count, shared_edge_rows, lanes),
        ],
        axis=1,
    )
    row_total = packed.shape[1]

    moving = mig_ids.shape[0] // groups
    own_id = mig_ids[device * moving]
    mig_local = own_id - first_slot
    item = jnp.concatenate(
        [
            lax.dynamic_index_in_dim(part, mig_local, 0, keepdims=False).reshape(-1)
            for part in (states, edge_inner, edge_shared)
        ]
    )
    arrived, target_local = migrate(item, mig_dest, slot_count, groups, device)
    arrived = arrived.reshape(row_total, lanes)

    send_rows, recv_rows = route_rows(reorder, first_slot, slot_count, all_slots, stride)
    buffer_rows = groups * stride
    send_idx = invert(send_rows, buffer_rows)
    send_buf = jnp.where(
        (send_idx == target_local)[:, None, None], arrived[None], packed[send_idx]
    )
    received = lax.all_to_all(send_buf, "req", 0, 0, tiled=True)
    moved = received[:, state_rows:][recv_rows]
    moved_inner = moved[:, :inner_edge_rows].reshape(edge_inner.shape)
    moved_shared = moved[:, inner_edge_rows:].reshape(edge_shared.shape)

    window = inner_rows.shape[0] // slot_count
    inner_rows = inner_rows.reshape(slot_count, window, 2 * inner_here)
    shared_rows = shared_rows.reshape(slot_count, window, shared_rows.shape[1])
    gate_part = inner_rows[:, :, :inner_here]
    value_part = inner_rows[:, :, inner_here:]
    fresh_shared = shared_rows[:, :, : 2 * state_dim]
    head_index = lax.axis_index("head")
    step_raw = lax.dynamic_slice_in_dim(
        shared_rows[:, :, 2 * state_dim :], head_index * heads_here, heads_here, axis=2
    )
    edge_inner_out = new_edge(moved_inner, value_part, counts)
    edge_shared_out = new_edge(moved_shared, fresh_shared, counts)
    mixed_inner = depthwise(moved_inner, value_part, conv_inner, conv_inner_bias)
    mixed_shared = depthwise(moved_shared, fresh_shared, conv_shared, conv_shared_bias)
    valid = jnp.arange(window)[None, :] < counts[:, None]
    step_size = jax.nn.softplus(step_raw.astype(jnp.float32) + step_bias)
    step_size = jnp.where(valid[:, :, None], step_size, 0.0)
    decay = -jnp.exp(decay_log)
    entries = mixed_shared[:, :, :state_dim]
    readouts = mixed_shared[:, :, state_dim:]

    factor = jnp.exp(step_size * decay)
    cum = [factor[:, 0]]
    for t in range(1, window):
        cum.append(cum[-1] * factor[:, t])
    span = {}
    for t in range(window):
        span[(t, t)] = jnp.ones_like(factor[:, 0])
        for s in range(t - 1, -1, -1):
            span[(t, s)] = span[(t, s + 1)] * factor[:, s + 1]

    def per_head(v):
        return jnp.repeat(v, head_dim, axis=-1)

    flat_inputs = mixed_inner.reshape(slot_count, window, inner_here)
    weighted = per_head(step_size) * flat_inputs
    last = window - 1
    pushed = jnp.stack([per_head(span[(last, s)]) * weighted[:, s] for s in range(window)], axis=1)
    weight = jnp.concatenate([pushed, jnp.zeros_like(pushed)], axis=1)
    carry = jnp.pad(cum[last], ((0, 0), (0, state_dim - heads_here)))[:, None, :]
    mix = jnp.concatenate(
        [readouts, entries, carry, jnp.zeros((slot_count, 2 * window - 1, state_dim), jnp.float32)],
        axis=1,
    )
    read, states_out = recurrence(received, recv_rows, mix, weight, state_rows, heads_here)
    states_out = states_out.reshape(states.shape)
    overlap = jnp.einsum("rtn,rsn->rts", readouts, entries, precision=HIGH)
    skip_wide = jnp.repeat(skip_gain, head_dim)
    produced = []
    for t in range(window):
        acc = per_head(cum[t]) * read[:, t]
        for s in range(t + 1):
            acc = acc + per_head(span[(t, s)] * overlap[:, t, s, None]) * weighted[:, s]
        produced.append(acc + skip_wide * flat_inputs[:, t])
    outputs = jnp.stack(produced, axis=1)

    gated = outputs * jax.nn.silu(gate_part.astype(jnp.float32))
    square_part = jnp.sum(gated * gated, axis=-1).reshape(slot_count * window, 1)
    pre_scaled = (
        jnp.where(valid[:, :, None], gated * gate_gain, 0.0)
        .astype(jnp.bfloat16)
        .reshape(slot_count * window, inner_here)
    )
    partial = jnp.dot(pre_scaled, out_weight, preferred_element_type=jnp.float32)
    square_hi = square_part.astype(jnp.bfloat16)
    square_lo = (square_part - square_hi.astype(jnp.float32)).astype(jnp.bfloat16)
    extra = jnp.pad(
        jnp.concatenate([square_hi, square_lo], axis=1), ((0, 0), (0, 126))
    )
    combined = jnp.concatenate([partial.astype(jnp.bfloat16), extra], axis=1)
    reduced = scatter_sum(combined, lax.axis_size("head"))
    full_inner = inner_here * lax.axis_size("head")
    width = partial.shape[1]
    square_sum = reduced[:, width : width + 1] + reduced[:, width + 1 : width + 2]
    scale = lax.rsqrt(square_sum / full_inner + EPS)
    hidden_out = (rows_in + reduced[:, :width] * scale).astype(jnp.bfloat16)
    return (hidden_out, states_out, edge_inner_out, edge_shared_out)


def solution(mesh):
    placed = (
        P(("req", "head"), None),
        P(),
        P(None, None, "head"),
        P(),
        P(None, "head"),
        P("head"),
        P(),
        P(),
        P("head"),
        P("head"),
        P("head"),
        P("head"),
        P("head", None),
        P("req", "head", None, None),
        P("req", None, "head"),
        P("req", None, None),
        P("req"),
        P(),
        P(),
        P(),
    )
    return jax.shard_map(
        local,
        mesh=mesh,
        in_specs=placed,
        out_specs=(
            P(("req", "head"), None),
            P("req", "head", None, None),
            P("req", None, "head"),
            P("req", None, None),
        ),
        check_vma=False,
    )
```

```python
import functools

import jax
import jax.numpy as jnp
from jax import lax
from jax.sharding import PartitionSpec as P
from jax.experimental import pallas as pl
from jax.experimental.pallas import tpu as pltpu

EPS = 1e-05
HIGH = lax.Precision.HIGHEST


def depthwise(edge, fresh, weight, offset_bias):
    sequence = jnp.concatenate([edge, fresh], axis=1).astype(jnp.float32)
    window = fresh.shape[1]
    summed = sequence[:, 0:window] * weight[0]
    for offset in range(1, weight.shape[0]):
        summed = summed + sequence[:, offset : offset + window] * weight[offset]
    return jax.nn.silu(summed + offset_bias)


def new_edge(edge, fresh, counts):
    sequence = jnp.concatenate([edge, fresh], axis=1)
    keep_rows = edge.shape[1]
    result = edge
    for length in range(1, fresh.shape[1] + 1):
        result = jnp.where(
            (counts == length)[:, None, None], sequence[:, length : length + keep_rows], result
        )
    return result


def rank_rows(partner, position, capacity):
    matching = partner[:, None] == partner[None, :]
    earlier = position[None, :] < position[:, None]
    ranking = jnp.sum(jnp.logical_and(matching, earlier), axis=1)
    return partner * capacity + ranking


def invert(values, size):
    hits = values[None, :] == jnp.arange(size, dtype=jnp.int32)[:, None]
    return jnp.sum(jnp.where(hits, jnp.arange(values.shape[0], dtype=jnp.int32)[None, :], 0), axis=1)


def route_rows(anchor, first_slot, slot_count, all_slots, capacity):
    mine = first_slot + jnp.arange(slot_count, dtype=jnp.int32)
    hits = anchor[None, :] == mine[:, None]
    targets = jnp.sum(jnp.where(hits, all_slots[None, :], 0), axis=1)
    send_rows = rank_rows(targets // slot_count, targets % slot_count, capacity)
    sources = lax.dynamic_slice_in_dim(anchor, first_slot, slot_count)
    recv_rows = rank_rows(sources // slot_count, jnp.arange(slot_count, dtype=jnp.int32), capacity)
    return (send_rows, recv_rows)


def recurrence_kernel(rows_ref, *refs, group, window, heads):
    held_refs = refs[:group]
    mix_ref, weight_ref, read_ref, out_ref = refs[group:]
    nt = (((1,), (1,)), ((), ()))
    tn = (((0,), (0,)), ((), ()))
    for q in range(group):
        held_low = held_refs[q][0]
        mix = mix_ref[q]
        read = None
        rest = mix[: 2 * window]
        for _ in range(3):
            part = rest.astype(jnp.bfloat16)
            rest = rest - part.astype(jnp.float32)
            term = lax.dot_general(part, held_low, nt, preferred_element_type=jnp.float32)
            read = term if read is None else read + term
        read_ref[q] = read
        weight = weight_ref[q]
        entry = mix[window : 3 * window]
        w_hi = weight.astype(jnp.bfloat16)
        w_lo = (weight - w_hi.astype(jnp.float32)).astype(jnp.bfloat16)
        e_hi = entry.astype(jnp.bfloat16)
        e_lo = (entry - e_hi.astype(jnp.float32)).astype(jnp.bfloat16)
        pushed = (
            lax.dot_general(w_hi, e_hi, tn, preferred_element_type=jnp.float32)
            + lax.dot_general(w_hi, e_lo, tn, preferred_element_type=jnp.float32)
            + lax.dot_general(w_lo, e_hi, tn, preferred_element_type=jnp.float32)
        )
        held = held_low.astype(jnp.float32)
        rows = held.shape[0] // heads
        carry = mix[2 * window : 2 * window + 1]
        for h in range(heads):
            part = slice(h * rows, (h + 1) * rows)
            out_ref[q, part] = (carry[:, h : h + 1] * held[part] + pushed[part]).astype(
                out_ref.dtype
            )


def recurrence(received, rows, mix, weight, state_rows, heads, group=4):
    slot_count, _, lanes = received.shape
    window = mix.shape[1] // 4
    held_specs = [
        pl.BlockSpec((1, state_rows, lanes), lambda i, r, q=q: (r[i * group + q], 0, 0))
        for q in range(group)
    ]
    grid_spec = pltpu.PrefetchScalarGridSpec(
        num_scalar_prefetch=1,
        grid=(slot_count // group,),
        in_specs=held_specs
        + [
            pl.BlockSpec((group, 4 * window, lanes), lambda i, r: (i, 0, 0)),
            pl.BlockSpec((group, 2 * window, state_rows), lambda i, r: (i, 0, 0)),
        ],
        out_specs=[
            pl.BlockSpec((group, 2 * window, state_rows), lambda i, r: (i, 0, 0)),
            pl.BlockSpec((group, state_rows, lanes), lambda i, r: (i, 0, 0)),
        ],
    )
    return pl.pallas_call(
        functools.partial(recurrence_kernel, group=group, window=window, heads=heads),
        grid_spec=grid_spec,
        out_shape=[
            jax.ShapeDtypeStruct((slot_count, 2 * window, state_rows), jnp.float32),
            jax.ShapeDtypeStruct((slot_count, state_rows, lanes), jnp.bfloat16),
        ],
    )(rows, *([received] * group), mix, weight)

MESH = pl.DeviceIdType.MESH


def scatter_sum_kernel(x_ref, out_ref, slots, send_sem, recv_sem, *, n, rows):
    me = lax.axis_index("head")
    group = lax.axis_index("req")
    barrier = pltpu.get_barrier_semaphore()
    for k in range(1, n):
        pl.semaphore_signal(
            barrier, inc=1, device_id=(group, lax.rem(me + k, n)), device_id_type=MESH
        )
    pl.semaphore_wait(barrier, n - 1)
    copies = []
    for k in range(1, n):
        peer = lax.rem(me + k, n)
        start = pl.multiple_of(peer * rows, rows)
        copy = pltpu.make_async_remote_copy(
            src_ref=x_ref.at[pl.ds(start, rows)],
            dst_ref=slots.at[k - 1],
            send_sem=send_sem.at[k - 1],
            recv_sem=recv_sem.at[k - 1],
            device_id=(group, peer),
            device_id_type=MESH,
        )
        copy.start()
        copies.append(copy)
    own = pl.multiple_of(me * rows, rows)
    total = x_ref[pl.ds(own, rows)].astype(jnp.float32)
    for k, copy in enumerate(copies):
        copy.wait()
        total = total + slots[k].astype(jnp.float32)
    out_ref[...] = total


def scatter_sum(x, n):
    rows = x.shape[0] // n
    return pl.pallas_call(
        functools.partial(scatter_sum_kernel, n=n, rows=rows),
        out_shape=jax.ShapeDtypeStruct((rows, x.shape[1]), jnp.float32),
        in_specs=[pl.BlockSpec(memory_space=pltpu.VMEM)],
        out_specs=pl.BlockSpec(memory_space=pltpu.VMEM),
        scratch_shapes=[
            pltpu.VMEM((n - 1, rows, x.shape[1]), x.dtype),
            pltpu.SemaphoreType.DMA((n - 1,)),
            pltpu.SemaphoreType.DMA((n - 1,)),
        ],
        compiler_params=pltpu.CompilerParams(collective_id=0, has_side_effects=True),
    )(x)


def exchange_kernel(x_ref, out_ref, send_sem, recv_sem, local_sem, *, n):
    me = lax.axis_index("req")
    head = lax.axis_index("head")
    barrier = pltpu.get_barrier_semaphore()
    for k in range(1, n):
        pl.semaphore_signal(
            barrier, inc=1, device_id=(lax.rem(me + k, n), head), device_id_type=MESH
        )
    pl.semaphore_wait(barrier, n - 1)
    own = pltpu.make_async_copy(x_ref.at[me], out_ref.at[me], local_sem.at[0])
    own.start()
    copies = []
    for k in range(1, n):
        peer = lax.rem(me + k, n)
        copy = pltpu.make_async_remote_copy(
            src_ref=x_ref.at[peer],
            dst_ref=out_ref.at[me],
            send_sem=send_sem.at[k - 1],
            recv_sem=recv_sem.at[k - 1],
            device_id=(peer, head),
            device_id_type=MESH,
        )
        copy.start()
        copies.append(copy)
    own.wait()
    for copy in copies:
        copy.wait()


def exchange(x, tag):
    n = x.shape[0]
    return pl.pallas_call(
        functools.partial(exchange_kernel, n=n),
        out_shape=jax.ShapeDtypeStruct(x.shape, x.dtype),
        in_specs=[pl.BlockSpec(memory_space=pl.ANY)],
        out_specs=pl.BlockSpec(memory_space=pl.ANY),
        scratch_shapes=[
            pltpu.SemaphoreType.DMA((n - 1,)),
            pltpu.SemaphoreType.DMA((n - 1,)),
            pltpu.SemaphoreType.DMA((1,)),
        ],
        compiler_params=pltpu.CompilerParams(collective_id=tag, has_side_effects=True),
    )(x)


def migrate(item, mig_dest, slot_count, groups, device):
    length = item.shape[0]
    lanes = 128
    piece = -(-length // (groups * lanes)) * lanes
    padded = jnp.pad(item, (0, piece * groups - length)).reshape(groups, piece // lanes, lanes)
    first = exchange(padded, 1).reshape(groups, piece)
    dest_dev = mig_dest // slot_count
    order = invert(dest_dev, groups)
    pick = (order[:, None] == jnp.arange(groups, dtype=jnp.int32)[None, :]).astype(first.dtype)
    routed = jnp.dot(pick, first, preferred_element_type=jnp.float32).astype(first.dtype)
    second = exchange(routed.reshape(groups, piece // lanes, lanes), 2)
    arrived = second.reshape(-1)[:length]
    target_local = mig_dest[order[device]] - device * slot_count
    return arrived, target_local


def local(
    tokens,
    pre_gain,
    inner_weight,
    shared_weight,
    conv_inner,
    conv_inner_bias,
    conv_shared,
    conv_shared_bias,
    step_bias,
    decay_log,
    skip_gain,
    gate_gain,
    out_weight,
    states,
    edge_inner,
    edge_shared,
    counts,
    mig_ids,
    mig_dest,
    reorder,
):
    slot_count, heads_here, head_dim, state_dim = states.shape
    inner_here = heads_here * head_dim
    lanes = state_dim
    groups = lax.axis_size("req")
    device = lax.axis_index("req")
    first_slot = device * slot_count
    stride = (slot_count + groups - 1) // groups
    all_slots = jnp.arange(slot_count * groups, dtype=jnp.int32)

    rows_in = tokens.astype(jnp.float32)
    normed = (
        rows_in * lax.rsqrt(jnp.mean(rows_in * rows_in, axis=-1, keepdims=True) + EPS) * pre_gain
    ).astype(jnp.bfloat16)
    inner_flat = inner_weight.reshape(inner_weight.shape[0], 2 * inner_here)
    piece_rows = lax.all_gather(normed, "head", axis=0, tiled=True)
    inner_rows = jnp.dot(piece_rows, inner_flat, preferred_element_type=jnp.float32).astype(
        jnp.bfloat16
    )
    shared_rows = jnp.dot(piece_rows, shared_weight, preferred_element_type=jnp.float32).astype(
        jnp.bfloat16
    )

    state_rows = heads_here * head_dim * state_dim // lanes
    inner_edge_rows = edge_inner.shape[1] * edge_inner.shape[2] // lanes
    shared_edge_rows = edge_shared.shape[1] * edge_shared.shape[2] // lanes
    packed = jnp.concatenate(
        [
            states.reshape(slot_count, state_rows, lanes),
            edge_inner.reshape(slot_count, inner_edge_rows, lanes),
            edge_shared.reshape(slot_count, shared_edge_rows, lanes),
        ],
        axis=1,
    )
    row_total = packed.shape[1]

    moving = mig_ids.shape[0] // groups
    own_id = mig_ids[device * moving]
    mig_local = own_id - first_slot
    item = jnp.concatenate(
        [
            lax.dynamic_index_in_dim(part, mig_local, 0, keepdims=False).reshape(-1)
            for part in (states, edge_inner, edge_shared)
        ]
    )
    arrived, target_local = migrate(item, mig_dest, slot_count, groups, device)
    arrived = arrived.reshape(row_total, lanes)

    send_rows, recv_rows = route_rows(reorder, first_slot, slot_count, all_slots, stride)
    buffer_rows = groups * stride
    send_idx = invert(send_rows, buffer_rows)
    send_buf = jnp.where(
        (send_idx == target_local)[:, None, None], arrived[None], packed[send_idx]
    )
    received = exchange(send_buf, 3)
    moved = received[:, state_rows:][recv_rows]
    moved_inner = moved[:, :inner_edge_rows].reshape(edge_inner.shape)
    moved_shared = moved[:, inner_edge_rows:].reshape(edge_shared.shape)

    window = inner_rows.shape[0] // slot_count
    inner_rows = inner_rows.reshape(slot_count, window, 2 * inner_here)
    shared_rows = shared_rows.reshape(slot_count, window, shared_rows.shape[1])
    gate_part = inner_rows[:, :, :inner_here]
    value_part = inner_rows[:, :, inner_here:]
    fresh_shared = shared_rows[:, :, : 2 * state_dim]
    head_index = lax.axis_index("head")
    step_raw = lax.dynamic_slice_in_dim(
        shared_rows[:, :, 2 * state_dim :], head_index * heads_here, heads_here, axis=2
    )
    edge_inner_out = new_edge(moved_inner, value_part, counts)
    edge_shared_out = new_edge(moved_shared, fresh_shared, counts)
    mixed_inner = depthwise(moved_inner, value_part, conv_inner, conv_inner_bias)
    mixed_shared = depthwise(moved_shared, fresh_shared, conv_shared, conv_shared_bias)
    valid = jnp.arange(window)[None, :] < counts[:, None]
    step_size = jax.nn.softplus(step_raw.astype(jnp.float32) + step_bias)
    step_size = jnp.where(valid[:, :, None], step_size, 0.0)
    decay = -jnp.exp(decay_log)
    entries = mixed_shared[:, :, :state_dim]
    readouts = mixed_shared[:, :, state_dim:]

    factor = jnp.exp(step_size * decay)
    cum = [factor[:, 0]]
    for t in range(1, window):
        cum.append(cum[-1] * factor[:, t])
    span = {}
    for t in range(window):
        span[(t, t)] = jnp.ones_like(factor[:, 0])
        for s in range(t - 1, -1, -1):
            span[(t, s)] = span[(t, s + 1)] * factor[:, s + 1]

    def per_head(v):
        return jnp.repeat(v, head_dim, axis=-1)

    flat_inputs = mixed_inner.reshape(slot_count, window, inner_here)
    weighted = per_head(step_size) * flat_inputs
    last = window - 1
    pushed = jnp.stack([per_head(span[(last, s)]) * weighted[:, s] for s in range(window)], axis=1)
    weight = jnp.concatenate([pushed, jnp.zeros_like(pushed)], axis=1)
    carry = jnp.pad(cum[last], ((0, 0), (0, state_dim - heads_here)))[:, None, :]
    mix = jnp.concatenate(
        [readouts, entries, carry, jnp.zeros((slot_count, 2 * window - 1, state_dim), jnp.float32)],
        axis=1,
    )
    read, states_out = recurrence(received, recv_rows, mix, weight, state_rows, heads_here)
    states_out = states_out.reshape(states.shape)
    overlap = jnp.einsum("rtn,rsn->rts", readouts, entries, precision=HIGH)
    skip_wide = jnp.repeat(skip_gain, head_dim)
    produced = []
    for t in range(window):
        acc = per_head(cum[t]) * read[:, t]
        for s in range(t + 1):
            acc = acc + per_head(span[(t, s)] * overlap[:, t, s, None]) * weighted[:, s]
        produced.append(acc + skip_wide * flat_inputs[:, t])
    outputs = jnp.stack(produced, axis=1)

    gated = outputs * jax.nn.silu(gate_part.astype(jnp.float32))
    square_part = jnp.sum(gated * gated, axis=-1).reshape(slot_count * window, 1)
    pre_scaled = (
        jnp.where(valid[:, :, None], gated * gate_gain, 0.0)
        .astype(jnp.bfloat16)
        .reshape(slot_count * window, inner_here)
    )
    partial = jnp.dot(pre_scaled, out_weight, preferred_element_type=jnp.float32)
    square_hi = square_part.astype(jnp.bfloat16)
    square_lo = (square_part - square_hi.astype(jnp.float32)).astype(jnp.bfloat16)
    extra = jnp.pad(
        jnp.concatenate([square_hi, square_lo], axis=1), ((0, 0), (0, 126))
    )
    combined = jnp.concatenate([partial.astype(jnp.bfloat16), extra], axis=1)
    reduced = scatter_sum(combined, lax.axis_size("head"))
    full_inner = inner_here * lax.axis_size("head")
    width = partial.shape[1]
    square_sum = reduced[:, width : width + 1] + reduced[:, width + 1 : width + 2]
    scale = lax.rsqrt(square_sum / full_inner + EPS)
    hidden_out = (rows_in + reduced[:, :width] * scale).astype(jnp.bfloat16)
    return (hidden_out, states_out, edge_inner_out, edge_shared_out)


def solution(mesh):
    placed = (
        P(("req", "head"), None),
        P(),
        P(None, None, "head"),
        P(),
        P(None, "head"),
        P("head"),
        P(),
        P(),
        P("head"),
        P("head"),
        P("head"),
        P("head"),
        P("head", None),
        P("req", "head", None, None),
        P("req", None, "head"),
        P("req", None, None),
        P("req"),
        P(),
        P(),
        P(),
    )
    return jax.shard_map(
        local,
        mesh=mesh,
        in_specs=placed,
        out_specs=(
            P(("req", "head"), None),
            P("req", "head", None, None),
            P("req", None, "head"),
            P("req", None, None),
        ),
        check_vma=False,
    )
```

```python
import functools

import jax
import jax.numpy as jnp
from jax import lax
from jax.sharding import PartitionSpec as P
from jax.experimental import pallas as pl
from jax.experimental.pallas import tpu as pltpu

EPS = 1e-05
HIGH = lax.Precision.HIGHEST


def depthwise(edge, fresh, weight, offset_bias):
    sequence = jnp.concatenate([edge, fresh], axis=1).astype(jnp.float32)
    window = fresh.shape[1]
    summed = sequence[:, 0:window] * weight[0]
    for offset in range(1, weight.shape[0]):
        summed = summed + sequence[:, offset : offset + window] * weight[offset]
    return jax.nn.silu(summed + offset_bias)


def new_edge(edge, fresh, counts):
    sequence = jnp.concatenate([edge, fresh], axis=1)
    keep_rows = edge.shape[1]
    result = edge
    for length in range(1, fresh.shape[1] + 1):
        result = jnp.where(
            (counts == length)[:, None, None], sequence[:, length : length + keep_rows], result
        )
    return result


def rank_rows(partner, position, capacity):
    matching = partner[:, None] == partner[None, :]
    earlier = position[None, :] < position[:, None]
    ranking = jnp.sum(jnp.logical_and(matching, earlier), axis=1)
    return partner * capacity + ranking


def invert(values, size):
    hits = values[None, :] == jnp.arange(size, dtype=jnp.int32)[:, None]
    return jnp.sum(jnp.where(hits, jnp.arange(values.shape[0], dtype=jnp.int32)[None, :], 0), axis=1)


def route_rows(anchor, first_slot, slot_count, all_slots, capacity):
    mine = first_slot + jnp.arange(slot_count, dtype=jnp.int32)
    hits = anchor[None, :] == mine[:, None]
    targets = jnp.sum(jnp.where(hits, all_slots[None, :], 0), axis=1)
    send_rows = rank_rows(targets // slot_count, targets % slot_count, capacity)
    sources = lax.dynamic_slice_in_dim(anchor, first_slot, slot_count)
    recv_rows = rank_rows(sources // slot_count, jnp.arange(slot_count, dtype=jnp.int32), capacity)
    return (send_rows, recv_rows)


def recurrence_kernel(rows_ref, *refs, group, window, heads):
    held_refs = refs[:group]
    mix_ref, weight_ref, read_ref, out_ref = refs[group:]
    nt = (((1,), (1,)), ((), ()))
    tn = (((0,), (0,)), ((), ()))
    for q in range(group):
        held_low = held_refs[q][0]
        mix = mix_ref[q]
        read = None
        rest = mix[: 2 * window]
        for _ in range(3):
            part = rest.astype(jnp.bfloat16)
            rest = rest - part.astype(jnp.float32)
            term = lax.dot_general(part, held_low, nt, preferred_element_type=jnp.float32)
            read = term if read is None else read + term
        read_ref[q] = read
        weight = weight_ref[q]
        entry = mix[window : 3 * window]
        w_hi = weight.astype(jnp.bfloat16)
        w_lo = (weight - w_hi.astype(jnp.float32)).astype(jnp.bfloat16)
        e_hi = entry.astype(jnp.bfloat16)
        e_lo = (entry - e_hi.astype(jnp.float32)).astype(jnp.bfloat16)
        pushed = (
            lax.dot_general(w_hi, e_hi, tn, preferred_element_type=jnp.float32)
            + lax.dot_general(w_hi, e_lo, tn, preferred_element_type=jnp.float32)
            + lax.dot_general(w_lo, e_hi, tn, preferred_element_type=jnp.float32)
        )
        held = held_low.astype(jnp.float32)
        rows = held.shape[0] // heads
        carry = mix[2 * window : 2 * window + 1]
        for h in range(heads):
            part = slice(h * rows, (h + 1) * rows)
            out_ref[q, part] = (carry[:, h : h + 1] * held[part] + pushed[part]).astype(
                out_ref.dtype
            )


def recurrence(received, rows, mix, weight, state_rows, heads, group=4):
    slot_count, _, lanes = received.shape
    window = mix.shape[1] // 4
    held_specs = [
        pl.BlockSpec((1, state_rows, lanes), lambda i, r, q=q: (r[i * group + q], 0, 0))
        for q in range(group)
    ]
    grid_spec = pltpu.PrefetchScalarGridSpec(
        num_scalar_prefetch=1,
        grid=(slot_count // group,),
        in_specs=held_specs
        + [
            pl.BlockSpec((group, 4 * window, lanes), lambda i, r: (i, 0, 0)),
            pl.BlockSpec((group, 2 * window, state_rows), lambda i, r: (i, 0, 0)),
        ],
        out_specs=[
            pl.BlockSpec((group, 2 * window, state_rows), lambda i, r: (i, 0, 0)),
            pl.BlockSpec((group, state_rows, lanes), lambda i, r: (i, 0, 0)),
        ],
    )
    return pl.pallas_call(
        functools.partial(recurrence_kernel, group=group, window=window, heads=heads),
        grid_spec=grid_spec,
        out_shape=[
            jax.ShapeDtypeStruct((slot_count, 2 * window, state_rows), jnp.float32),
            jax.ShapeDtypeStruct((slot_count, state_rows, lanes), jnp.bfloat16),
        ],
    )(rows, *([received] * group), mix, weight)

MESH = pl.DeviceIdType.MESH


def scatter_sum_kernel(x_ref, out_ref, slots, send_sem, recv_sem, *, n, rows):
    me = lax.axis_index("head")
    group = lax.axis_index("req")
    barrier = pltpu.get_barrier_semaphore()
    for k in range(1, n):
        pl.semaphore_signal(
            barrier, inc=1, device_id=(group, lax.rem(me + k, n)), device_id_type=MESH
        )
    pl.semaphore_wait(barrier, n - 1)
    copies = []
    for k in range(1, n):
        peer = lax.rem(me + k, n)
        start = pl.multiple_of(peer * rows, rows)
        copy = pltpu.make_async_remote_copy(
            src_ref=x_ref.at[pl.ds(start, rows)],
            dst_ref=slots.at[k - 1],
            send_sem=send_sem.at[k - 1],
            recv_sem=recv_sem.at[k - 1],
            device_id=(group, peer),
            device_id_type=MESH,
        )
        copy.start()
        copies.append(copy)
    own = pl.multiple_of(me * rows, rows)
    total = x_ref[pl.ds(own, rows)].astype(jnp.float32)
    for k, copy in enumerate(copies):
        copy.wait()
        total = total + slots[k].astype(jnp.float32)
    out_ref[...] = total


def scatter_sum(x, n):
    rows = x.shape[0] // n
    return pl.pallas_call(
        functools.partial(scatter_sum_kernel, n=n, rows=rows),
        out_shape=jax.ShapeDtypeStruct((rows, x.shape[1]), jnp.float32),
        in_specs=[pl.BlockSpec(memory_space=pltpu.VMEM)],
        out_specs=pl.BlockSpec(memory_space=pltpu.VMEM),
        scratch_shapes=[
            pltpu.VMEM((n - 1, rows, x.shape[1]), x.dtype),
            pltpu.SemaphoreType.DMA((n - 1,)),
            pltpu.SemaphoreType.DMA((n - 1,)),
        ],
        compiler_params=pltpu.CompilerParams(collective_id=0, has_side_effects=True),
    )(x)


def exchange_kernel(x_ref, out_ref, send_sem, recv_sem, local_sem, *, n):
    me = lax.axis_index("req")
    head = lax.axis_index("head")
    barrier = pltpu.get_barrier_semaphore()
    for k in range(1, n):
        pl.semaphore_signal(
            barrier, inc=1, device_id=(lax.rem(me + k, n), head), device_id_type=MESH
        )
    pl.semaphore_wait(barrier, n - 1)
    own = pltpu.make_async_copy(x_ref.at[me], out_ref.at[me], local_sem.at[0])
    own.start()
    copies = []
    for k in range(1, n):
        peer = lax.rem(me + k, n)
        copy = pltpu.make_async_remote_copy(
            src_ref=x_ref.at[peer],
            dst_ref=out_ref.at[me],
            send_sem=send_sem.at[k - 1],
            recv_sem=recv_sem.at[k - 1],
            device_id=(peer, head),
            device_id_type=MESH,
        )
        copy.start()
        copies.append(copy)
    own.wait()
    for copy in copies:
        copy.wait()


def exchange(x, tag):
    n = x.shape[0]
    return pl.pallas_call(
        functools.partial(exchange_kernel, n=n),
        out_shape=jax.ShapeDtypeStruct(x.shape, x.dtype),
        in_specs=[pl.BlockSpec(memory_space=pl.ANY)],
        out_specs=pl.BlockSpec(memory_space=pl.ANY),
        scratch_shapes=[
            pltpu.SemaphoreType.DMA((n - 1,)),
            pltpu.SemaphoreType.DMA((n - 1,)),
            pltpu.SemaphoreType.DMA((1,)),
        ],
        compiler_params=pltpu.CompilerParams(collective_id=tag, has_side_effects=True),
    )(x)


def migrate(item, mig_dest, slot_count, groups, device):
    length = item.shape[0]
    lanes = 128
    piece = -(-length // (groups * lanes)) * lanes
    padded = jnp.pad(item, (0, piece * groups - length)).reshape(groups, piece // lanes, lanes)
    first = exchange(padded, 1).reshape(groups, piece)
    dest_dev = mig_dest // slot_count
    order = invert(dest_dev, groups)
    pick = (order[:, None] == jnp.arange(groups, dtype=jnp.int32)[None, :]).astype(first.dtype)
    routed = jnp.dot(pick, first, preferred_element_type=jnp.float32).astype(first.dtype)
    second = exchange(routed.reshape(groups, piece // lanes, lanes), 2)
    arrived = second.reshape(-1)[:length]
    target_local = mig_dest[order[device]] - device * slot_count
    return arrived, target_local


def local(
    tokens,
    pre_gain,
    inner_weight,
    shared_weight,
    conv_inner,
    conv_inner_bias,
    conv_shared,
    conv_shared_bias,
    step_bias,
    decay_log,
    skip_gain,
    gate_gain,
    out_weight,
    states,
    edge_inner,
    edge_shared,
    counts,
    mig_ids,
    mig_dest,
    reorder,
):
    slot_count, heads_here, head_dim, state_dim = states.shape
    inner_here = heads_here * head_dim
    lanes = state_dim
    groups = lax.axis_size("req")
    device = lax.axis_index("req")
    first_slot = device * slot_count
    stride = (slot_count + groups - 1) // groups
    all_slots = jnp.arange(slot_count * groups, dtype=jnp.int32)

    rows_in = tokens.astype(jnp.float32)
    normed = (
        rows_in * lax.rsqrt(jnp.mean(rows_in * rows_in, axis=-1, keepdims=True) + EPS) * pre_gain
    ).astype(jnp.bfloat16)
    inner_flat = inner_weight.reshape(inner_weight.shape[0], 2 * inner_here)
    piece_rows = lax.all_gather(normed, "head", axis=0, tiled=True)
    inner_rows = jnp.dot(piece_rows, inner_flat, preferred_element_type=jnp.float32).astype(
        jnp.bfloat16
    )
    shared_rows = jnp.dot(piece_rows, shared_weight, preferred_element_type=jnp.float32).astype(
        jnp.bfloat16
    )

    state_rows = heads_here * head_dim * state_dim // lanes
    inner_edge_rows = edge_inner.shape[1] * edge_inner.shape[2] // lanes
    shared_edge_rows = edge_shared.shape[1] * edge_shared.shape[2] // lanes
    packed = jnp.concatenate(
        [
            states.reshape(slot_count, state_rows, lanes),
            edge_inner.reshape(slot_count, inner_edge_rows, lanes),
            edge_shared.reshape(slot_count, shared_edge_rows, lanes),
        ],
        axis=1,
    )
    row_total = packed.shape[1]

    moving = mig_ids.shape[0] // groups
    own_id = mig_ids[device * moving]
    mig_local = own_id - first_slot
    item = jnp.concatenate(
        [
            lax.dynamic_index_in_dim(part, mig_local, 0, keepdims=False).reshape(-1)
            for part in (states, edge_inner, edge_shared)
        ]
    )
    arrived, target_local = migrate(item, mig_dest, slot_count, groups, device)
    arrived = arrived.reshape(row_total, lanes)

    send_rows, recv_rows = route_rows(reorder, first_slot, slot_count, all_slots, stride)
    buffer_rows = groups * stride
    send_idx = invert(send_rows, buffer_rows)
    send_base = packed[send_idx]
    target_row = lax.dynamic_index_in_dim(send_rows, target_local, 0, keepdims=False)
    send_buf = lax.dynamic_update_slice(send_base, arrived[None], (target_row, 0, 0))
    received = lax.all_to_all(send_buf, "req", 0, 0, tiled=True)
    moved = received[:, state_rows:][recv_rows]
    moved_inner = moved[:, :inner_edge_rows].reshape(edge_inner.shape)
    moved_shared = moved[:, inner_edge_rows:].reshape(edge_shared.shape)

    window = inner_rows.shape[0] // slot_count
    inner_rows = inner_rows.reshape(slot_count, window, 2 * inner_here)
    shared_rows = shared_rows.reshape(slot_count, window, shared_rows.shape[1])
    gate_part = inner_rows[:, :, :inner_here]
    value_part = inner_rows[:, :, inner_here:]
    fresh_shared = shared_rows[:, :, : 2 * state_dim]
    head_index = lax.axis_index("head")
    step_raw = lax.dynamic_slice_in_dim(
        shared_rows[:, :, 2 * state_dim :], head_index * heads_here, heads_here, axis=2
    )
    edge_inner_out = new_edge(moved_inner, value_part, counts)
    edge_shared_out = new_edge(moved_shared, fresh_shared, counts)
    mixed_inner = depthwise(moved_inner, value_part, conv_inner, conv_inner_bias)
    mixed_shared = depthwise(moved_shared, fresh_shared, conv_shared, conv_shared_bias)
    valid = jnp.arange(window)[None, :] < counts[:, None]
    step_size = jax.nn.softplus(step_raw.astype(jnp.float32) + step_bias)
    step_size = jnp.where(valid[:, :, None], step_size, 0.0)
    decay = -jnp.exp(decay_log)
    entries = mixed_shared[:, :, :state_dim]
    readouts = mixed_shared[:, :, state_dim:]

    factor = jnp.exp(step_size * decay)
    cum = [factor[:, 0]]
    for t in range(1, window):
        cum.append(cum[-1] * factor[:, t])
    span = {}
    for t in range(window):
        span[(t, t)] = jnp.ones_like(factor[:, 0])
        for s in range(t - 1, -1, -1):
            span[(t, s)] = span[(t, s + 1)] * factor[:, s + 1]

    def per_head(v):
        return jnp.repeat(v, head_dim, axis=-1)

    flat_inputs = mixed_inner.reshape(slot_count, window, inner_here)
    weighted = per_head(step_size) * flat_inputs
    last = window - 1
    pushed = jnp.stack([per_head(span[(last, s)]) * weighted[:, s] for s in range(window)], axis=1)
    weight = jnp.concatenate([pushed, jnp.zeros_like(pushed)], axis=1)
    carry = jnp.pad(cum[last], ((0, 0), (0, state_dim - heads_here)))[:, None, :]
    mix = jnp.concatenate(
        [readouts, entries, carry, jnp.zeros((slot_count, 2 * window - 1, state_dim), jnp.float32)],
        axis=1,
    )
    read, states_out = recurrence(received, recv_rows, mix, weight, state_rows, heads_here)
    states_out = states_out.reshape(states.shape)
    overlap = jnp.einsum("rtn,rsn->rts", readouts, entries, precision=HIGH)
    skip_wide = jnp.repeat(skip_gain, head_dim)
    produced = []
    for t in range(window):
        acc = per_head(cum[t]) * read[:, t]
        for s in range(t + 1):
            acc = acc + per_head(span[(t, s)] * overlap[:, t, s, None]) * weighted[:, s]
        produced.append(acc + skip_wide * flat_inputs[:, t])
    outputs = jnp.stack(produced, axis=1)

    gated = outputs * jax.nn.silu(gate_part.astype(jnp.float32))
    square_part = jnp.sum(gated * gated, axis=-1).reshape(slot_count * window, 1)
    pre_scaled = (
        jnp.where(valid[:, :, None], gated * gate_gain, 0.0)
        .astype(jnp.bfloat16)
        .reshape(slot_count * window, inner_here)
    )
    partial = jnp.dot(pre_scaled, out_weight, preferred_element_type=jnp.float32)
    square_hi = square_part.astype(jnp.bfloat16)
    square_lo = (square_part - square_hi.astype(jnp.float32)).astype(jnp.bfloat16)
    extra = jnp.pad(
        jnp.concatenate([square_hi, square_lo], axis=1), ((0, 0), (0, 126))
    )
    combined = jnp.concatenate([partial.astype(jnp.bfloat16), extra], axis=1)
    reduced = scatter_sum(combined, lax.axis_size("head"))
    full_inner = inner_here * lax.axis_size("head")
    width = partial.shape[1]
    square_sum = reduced[:, width : width + 1] + reduced[:, width + 1 : width + 2]
    scale = lax.rsqrt(square_sum / full_inner + EPS)
    hidden_out = (rows_in + reduced[:, :width] * scale).astype(jnp.bfloat16)
    return (hidden_out, states_out, edge_inner_out, edge_shared_out)


def solution(mesh):
    placed = (
        P(("req", "head"), None),
        P(),
        P(None, None, "head"),
        P(),
        P(None, "head"),
        P("head"),
        P(),
        P(),
        P("head"),
        P("head"),
        P("head"),
        P("head"),
        P("head", None),
        P("req", "head", None, None),
        P("req", None, "head"),
        P("req", None, None),
        P("req"),
        P(),
        P(),
        P(),
    )
    return jax.shard_map(
        local,
        mesh=mesh,
        in_specs=placed,
        out_specs=(
            P(("req", "head"), None),
            P("req", "head", None, None),
            P("req", None, "head"),
            P("req", None, None),
        ),
        check_vma=False,
    )
```

```python
import functools

import jax
import jax.numpy as jnp
from jax import lax
from jax.sharding import PartitionSpec as P
from jax.experimental import pallas as pl
from jax.experimental.pallas import tpu as pltpu

EPS = 1e-05
HIGH = lax.Precision.HIGHEST


def depthwise(edge, fresh, weight, offset_bias):
    sequence = jnp.concatenate([edge, fresh], axis=1).astype(jnp.float32)
    window = fresh.shape[1]
    summed = sequence[:, 0:window] * weight[0]
    for offset in range(1, weight.shape[0]):
        summed = summed + sequence[:, offset : offset + window] * weight[offset]
    return jax.nn.silu(summed + offset_bias)


def new_edge(edge, fresh, counts):
    sequence = jnp.concatenate([edge, fresh], axis=1)
    keep_rows = edge.shape[1]
    result = edge
    for length in range(1, fresh.shape[1] + 1):
        result = jnp.where(
            (counts == length)[:, None, None], sequence[:, length : length + keep_rows], result
        )
    return result


def rank_rows(partner, position, capacity):
    matching = partner[:, None] == partner[None, :]
    earlier = position[None, :] < position[:, None]
    ranking = jnp.sum(jnp.logical_and(matching, earlier), axis=1)
    return partner * capacity + ranking


def invert(values, size):
    hits = values[None, :] == jnp.arange(size, dtype=jnp.int32)[:, None]
    return jnp.sum(jnp.where(hits, jnp.arange(values.shape[0], dtype=jnp.int32)[None, :], 0), axis=1)


def route_rows(anchor, first_slot, slot_count, all_slots, capacity):
    mine = first_slot + jnp.arange(slot_count, dtype=jnp.int32)
    hits = anchor[None, :] == mine[:, None]
    targets = jnp.sum(jnp.where(hits, all_slots[None, :], 0), axis=1)
    send_rows = rank_rows(targets // slot_count, targets % slot_count, capacity)
    sources = lax.dynamic_slice_in_dim(anchor, first_slot, slot_count)
    recv_rows = rank_rows(sources // slot_count, jnp.arange(slot_count, dtype=jnp.int32), capacity)
    return (send_rows, recv_rows)


def recurrence_kernel(rows_ref, *refs, group, window, heads):
    held_refs = refs[:group]
    mix_ref, weight_ref, read_ref, out_ref = refs[group:]
    nt = (((1,), (1,)), ((), ()))
    tn = (((0,), (0,)), ((), ()))
    for q in range(group):
        held_low = held_refs[q][0]
        mix = mix_ref[q]
        read = None
        rest = mix[: 2 * window]
        for _ in range(3):
            part = rest.astype(jnp.bfloat16)
            rest = rest - part.astype(jnp.float32)
            term = lax.dot_general(part, held_low, nt, preferred_element_type=jnp.float32)
            read = term if read is None else read + term
        read_ref[q] = read
        weight = weight_ref[q]
        entry = mix[window : 3 * window]
        w_hi = weight.astype(jnp.bfloat16)
        w_lo = (weight - w_hi.astype(jnp.float32)).astype(jnp.bfloat16)
        e_hi = entry.astype(jnp.bfloat16)
        e_lo = (entry - e_hi.astype(jnp.float32)).astype(jnp.bfloat16)
        pushed = (
            lax.dot_general(w_hi, e_hi, tn, preferred_element_type=jnp.float32)
            + lax.dot_general(w_hi, e_lo, tn, preferred_element_type=jnp.float32)
            + lax.dot_general(w_lo, e_hi, tn, preferred_element_type=jnp.float32)
        )
        held = held_low.astype(jnp.float32)
        rows = held.shape[0] // heads
        carry = mix[2 * window : 2 * window + 1]
        for h in range(heads):
            part = slice(h * rows, (h + 1) * rows)
            out_ref[q, part] = (carry[:, h : h + 1] * held[part] + pushed[part]).astype(
                out_ref.dtype
            )


def recurrence(received, rows, mix, weight, state_rows, heads, group=8):
    slot_count, _, lanes = received.shape
    window = mix.shape[1] // 4
    held_specs = [
        pl.BlockSpec((1, state_rows, lanes), lambda i, r, q=q: (r[i * group + q], 0, 0))
        for q in range(group)
    ]
    grid_spec = pltpu.PrefetchScalarGridSpec(
        num_scalar_prefetch=1,
        grid=(slot_count // group,),
        in_specs=held_specs
        + [
            pl.BlockSpec((group, 4 * window, lanes), lambda i, r: (i, 0, 0)),
            pl.BlockSpec((group, 2 * window, state_rows), lambda i, r: (i, 0, 0)),
        ],
        out_specs=[
            pl.BlockSpec((group, 2 * window, state_rows), lambda i, r: (i, 0, 0)),
            pl.BlockSpec((group, state_rows, lanes), lambda i, r: (i, 0, 0)),
        ],
    )
    return pl.pallas_call(
        functools.partial(recurrence_kernel, group=group, window=window, heads=heads),
        grid_spec=grid_spec,
        out_shape=[
            jax.ShapeDtypeStruct((slot_count, 2 * window, state_rows), jnp.float32),
            jax.ShapeDtypeStruct((slot_count, state_rows, lanes), jnp.bfloat16),
        ],
    )(rows, *([received] * group), mix, weight)

MESH = pl.DeviceIdType.MESH


def scatter_sum_kernel(x_ref, out_ref, slots, send_sem, recv_sem, *, n, rows):
    me = lax.axis_index("head")
    group = lax.axis_index("req")
    barrier = pltpu.get_barrier_semaphore()
    for k in range(1, n):
        pl.semaphore_signal(
            barrier, inc=1, device_id=(group, lax.rem(me + k, n)), device_id_type=MESH
        )
    pl.semaphore_wait(barrier, n - 1)
    copies = []
    for k in range(1, n):
        peer = lax.rem(me + k, n)
        start = pl.multiple_of(peer * rows, rows)
        copy = pltpu.make_async_remote_copy(
            src_ref=x_ref.at[pl.ds(start, rows)],
            dst_ref=slots.at[k - 1],
            send_sem=send_sem.at[k - 1],
            recv_sem=recv_sem.at[k - 1],
            device_id=(group, peer),
            device_id_type=MESH,
        )
        copy.start()
        copies.append(copy)
    own = pl.multiple_of(me * rows, rows)
    total = x_ref[pl.ds(own, rows)].astype(jnp.float32)
    for k, copy in enumerate(copies):
        copy.wait()
        total = total + slots[k].astype(jnp.float32)
    out_ref[...] = total


def scatter_sum(x, n):
    rows = x.shape[0] // n
    return pl.pallas_call(
        functools.partial(scatter_sum_kernel, n=n, rows=rows),
        out_shape=jax.ShapeDtypeStruct((rows, x.shape[1]), jnp.float32),
        in_specs=[pl.BlockSpec(memory_space=pltpu.VMEM)],
        out_specs=pl.BlockSpec(memory_space=pltpu.VMEM),
        scratch_shapes=[
            pltpu.VMEM((n - 1, rows, x.shape[1]), x.dtype),
            pltpu.SemaphoreType.DMA((n - 1,)),
            pltpu.SemaphoreType.DMA((n - 1,)),
        ],
        compiler_params=pltpu.CompilerParams(collective_id=0, has_side_effects=True),
    )(x)


def exchange_kernel(x_ref, out_ref, send_sem, recv_sem, local_sem, *, n):
    me = lax.axis_index("req")
    head = lax.axis_index("head")
    barrier = pltpu.get_barrier_semaphore()
    for k in range(1, n):
        pl.semaphore_signal(
            barrier, inc=1, device_id=(lax.rem(me + k, n), head), device_id_type=MESH
        )
    pl.semaphore_wait(barrier, n - 1)
    own = pltpu.make_async_copy(x_ref.at[me], out_ref.at[me], local_sem.at[0])
    own.start()
    copies = []
    for k in range(1, n):
        peer = lax.rem(me + k, n)
        copy = pltpu.make_async_remote_copy(
            src_ref=x_ref.at[peer],
            dst_ref=out_ref.at[me],
            send_sem=send_sem.at[k - 1],
            recv_sem=recv_sem.at[k - 1],
            device_id=(peer, head),
            device_id_type=MESH,
        )
        copy.start()
        copies.append(copy)
    own.wait()
    for copy in copies:
        copy.wait()


def exchange(x, tag):
    n = x.shape[0]
    return pl.pallas_call(
        functools.partial(exchange_kernel, n=n),
        out_shape=jax.ShapeDtypeStruct(x.shape, x.dtype),
        in_specs=[pl.BlockSpec(memory_space=pl.ANY)],
        out_specs=pl.BlockSpec(memory_space=pl.ANY),
        scratch_shapes=[
            pltpu.SemaphoreType.DMA((n - 1,)),
            pltpu.SemaphoreType.DMA((n - 1,)),
            pltpu.SemaphoreType.DMA((1,)),
        ],
        compiler_params=pltpu.CompilerParams(collective_id=tag, has_side_effects=True),
    )(x)


def migrate(item, mig_dest, slot_count, groups, device):
    length = item.shape[0]
    lanes = 128
    piece = -(-length // (groups * lanes)) * lanes
    padded = jnp.pad(item, (0, piece * groups - length)).reshape(groups, piece // lanes, lanes)
    first = exchange(padded, 1).reshape(groups, piece)
    dest_dev = mig_dest // slot_count
    order = invert(dest_dev, groups)
    pick = (order[:, None] == jnp.arange(groups, dtype=jnp.int32)[None, :]).astype(first.dtype)
    routed = jnp.dot(pick, first, preferred_element_type=jnp.float32).astype(first.dtype)
    second = exchange(routed.reshape(groups, piece // lanes, lanes), 2)
    arrived = second.reshape(-1)[:length]
    target_local = mig_dest[order[device]] - device * slot_count
    return arrived, target_local


def local(
    tokens,
    pre_gain,
    inner_weight,
    shared_weight,
    conv_inner,
    conv_inner_bias,
    conv_shared,
    conv_shared_bias,
    step_bias,
    decay_log,
    skip_gain,
    gate_gain,
    out_weight,
    states,
    edge_inner,
    edge_shared,
    counts,
    mig_ids,
    mig_dest,
    reorder,
):
    slot_count, heads_here, head_dim, state_dim = states.shape
    inner_here = heads_here * head_dim
    lanes = state_dim
    groups = lax.axis_size("req")
    device = lax.axis_index("req")
    first_slot = device * slot_count
    stride = (slot_count + groups - 1) // groups
    all_slots = jnp.arange(slot_count * groups, dtype=jnp.int32)

    rows_in = tokens.astype(jnp.float32)
    normed = (
        rows_in * lax.rsqrt(jnp.mean(rows_in * rows_in, axis=-1, keepdims=True) + EPS) * pre_gain
    ).astype(jnp.bfloat16)
    inner_flat = inner_weight.reshape(inner_weight.shape[0], 2 * inner_here)
    piece_rows = lax.all_gather(normed, "head", axis=0, tiled=True)
    inner_rows = jnp.dot(piece_rows, inner_flat, preferred_element_type=jnp.float32).astype(
        jnp.bfloat16
    )
    shared_rows = jnp.dot(piece_rows, shared_weight, preferred_element_type=jnp.float32).astype(
        jnp.bfloat16
    )

    state_rows = heads_here * head_dim * state_dim // lanes
    inner_edge_rows = edge_inner.shape[1] * edge_inner.shape[2] // lanes
    shared_edge_rows = edge_shared.shape[1] * edge_shared.shape[2] // lanes
    packed = jnp.concatenate(
        [
            states.reshape(slot_count, state_rows, lanes),
            edge_inner.reshape(slot_count, inner_edge_rows, lanes),
            edge_shared.reshape(slot_count, shared_edge_rows, lanes),
        ],
        axis=1,
    )
    row_total = packed.shape[1]

    moving = mig_ids.shape[0] // groups
    own_id = mig_ids[device * moving]
    mig_local = own_id - first_slot
    item = jnp.concatenate(
        [
            lax.dynamic_index_in_dim(part, mig_local, 0, keepdims=False).reshape(-1)
            for part in (states, edge_inner, edge_shared)
        ]
    )
    arrived, target_local = migrate(item, mig_dest, slot_count, groups, device)
    arrived = arrived.reshape(row_total, lanes)

    send_rows, recv_rows = route_rows(reorder, first_slot, slot_count, all_slots, stride)
    buffer_rows = groups * stride
    send_idx = invert(send_rows, buffer_rows)
    send_base = packed[send_idx]
    target_row = lax.dynamic_index_in_dim(send_rows, target_local, 0, keepdims=False)
    send_buf = lax.dynamic_update_slice(send_base, arrived[None], (target_row, 0, 0))
    received = lax.all_to_all(send_buf, "req", 0, 0, tiled=True)
    moved = received[:, state_rows:][recv_rows]
    moved_inner = moved[:, :inner_edge_rows].reshape(edge_inner.shape)
    moved_shared = moved[:, inner_edge_rows:].reshape(edge_shared.shape)

    window = inner_rows.shape[0] // slot_count
    inner_rows = inner_rows.reshape(slot_count, window, 2 * inner_here)
    shared_rows = shared_rows.reshape(slot_count, window, shared_rows.shape[1])
    gate_part = inner_rows[:, :, :inner_here]
    value_part = inner_rows[:, :, inner_here:]
    fresh_shared = shared_rows[:, :, : 2 * state_dim]
    head_index = lax.axis_index("head")
    step_raw = lax.dynamic_slice_in_dim(
        shared_rows[:, :, 2 * state_dim :], head_index * heads_here, heads_here, axis=2
    )
    edge_inner_out = new_edge(moved_inner, value_part, counts)
    edge_shared_out = new_edge(moved_shared, fresh_shared, counts)
    mixed_inner = depthwise(moved_inner, value_part, conv_inner, conv_inner_bias)
    mixed_shared = depthwise(moved_shared, fresh_shared, conv_shared, conv_shared_bias)
    valid = jnp.arange(window)[None, :] < counts[:, None]
    step_size = jax.nn.softplus(step_raw.astype(jnp.float32) + step_bias)
    step_size = jnp.where(valid[:, :, None], step_size, 0.0)
    decay = -jnp.exp(decay_log)
    entries = mixed_shared[:, :, :state_dim]
    readouts = mixed_shared[:, :, state_dim:]

    factor = jnp.exp(step_size * decay)
    cum = [factor[:, 0]]
    for t in range(1, window):
        cum.append(cum[-1] * factor[:, t])
    span = {}
    for t in range(window):
        span[(t, t)] = jnp.ones_like(factor[:, 0])
        for s in range(t - 1, -1, -1):
            span[(t, s)] = span[(t, s + 1)] * factor[:, s + 1]

    def per_head(v):
        return jnp.repeat(v, head_dim, axis=-1)

    flat_inputs = mixed_inner.reshape(slot_count, window, inner_here)
    weighted = per_head(step_size) * flat_inputs
    last = window - 1
    pushed = jnp.stack([per_head(span[(last, s)]) * weighted[:, s] for s in range(window)], axis=1)
    weight = jnp.concatenate([pushed, jnp.zeros_like(pushed)], axis=1)
    carry = jnp.pad(cum[last], ((0, 0), (0, state_dim - heads_here)))[:, None, :]
    mix = jnp.concatenate(
        [readouts, entries, carry, jnp.zeros((slot_count, 2 * window - 1, state_dim), jnp.float32)],
        axis=1,
    )
    read, states_out = recurrence(received, recv_rows, mix, weight, state_rows, heads_here)
    states_out = states_out.reshape(states.shape)
    overlap = jnp.einsum("rtn,rsn->rts", readouts, entries, precision=HIGH)
    skip_wide = jnp.repeat(skip_gain, head_dim)
    produced = []
    for t in range(window):
        acc = per_head(cum[t]) * read[:, t]
        for s in range(t + 1):
            acc = acc + per_head(span[(t, s)] * overlap[:, t, s, None]) * weighted[:, s]
        produced.append(acc + skip_wide * flat_inputs[:, t])
    outputs = jnp.stack(produced, axis=1)

    gated = outputs * jax.nn.silu(gate_part.astype(jnp.float32))
    square_part = jnp.sum(gated * gated, axis=-1).reshape(slot_count * window, 1)
    pre_scaled = (
        jnp.where(valid[:, :, None], gated * gate_gain, 0.0)
        .astype(jnp.bfloat16)
        .reshape(slot_count * window, inner_here)
    )
    partial = jnp.dot(pre_scaled, out_weight, preferred_element_type=jnp.float32)
    square_hi = square_part.astype(jnp.bfloat16)
    square_lo = (square_part - square_hi.astype(jnp.float32)).astype(jnp.bfloat16)
    extra = jnp.pad(
        jnp.concatenate([square_hi, square_lo], axis=1), ((0, 0), (0, 126))
    )
    combined = jnp.concatenate([partial.astype(jnp.bfloat16), extra], axis=1)
    reduced = scatter_sum(combined, lax.axis_size("head"))
    full_inner = inner_here * lax.axis_size("head")
    width = partial.shape[1]
    square_sum = reduced[:, width : width + 1] + reduced[:, width + 1 : width + 2]
    scale = lax.rsqrt(square_sum / full_inner + EPS)
    hidden_out = (rows_in + reduced[:, :width] * scale).astype(jnp.bfloat16)
    return (hidden_out, states_out, edge_inner_out, edge_shared_out)


def solution(mesh):
    placed = (
        P(("req", "head"), None),
        P(),
        P(None, None, "head"),
        P(),
        P(None, "head"),
        P("head"),
        P(),
        P(),
        P("head"),
        P("head"),
        P("head"),
        P("head"),
        P("head", None),
        P("req", "head", None, None),
        P("req", None, "head"),
        P("req", None, None),
        P("req"),
        P(),
        P(),
        P(),
    )
    return jax.shard_map(
        local,
        mesh=mesh,
        in_specs=placed,
        out_specs=(
            P(("req", "head"), None),
            P("req", "head", None, None),
            P("req", None, "head"),
            P("req", None, None),
        ),
        check_vma=False,
    )
```

```python
import functools

import jax
import jax.numpy as jnp
from jax import lax
from jax.sharding import PartitionSpec as P
from jax.experimental import pallas as pl
from jax.experimental.pallas import tpu as pltpu

EPS = 1e-05
HIGH = lax.Precision.HIGHEST


def depthwise(edge, fresh, weight, offset_bias):
    sequence = jnp.concatenate([edge, fresh], axis=1).astype(jnp.float32)
    window = fresh.shape[1]
    summed = sequence[:, 0:window] * weight[0]
    for offset in range(1, weight.shape[0]):
        summed = summed + sequence[:, offset : offset + window] * weight[offset]
    return jax.nn.silu(summed + offset_bias)


def new_edge(edge, fresh, counts):
    sequence = jnp.concatenate([edge, fresh], axis=1)
    keep_rows = edge.shape[1]
    result = edge
    for length in range(1, fresh.shape[1] + 1):
        result = jnp.where(
            (counts == length)[:, None, None], sequence[:, length : length + keep_rows], result
        )
    return result


def rank_rows(partner, position, capacity):
    matching = partner[:, None] == partner[None, :]
    earlier = position[None, :] < position[:, None]
    ranking = jnp.sum(jnp.logical_and(matching, earlier), axis=1)
    return partner * capacity + ranking


def invert(values, size):
    hits = values[None, :] == jnp.arange(size, dtype=jnp.int32)[:, None]
    return jnp.sum(jnp.where(hits, jnp.arange(values.shape[0], dtype=jnp.int32)[None, :], 0), axis=1)


def route_rows(anchor, first_slot, slot_count, all_slots, capacity):
    mine = first_slot + jnp.arange(slot_count, dtype=jnp.int32)
    hits = anchor[None, :] == mine[:, None]
    targets = jnp.sum(jnp.where(hits, all_slots[None, :], 0), axis=1)
    send_rows = rank_rows(targets // slot_count, targets % slot_count, capacity)
    sources = lax.dynamic_slice_in_dim(anchor, first_slot, slot_count)
    recv_rows = rank_rows(sources // slot_count, jnp.arange(slot_count, dtype=jnp.int32), capacity)
    return (send_rows, recv_rows)


def recurrence_kernel(rows_ref, *refs, group, window, heads):
    held_refs = refs[:group]
    mix_ref, weight_ref, read_ref, out_ref = refs[group:]
    nt = (((1,), (1,)), ((), ()))
    tn = (((0,), (0,)), ((), ()))
    for q in range(group):
        held_low = held_refs[q][0]
        mix = mix_ref[q]
        read = None
        rest = mix[: 2 * window]
        for _ in range(3):
            part = rest.astype(jnp.bfloat16)
            rest = rest - part.astype(jnp.float32)
            term = lax.dot_general(part, held_low, nt, preferred_element_type=jnp.float32)
            read = term if read is None else read + term
        read_ref[q] = read
        weight = weight_ref[q]
        entry = mix[window : 3 * window]
        w_hi = weight.astype(jnp.bfloat16)
        w_lo = (weight - w_hi.astype(jnp.float32)).astype(jnp.bfloat16)
        e_hi = entry.astype(jnp.bfloat16)
        e_lo = (entry - e_hi.astype(jnp.float32)).astype(jnp.bfloat16)
        pushed = (
            lax.dot_general(w_hi, e_hi, tn, preferred_element_type=jnp.float32)
            + lax.dot_general(w_hi, e_lo, tn, preferred_element_type=jnp.float32)
            + lax.dot_general(w_lo, e_hi, tn, preferred_element_type=jnp.float32)
        )
        held = held_low.astype(jnp.float32)
        rows = held.shape[0] // heads
        carry = mix[2 * window : 2 * window + 1]
        for h in range(heads):
            part = slice(h * rows, (h + 1) * rows)
            out_ref[q, part] = (carry[:, h : h + 1] * held[part] + pushed[part]).astype(
                out_ref.dtype
            )


def recurrence(received, rows, mix, weight, state_rows, heads, group=8):
    slot_count, _, lanes = received.shape
    window = mix.shape[1] // 4
    held_specs = [
        pl.BlockSpec((1, state_rows, lanes), lambda i, r, q=q: (r[i * group + q], 0, 0))
        for q in range(group)
    ]
    grid_spec = pltpu.PrefetchScalarGridSpec(
        num_scalar_prefetch=1,
        grid=(slot_count // group,),
        in_specs=held_specs
        + [
            pl.BlockSpec((group, 4 * window, lanes), lambda i, r: (i, 0, 0)),
            pl.BlockSpec((group, 2 * window, state_rows), lambda i, r: (i, 0, 0)),
        ],
        out_specs=[
            pl.BlockSpec((group, 2 * window, state_rows), lambda i, r: (i, 0, 0)),
            pl.BlockSpec((group, state_rows, lanes), lambda i, r: (i, 0, 0)),
        ],
    )
    return pl.pallas_call(
        functools.partial(recurrence_kernel, group=group, window=window, heads=heads),
        grid_spec=grid_spec,
        out_shape=[
            jax.ShapeDtypeStruct((slot_count, 2 * window, state_rows), jnp.float32),
            jax.ShapeDtypeStruct((slot_count, state_rows, lanes), jnp.bfloat16),
        ],
    )(rows, *([received] * group), mix, weight)

MESH = pl.DeviceIdType.MESH


def scatter_sum_kernel(x_ref, out_ref, slots, send_sem, recv_sem, *, n, rows):
    me = lax.axis_index("head")
    group = lax.axis_index("req")
    barrier = pltpu.get_barrier_semaphore()
    for k in range(1, n):
        pl.semaphore_signal(
            barrier, inc=1, device_id=(group, lax.rem(me + k, n)), device_id_type=MESH
        )
    pl.semaphore_wait(barrier, n - 1)
    copies = []
    for k in range(1, n):
        peer = lax.rem(me + k, n)
        start = pl.multiple_of(peer * rows, rows)
        copy = pltpu.make_async_remote_copy(
            src_ref=x_ref.at[pl.ds(start, rows)],
            dst_ref=slots.at[k - 1],
            send_sem=send_sem.at[k - 1],
            recv_sem=recv_sem.at[k - 1],
            device_id=(group, peer),
            device_id_type=MESH,
        )
        copy.start()
        copies.append(copy)
    own = pl.multiple_of(me * rows, rows)
    total = x_ref[pl.ds(own, rows)].astype(jnp.float32)
    for k, copy in enumerate(copies):
        copy.wait()
        total = total + slots[k].astype(jnp.float32)
    out_ref[...] = total


def scatter_sum(x, n):
    rows = x.shape[0] // n
    return pl.pallas_call(
        functools.partial(scatter_sum_kernel, n=n, rows=rows),
        out_shape=jax.ShapeDtypeStruct((rows, x.shape[1]), jnp.float32),
        in_specs=[pl.BlockSpec(memory_space=pltpu.VMEM)],
        out_specs=pl.BlockSpec(memory_space=pltpu.VMEM),
        scratch_shapes=[
            pltpu.VMEM((n - 1, rows, x.shape[1]), x.dtype),
            pltpu.SemaphoreType.DMA((n - 1,)),
            pltpu.SemaphoreType.DMA((n - 1,)),
        ],
        compiler_params=pltpu.CompilerParams(collective_id=0, has_side_effects=True),
    )(x)


def exchange_kernel(x_ref, out_ref, send_sem, recv_sem, local_sem, *, n):
    me = lax.axis_index("req")
    head = lax.axis_index("head")
    barrier = pltpu.get_barrier_semaphore()
    for k in range(1, n):
        pl.semaphore_signal(
            barrier, inc=1, device_id=(lax.rem(me + k, n), head), device_id_type=MESH
        )
    pl.semaphore_wait(barrier, n - 1)
    own = pltpu.make_async_copy(x_ref.at[me], out_ref.at[me], local_sem.at[0])
    own.start()
    copies = []
    for k in range(1, n):
        peer = lax.rem(me + k, n)
        copy = pltpu.make_async_remote_copy(
            src_ref=x_ref.at[peer],
            dst_ref=out_ref.at[me],
            send_sem=send_sem.at[k - 1],
            recv_sem=recv_sem.at[k - 1],
            device_id=(peer, head),
            device_id_type=MESH,
        )
        copy.start()
        copies.append(copy)
    own.wait()
    for copy in copies:
        copy.wait()


def exchange(x, tag):
    n = x.shape[0]
    return pl.pallas_call(
        functools.partial(exchange_kernel, n=n),
        out_shape=jax.ShapeDtypeStruct(x.shape, x.dtype),
        in_specs=[pl.BlockSpec(memory_space=pl.ANY)],
        out_specs=pl.BlockSpec(memory_space=pl.ANY),
        scratch_shapes=[
            pltpu.SemaphoreType.DMA((n - 1,)),
            pltpu.SemaphoreType.DMA((n - 1,)),
            pltpu.SemaphoreType.DMA((1,)),
        ],
        compiler_params=pltpu.CompilerParams(collective_id=tag, has_side_effects=True),
    )(x)


def migrate(item, mig_dest, slot_count, groups, device):
    length = item.shape[0]
    lanes = 128
    piece = -(-length // (groups * lanes)) * lanes
    padded = jnp.pad(item, (0, piece * groups - length)).reshape(groups, piece // lanes, lanes)
    first = exchange(padded, 1).reshape(groups, piece)
    dest_dev = mig_dest // slot_count
    order = invert(dest_dev, groups)
    pick = (order[:, None] == jnp.arange(groups, dtype=jnp.int32)[None, :]).astype(first.dtype)
    routed = jnp.dot(pick, first, preferred_element_type=jnp.float32).astype(first.dtype)
    second = exchange(routed.reshape(groups, piece // lanes, lanes), 2)
    arrived = second.reshape(-1)[:length]
    target_local = jnp.sum(jnp.where(dest_dev == device, mig_dest, 0)) - device * slot_count
    return arrived, target_local


def local(
    tokens,
    pre_gain,
    inner_weight,
    shared_weight,
    conv_inner,
    conv_inner_bias,
    conv_shared,
    conv_shared_bias,
    step_bias,
    decay_log,
    skip_gain,
    gate_gain,
    out_weight,
    states,
    edge_inner,
    edge_shared,
    counts,
    mig_ids,
    mig_dest,
    reorder,
):
    slot_count, heads_here, head_dim, state_dim = states.shape
    inner_here = heads_here * head_dim
    lanes = state_dim
    groups = lax.axis_size("req")
    device = lax.axis_index("req")
    first_slot = device * slot_count
    stride = (slot_count + groups - 1) // groups
    all_slots = jnp.arange(slot_count * groups, dtype=jnp.int32)

    rows_in = tokens.astype(jnp.float32)
    normed = (
        rows_in * lax.rsqrt(jnp.mean(rows_in * rows_in, axis=-1, keepdims=True) + EPS) * pre_gain
    ).astype(jnp.bfloat16)
    inner_flat = inner_weight.reshape(inner_weight.shape[0], 2 * inner_here)
    piece_rows = lax.all_gather(normed, "head", axis=0, tiled=True)
    inner_rows = jnp.dot(piece_rows, inner_flat, preferred_element_type=jnp.float32).astype(
        jnp.bfloat16
    )
    shared_rows = jnp.dot(piece_rows, shared_weight, preferred_element_type=jnp.float32).astype(
        jnp.bfloat16
    )

    state_rows = heads_here * head_dim * state_dim // lanes
    inner_edge_rows = edge_inner.shape[1] * edge_inner.shape[2] // lanes
    shared_edge_rows = edge_shared.shape[1] * edge_shared.shape[2] // lanes
    packed = jnp.concatenate(
        [
            states.reshape(slot_count, state_rows, lanes),
            edge_inner.reshape(slot_count, inner_edge_rows, lanes),
            edge_shared.reshape(slot_count, shared_edge_rows, lanes),
        ],
        axis=1,
    )
    row_total = packed.shape[1]

    moving = mig_ids.shape[0] // groups
    own_id = jnp.sum(jnp.where(jnp.arange(mig_ids.shape[0]) == device * moving, mig_ids, 0))
    mig_local = own_id - first_slot
    item = jnp.concatenate(
        [
            lax.dynamic_index_in_dim(part, mig_local, 0, keepdims=False).reshape(-1)
            for part in (states, edge_inner, edge_shared)
        ]
    )
    arrived, target_local = migrate(item, mig_dest, slot_count, groups, device)
    arrived = arrived.reshape(row_total, lanes)

    send_rows, recv_rows = route_rows(reorder, first_slot, slot_count, all_slots, stride)
    buffer_rows = groups * stride
    send_idx = invert(send_rows, buffer_rows)
    send_base = packed[send_idx]
    target_row = jnp.sum(jnp.where(jnp.arange(slot_count) == target_local, send_rows, 0))
    send_buf = lax.dynamic_update_slice(send_base, arrived[None], (target_row, 0, 0))
    received = lax.all_to_all(send_buf, "req", 0, 0, tiled=True)
    moved = received[:, state_rows:][recv_rows]
    moved_inner = moved[:, :inner_edge_rows].reshape(edge_inner.shape)
    moved_shared = moved[:, inner_edge_rows:].reshape(edge_shared.shape)

    window = inner_rows.shape[0] // slot_count
    inner_rows = inner_rows.reshape(slot_count, window, 2 * inner_here)
    shared_rows = shared_rows.reshape(slot_count, window, shared_rows.shape[1])
    gate_part = inner_rows[:, :, :inner_here]
    value_part = inner_rows[:, :, inner_here:]
    fresh_shared = shared_rows[:, :, : 2 * state_dim]
    head_index = lax.axis_index("head")
    step_raw = lax.dynamic_slice_in_dim(
        shared_rows[:, :, 2 * state_dim :], head_index * heads_here, heads_here, axis=2
    )
    edge_inner_out = new_edge(moved_inner, value_part, counts)
    edge_shared_out = new_edge(moved_shared, fresh_shared, counts)
    mixed_inner = depthwise(moved_inner, value_part, conv_inner, conv_inner_bias)
    mixed_shared = depthwise(moved_shared, fresh_shared, conv_shared, conv_shared_bias)
    valid = jnp.arange(window)[None, :] < counts[:, None]
    step_size = jax.nn.softplus(step_raw.astype(jnp.float32) + step_bias)
    step_size = jnp.where(valid[:, :, None], step_size, 0.0)
    decay = -jnp.exp(decay_log)
    entries = mixed_shared[:, :, :state_dim]
    readouts = mixed_shared[:, :, state_dim:]

    factor = jnp.exp(step_size * decay)
    cum = [factor[:, 0]]
    for t in range(1, window):
        cum.append(cum[-1] * factor[:, t])
    span = {}
    for t in range(window):
        span[(t, t)] = jnp.ones_like(factor[:, 0])
        for s in range(t - 1, -1, -1):
            span[(t, s)] = span[(t, s + 1)] * factor[:, s + 1]

    def per_head(v):
        return jnp.repeat(v, head_dim, axis=-1)

    flat_inputs = mixed_inner.reshape(slot_count, window, inner_here)
    weighted = per_head(step_size) * flat_inputs
    last = window - 1
    pushed = jnp.stack([per_head(span[(last, s)]) * weighted[:, s] for s in range(window)], axis=1)
    weight = jnp.concatenate([pushed, jnp.zeros_like(pushed)], axis=1)
    carry = jnp.pad(cum[last], ((0, 0), (0, state_dim - heads_here)))[:, None, :]
    mix = jnp.concatenate(
        [readouts, entries, carry, jnp.zeros((slot_count, 2 * window - 1, state_dim), jnp.float32)],
        axis=1,
    )
    read, states_out = recurrence(received, recv_rows, mix, weight, state_rows, heads_here)
    states_out = states_out.reshape(states.shape)
    overlap = jnp.einsum("rtn,rsn->rts", readouts, entries, precision=HIGH)
    skip_wide = jnp.repeat(skip_gain, head_dim)
    produced = []
    for t in range(window):
        acc = per_head(cum[t]) * read[:, t]
        for s in range(t + 1):
            acc = acc + per_head(span[(t, s)] * overlap[:, t, s, None]) * weighted[:, s]
        produced.append(acc + skip_wide * flat_inputs[:, t])
    outputs = jnp.stack(produced, axis=1)

    gated = outputs * jax.nn.silu(gate_part.astype(jnp.float32))
    square_part = jnp.sum(gated * gated, axis=-1).reshape(slot_count * window, 1)
    pre_scaled = (
        jnp.where(valid[:, :, None], gated * gate_gain, 0.0)
        .astype(jnp.bfloat16)
        .reshape(slot_count * window, inner_here)
    )
    partial = jnp.dot(pre_scaled, out_weight, preferred_element_type=jnp.float32)
    square_hi = square_part.astype(jnp.bfloat16)
    square_lo = (square_part - square_hi.astype(jnp.float32)).astype(jnp.bfloat16)
    extra = jnp.pad(
        jnp.concatenate([square_hi, square_lo], axis=1), ((0, 0), (0, 126))
    )
    combined = jnp.concatenate([partial.astype(jnp.bfloat16), extra], axis=1)
    reduced = scatter_sum(combined, lax.axis_size("head"))
    full_inner = inner_here * lax.axis_size("head")
    width = partial.shape[1]
    square_sum = reduced[:, width : width + 1] + reduced[:, width + 1 : width + 2]
    scale = lax.rsqrt(square_sum / full_inner + EPS)
    hidden_out = (rows_in + reduced[:, :width] * scale).astype(jnp.bfloat16)
    return (hidden_out, states_out, edge_inner_out, edge_shared_out)


def solution(mesh):
    placed = (
        P(("req", "head"), None),
        P(),
        P(None, None, "head"),
        P(),
        P(None, "head"),
        P("head"),
        P(),
        P(),
        P("head"),
        P("head"),
        P("head"),
        P("head"),
        P("head", None),
        P("req", "head", None, None),
        P("req", None, "head"),
        P("req", None, None),
        P("req"),
        P(),
        P(),
        P(),
    )
    return jax.shard_map(
        local,
        mesh=mesh,
        in_specs=placed,
        out_specs=(
            P(("req", "head"), None),
            P("req", "head", None, None),
            P("req", None, "head"),
            P("req", None, None),
        ),
        check_vma=False,
    )
```

```python
import functools

import jax
import jax.numpy as jnp
from jax import lax
from jax.sharding import PartitionSpec as P
from jax.experimental import pallas as pl
from jax.experimental.pallas import tpu as pltpu

EPS = 1e-05
HIGH = lax.Precision.HIGHEST


def depthwise(edge, fresh, weight, offset_bias):
    sequence = jnp.concatenate([edge, fresh], axis=1).astype(jnp.float32)
    window = fresh.shape[1]
    summed = sequence[:, 0:window] * weight[0]
    for offset in range(1, weight.shape[0]):
        summed = summed + sequence[:, offset : offset + window] * weight[offset]
    return jax.nn.silu(summed + offset_bias)


def new_edge(edge, fresh, counts):
    sequence = jnp.concatenate([edge, fresh], axis=1)
    keep_rows = edge.shape[1]
    result = edge
    for length in range(1, fresh.shape[1] + 1):
        result = jnp.where(
            (counts == length)[:, None, None], sequence[:, length : length + keep_rows], result
        )
    return result


def rank_rows(partner, position, capacity):
    matching = partner[:, None] == partner[None, :]
    earlier = position[None, :] < position[:, None]
    ranking = jnp.sum(jnp.logical_and(matching, earlier), axis=1)
    return partner * capacity + ranking


def invert(values, size):
    hits = values[None, :] == jnp.arange(size, dtype=jnp.int32)[:, None]
    return jnp.sum(jnp.where(hits, jnp.arange(values.shape[0], dtype=jnp.int32)[None, :], 0), axis=1)


def route_rows(anchor, first_slot, slot_count, all_slots, capacity):
    mine = first_slot + jnp.arange(slot_count, dtype=jnp.int32)
    hits = anchor[None, :] == mine[:, None]
    targets = jnp.sum(jnp.where(hits, all_slots[None, :], 0), axis=1)
    send_rows = rank_rows(targets // slot_count, targets % slot_count, capacity)
    sources = lax.dynamic_slice_in_dim(anchor, first_slot, slot_count)
    recv_rows = rank_rows(sources // slot_count, jnp.arange(slot_count, dtype=jnp.int32), capacity)
    return (send_rows, recv_rows)


def recurrence_kernel(rows_ref, *refs, group, window, heads):
    held_refs = refs[:group]
    mix_ref, weight_ref, read_ref, out_ref = refs[group:]
    nt = (((1,), (1,)), ((), ()))
    tn = (((0,), (0,)), ((), ()))
    for q in range(group):
        held_low = held_refs[q][0]
        mix = mix_ref[q]
        read = None
        rest = mix[: 2 * window]
        for _ in range(3):
            part = rest.astype(jnp.bfloat16)
            rest = rest - part.astype(jnp.float32)
            term = lax.dot_general(part, held_low, nt, preferred_element_type=jnp.float32)
            read = term if read is None else read + term
        read_ref[q] = read
        weight = weight_ref[q]
        entry = mix[window : 3 * window]
        w_hi = weight.astype(jnp.bfloat16)
        w_lo = (weight - w_hi.astype(jnp.float32)).astype(jnp.bfloat16)
        e_hi = entry.astype(jnp.bfloat16)
        e_lo = (entry - e_hi.astype(jnp.float32)).astype(jnp.bfloat16)
        pushed = (
            lax.dot_general(w_hi, e_hi, tn, preferred_element_type=jnp.float32)
            + lax.dot_general(w_hi, e_lo, tn, preferred_element_type=jnp.float32)
            + lax.dot_general(w_lo, e_hi, tn, preferred_element_type=jnp.float32)
        )
        held = held_low.astype(jnp.float32)
        rows = held.shape[0] // heads
        carry = mix[2 * window : 2 * window + 1]
        for h in range(heads):
            part = slice(h * rows, (h + 1) * rows)
            out_ref[q, part] = (carry[:, h : h + 1] * held[part] + pushed[part]).astype(
                out_ref.dtype
            )


def recurrence(received, rows, mix, weight, state_rows, heads, group=8):
    slot_count, _, lanes = received.shape
    window = mix.shape[1] // 4
    held_specs = [
        pl.BlockSpec((1, state_rows, lanes), lambda i, r, q=q: (r[i * group + q], 0, 0))
        for q in range(group)
    ]
    grid_spec = pltpu.PrefetchScalarGridSpec(
        num_scalar_prefetch=1,
        grid=(slot_count // group,),
        in_specs=held_specs
        + [
            pl.BlockSpec((group, 4 * window, lanes), lambda i, r: (i, 0, 0)),
            pl.BlockSpec((group, 2 * window, state_rows), lambda i, r: (i, 0, 0)),
        ],
        out_specs=[
            pl.BlockSpec((group, 2 * window, state_rows), lambda i, r: (i, 0, 0)),
            pl.BlockSpec((group, state_rows, lanes), lambda i, r: (i, 0, 0)),
        ],
    )
    return pl.pallas_call(
        functools.partial(recurrence_kernel, group=group, window=window, heads=heads),
        grid_spec=grid_spec,
        out_shape=[
            jax.ShapeDtypeStruct((slot_count, 2 * window, state_rows), jnp.float32),
            jax.ShapeDtypeStruct((slot_count, state_rows, lanes), jnp.bfloat16),
        ],
    )(rows, *([received] * group), mix, weight)

MESH = pl.DeviceIdType.MESH


def scatter_sum_kernel(x_ref, out_ref, slots, send_sem, recv_sem, *, n, rows):
    me = lax.axis_index("head")
    group = lax.axis_index("req")
    barrier = pltpu.get_barrier_semaphore()
    for k in range(1, n):
        pl.semaphore_signal(
            barrier, inc=1, device_id=(group, lax.rem(me + k, n)), device_id_type=MESH
        )
    pl.semaphore_wait(barrier, n - 1)
    copies = []
    for k in range(1, n):
        peer = lax.rem(me + k, n)
        start = pl.multiple_of(peer * rows, rows)
        copy = pltpu.make_async_remote_copy(
            src_ref=x_ref.at[pl.ds(start, rows)],
            dst_ref=slots.at[k - 1],
            send_sem=send_sem.at[k - 1],
            recv_sem=recv_sem.at[k - 1],
            device_id=(group, peer),
            device_id_type=MESH,
        )
        copy.start()
        copies.append(copy)
    own = pl.multiple_of(me * rows, rows)
    total = x_ref[pl.ds(own, rows)].astype(jnp.float32)
    for k, copy in enumerate(copies):
        copy.wait()
        total = total + slots[k].astype(jnp.float32)
    out_ref[...] = total


def scatter_sum(x, n):
    rows = x.shape[0] // n
    return pl.pallas_call(
        functools.partial(scatter_sum_kernel, n=n, rows=rows),
        out_shape=jax.ShapeDtypeStruct((rows, x.shape[1]), jnp.float32),
        in_specs=[pl.BlockSpec(memory_space=pltpu.VMEM)],
        out_specs=pl.BlockSpec(memory_space=pltpu.VMEM),
        scratch_shapes=[
            pltpu.VMEM((n - 1, rows, x.shape[1]), x.dtype),
            pltpu.SemaphoreType.DMA((n - 1,)),
            pltpu.SemaphoreType.DMA((n - 1,)),
        ],
        compiler_params=pltpu.CompilerParams(collective_id=0, has_side_effects=True),
    )(x)


def exchange_kernel(x_ref, out_ref, send_sem, recv_sem, local_sem, *, n):
    me = lax.axis_index("req")
    head = lax.axis_index("head")
    barrier = pltpu.get_barrier_semaphore()
    for k in range(1, n):
        pl.semaphore_signal(
            barrier, inc=1, device_id=(lax.rem(me + k, n), head), device_id_type=MESH
        )
    pl.semaphore_wait(barrier, n - 1)
    own = pltpu.make_async_copy(x_ref.at[me], out_ref.at[me], local_sem.at[0])
    own.start()
    copies = []
    for k in range(1, n):
        peer = lax.rem(me + k, n)
        copy = pltpu.make_async_remote_copy(
            src_ref=x_ref.at[peer],
            dst_ref=out_ref.at[me],
            send_sem=send_sem.at[k - 1],
            recv_sem=recv_sem.at[k - 1],
            device_id=(peer, head),
            device_id_type=MESH,
        )
        copy.start()
        copies.append(copy)
    own.wait()
    for copy in copies:
        copy.wait()


def exchange(x, tag):
    n = x.shape[0]
    return pl.pallas_call(
        functools.partial(exchange_kernel, n=n),
        out_shape=jax.ShapeDtypeStruct(x.shape, x.dtype),
        in_specs=[pl.BlockSpec(memory_space=pl.ANY)],
        out_specs=pl.BlockSpec(memory_space=pl.ANY),
        scratch_shapes=[
            pltpu.SemaphoreType.DMA((n - 1,)),
            pltpu.SemaphoreType.DMA((n - 1,)),
            pltpu.SemaphoreType.DMA((1,)),
        ],
        compiler_params=pltpu.CompilerParams(collective_id=tag, has_side_effects=True),
    )(x)


def migrate(item, mig_dest, slot_count, groups, device):
    length = item.shape[0]
    lanes = 128
    piece = -(-length // (groups * lanes)) * lanes
    padded = jnp.pad(item, (0, piece * groups - length)).reshape(groups, piece // lanes, lanes)
    first = exchange(padded, 1).reshape(groups, piece)
    dest_dev = mig_dest // slot_count
    order = invert(dest_dev, groups)
    pick = (order[:, None] == jnp.arange(groups, dtype=jnp.int32)[None, :]).astype(first.dtype)
    routed = jnp.dot(pick, first, preferred_element_type=jnp.float32).astype(first.dtype)
    second = exchange(routed.reshape(groups, piece // lanes, lanes), 2)
    arrived = second.reshape(-1)[:length]
    target_local = jnp.sum(jnp.where(dest_dev == device, mig_dest, 0)) - device * slot_count
    return arrived, target_local


def local(
    tokens,
    pre_gain,
    inner_weight,
    shared_weight,
    conv_inner,
    conv_inner_bias,
    conv_shared,
    conv_shared_bias,
    step_bias,
    decay_log,
    skip_gain,
    gate_gain,
    out_weight,
    states,
    edge_inner,
    edge_shared,
    counts,
    mig_ids,
    mig_dest,
    reorder,
):
    slot_count, heads_here, head_dim, state_dim = states.shape
    inner_here = heads_here * head_dim
    lanes = state_dim
    groups = lax.axis_size("req")
    device = lax.axis_index("req")
    first_slot = device * slot_count
    stride = (slot_count + groups - 1) // groups
    all_slots = jnp.arange(slot_count * groups, dtype=jnp.int32)

    rows_in = tokens.astype(jnp.float32)
    normed = (
        rows_in * lax.rsqrt(jnp.mean(rows_in * rows_in, axis=-1, keepdims=True) + EPS) * pre_gain
    ).astype(jnp.bfloat16)
    inner_flat = inner_weight.reshape(inner_weight.shape[0], 2 * inner_here)
    piece_rows = lax.all_gather(normed, "head", axis=0, tiled=True)
    inner_rows = jnp.dot(piece_rows, inner_flat, preferred_element_type=jnp.float32).astype(
        jnp.bfloat16
    )
    shared_rows = jnp.dot(piece_rows, shared_weight, preferred_element_type=jnp.float32).astype(
        jnp.bfloat16
    )

    state_rows = heads_here * head_dim * state_dim // lanes
    inner_edge_rows = edge_inner.shape[1] * edge_inner.shape[2] // lanes
    shared_edge_rows = edge_shared.shape[1] * edge_shared.shape[2] // lanes
    state_block = states.reshape(slot_count, state_rows, lanes)
    edge_block = jnp.concatenate(
        [
            edge_inner.reshape(slot_count, inner_edge_rows, lanes),
            edge_shared.reshape(slot_count, shared_edge_rows, lanes),
        ],
        axis=1,
    )
    row_total = state_rows + edge_block.shape[1]

    moving = mig_ids.shape[0] // groups
    own_id = jnp.sum(jnp.where(jnp.arange(mig_ids.shape[0]) == device * moving, mig_ids, 0))
    mig_local = own_id - first_slot
    item = jnp.concatenate(
        [
            lax.dynamic_index_in_dim(part, mig_local, 0, keepdims=False).reshape(-1)
            for part in (states, edge_inner, edge_shared)
        ]
    )
    arrived, target_local = migrate(item, mig_dest, slot_count, groups, device)
    arrived = arrived.reshape(row_total, lanes)

    send_rows, recv_rows = route_rows(reorder, first_slot, slot_count, all_slots, stride)
    buffer_rows = groups * stride
    send_idx = invert(send_rows, buffer_rows)
    target_row = jnp.sum(jnp.where(jnp.arange(slot_count) == target_local, send_rows, 0))
    send_edges = lax.dynamic_update_slice(
        edge_block[send_idx], arrived[None, state_rows:], (target_row, 0, 0)
    )
    send_states = lax.dynamic_update_slice(
        state_block[send_idx], arrived[None, :state_rows], (target_row, 0, 0)
    )
    received_edges = exchange(send_edges, 3)
    received = lax.all_to_all(send_states, "req", 0, 0, tiled=True)
    moved = received_edges[recv_rows]
    moved_inner = moved[:, :inner_edge_rows].reshape(edge_inner.shape)
    moved_shared = moved[:, inner_edge_rows:].reshape(edge_shared.shape)

    window = inner_rows.shape[0] // slot_count
    inner_rows = inner_rows.reshape(slot_count, window, 2 * inner_here)
    shared_rows = shared_rows.reshape(slot_count, window, shared_rows.shape[1])
    gate_part = inner_rows[:, :, :inner_here]
    value_part = inner_rows[:, :, inner_here:]
    fresh_shared = shared_rows[:, :, : 2 * state_dim]
    head_index = lax.axis_index("head")
    step_raw = lax.dynamic_slice_in_dim(
        shared_rows[:, :, 2 * state_dim :], head_index * heads_here, heads_here, axis=2
    )
    edge_inner_out = new_edge(moved_inner, value_part, counts)
    edge_shared_out = new_edge(moved_shared, fresh_shared, counts)
    mixed_inner = depthwise(moved_inner, value_part, conv_inner, conv_inner_bias)
    mixed_shared = depthwise(moved_shared, fresh_shared, conv_shared, conv_shared_bias)
    valid = jnp.arange(window)[None, :] < counts[:, None]
    step_size = jax.nn.softplus(step_raw.astype(jnp.float32) + step_bias)
    step_size = jnp.where(valid[:, :, None], step_size, 0.0)
    decay = -jnp.exp(decay_log)
    entries = mixed_shared[:, :, :state_dim]
    readouts = mixed_shared[:, :, state_dim:]

    factor = jnp.exp(step_size * decay)
    cum = [factor[:, 0]]
    for t in range(1, window):
        cum.append(cum[-1] * factor[:, t])
    span = {}
    for t in range(window):
        span[(t, t)] = jnp.ones_like(factor[:, 0])
        for s in range(t - 1, -1, -1):
            span[(t, s)] = span[(t, s + 1)] * factor[:, s + 1]

    def per_head(v):
        return jnp.repeat(v, head_dim, axis=-1)

    flat_inputs = mixed_inner.reshape(slot_count, window, inner_here)
    weighted = per_head(step_size) * flat_inputs
    last = window - 1
    pushed = jnp.stack([per_head(span[(last, s)]) * weighted[:, s] for s in range(window)], axis=1)
    weight = jnp.concatenate([pushed, jnp.zeros_like(pushed)], axis=1)
    carry = jnp.pad(cum[last], ((0, 0), (0, state_dim - heads_here)))[:, None, :]
    mix = jnp.concatenate(
        [readouts, entries, carry, jnp.zeros((slot_count, 2 * window - 1, state_dim), jnp.float32)],
        axis=1,
    )
    read, states_out = recurrence(received, recv_rows, mix, weight, state_rows, heads_here)
    states_out = states_out.reshape(states.shape)
    overlap = jnp.einsum("rtn,rsn->rts", readouts, entries, precision=HIGH)
    skip_wide = jnp.repeat(skip_gain, head_dim)
    produced = []
    for t in range(window):
        acc = per_head(cum[t]) * read[:, t]
        for s in range(t + 1):
            acc = acc + per_head(span[(t, s)] * overlap[:, t, s, None]) * weighted[:, s]
        produced.append(acc + skip_wide * flat_inputs[:, t])
    outputs = jnp.stack(produced, axis=1)

    gated = outputs * jax.nn.silu(gate_part.astype(jnp.float32))
    square_part = jnp.sum(gated * gated, axis=-1).reshape(slot_count * window, 1)
    pre_scaled = (
        jnp.where(valid[:, :, None], gated * gate_gain, 0.0)
        .astype(jnp.bfloat16)
        .reshape(slot_count * window, inner_here)
    )
    partial = jnp.dot(pre_scaled, out_weight, preferred_element_type=jnp.float32)
    square_hi = square_part.astype(jnp.bfloat16)
    square_lo = (square_part - square_hi.astype(jnp.float32)).astype(jnp.bfloat16)
    extra = jnp.pad(
        jnp.concatenate([square_hi, square_lo], axis=1), ((0, 0), (0, 126))
    )
    combined = jnp.concatenate([partial.astype(jnp.bfloat16), extra], axis=1)
    reduced = scatter_sum(combined, lax.axis_size("head"))
    full_inner = inner_here * lax.axis_size("head")
    width = partial.shape[1]
    square_sum = reduced[:, width : width + 1] + reduced[:, width + 1 : width + 2]
    scale = lax.rsqrt(square_sum / full_inner + EPS)
    hidden_out = (rows_in + reduced[:, :width] * scale).astype(jnp.bfloat16)
    return (hidden_out, states_out, edge_inner_out, edge_shared_out)


def solution(mesh):
    placed = (
        P(("req", "head"), None),
        P(),
        P(None, None, "head"),
        P(),
        P(None, "head"),
        P("head"),
        P(),
        P(),
        P("head"),
        P("head"),
        P("head"),
        P("head"),
        P("head", None),
        P("req", "head", None, None),
        P("req", None, "head"),
        P("req", None, None),
        P("req"),
        P(),
        P(),
        P(),
    )
    return jax.shard_map(
        local,
        mesh=mesh,
        in_specs=placed,
        out_specs=(
            P(("req", "head"), None),
            P("req", "head", None, None),
            P("req", None, "head"),
            P("req", None, None),
        ),
        check_vma=False,
    )
```

```python
import functools

import jax
import jax.numpy as jnp
from jax import lax
from jax.sharding import PartitionSpec as P
from jax.experimental import pallas as pl
from jax.experimental.pallas import tpu as pltpu

EPS = 1e-05
HIGH = lax.Precision.HIGHEST


def depthwise(edge, fresh, weight, offset_bias):
    sequence = jnp.concatenate([edge, fresh], axis=1).astype(jnp.float32)
    window = fresh.shape[1]
    summed = sequence[:, 0:window] * weight[0]
    for offset in range(1, weight.shape[0]):
        summed = summed + sequence[:, offset : offset + window] * weight[offset]
    return jax.nn.silu(summed + offset_bias)


def new_edge(edge, fresh, counts):
    sequence = jnp.concatenate([edge, fresh], axis=1)
    keep_rows = edge.shape[1]
    result = edge
    for length in range(1, fresh.shape[1] + 1):
        result = jnp.where(
            (counts == length)[:, None, None], sequence[:, length : length + keep_rows], result
        )
    return result


def rank_rows(partner, position, capacity):
    matching = partner[:, None] == partner[None, :]
    earlier = position[None, :] < position[:, None]
    ranking = jnp.sum(jnp.logical_and(matching, earlier), axis=1)
    return partner * capacity + ranking


def invert(values, size):
    hits = values[None, :] == jnp.arange(size, dtype=jnp.int32)[:, None]
    return jnp.sum(jnp.where(hits, jnp.arange(values.shape[0], dtype=jnp.int32)[None, :], 0), axis=1)


def route_rows(anchor, first_slot, slot_count, all_slots, capacity):
    mine = first_slot + jnp.arange(slot_count, dtype=jnp.int32)
    hits = anchor[None, :] == mine[:, None]
    targets = jnp.sum(jnp.where(hits, all_slots[None, :], 0), axis=1)
    send_rows = rank_rows(targets // slot_count, targets % slot_count, capacity)
    sources = lax.dynamic_slice_in_dim(anchor, first_slot, slot_count)
    recv_rows = rank_rows(sources // slot_count, jnp.arange(slot_count, dtype=jnp.int32), capacity)
    return (send_rows, recv_rows)


def recurrence_kernel(rows_ref, *refs, group, window, heads):
    held_refs = refs[:group]
    mix_ref, weight_ref, read_ref, out_ref = refs[group:]
    nt = (((1,), (1,)), ((), ()))
    tn = (((0,), (0,)), ((), ()))
    for q in range(group):
        held_low = held_refs[q][0]
        mix = mix_ref[q]
        read = None
        rest = mix[: 2 * window]
        for _ in range(3):
            part = rest.astype(jnp.bfloat16)
            rest = rest - part.astype(jnp.float32)
            term = lax.dot_general(part, held_low, nt, preferred_element_type=jnp.float32)
            read = term if read is None else read + term
        read_ref[q] = read
        weight = weight_ref[q]
        entry = mix[window : 3 * window]
        w_hi = weight.astype(jnp.bfloat16)
        w_lo = (weight - w_hi.astype(jnp.float32)).astype(jnp.bfloat16)
        e_hi = entry.astype(jnp.bfloat16)
        e_lo = (entry - e_hi.astype(jnp.float32)).astype(jnp.bfloat16)
        pushed = (
            lax.dot_general(w_hi, e_hi, tn, preferred_element_type=jnp.float32)
            + lax.dot_general(w_hi, e_lo, tn, preferred_element_type=jnp.float32)
            + lax.dot_general(w_lo, e_hi, tn, preferred_element_type=jnp.float32)
        )
        held = held_low.astype(jnp.float32)
        rows = held.shape[0] // heads
        carry = mix[2 * window : 2 * window + 1]
        for h in range(heads):
            part = slice(h * rows, (h + 1) * rows)
            out_ref[q, part] = (carry[:, h : h + 1] * held[part] + pushed[part]).astype(
                out_ref.dtype
            )


def recurrence(received, rows, mix, weight, state_rows, heads, group=8):
    slot_count, _, lanes = received.shape
    window = mix.shape[1] // 4
    held_specs = [
        pl.BlockSpec((1, state_rows, lanes), lambda i, r, q=q: (r[i * group + q], 0, 0))
        for q in range(group)
    ]
    grid_spec = pltpu.PrefetchScalarGridSpec(
        num_scalar_prefetch=1,
        grid=(slot_count // group,),
        in_specs=held_specs
        + [
            pl.BlockSpec((group, 4 * window, lanes), lambda i, r: (i, 0, 0)),
            pl.BlockSpec((group, 2 * window, state_rows), lambda i, r: (i, 0, 0)),
        ],
        out_specs=[
            pl.BlockSpec((group, 2 * window, state_rows), lambda i, r: (i, 0, 0)),
            pl.BlockSpec((group, state_rows, lanes), lambda i, r: (i, 0, 0)),
        ],
    )
    return pl.pallas_call(
        functools.partial(recurrence_kernel, group=group, window=window, heads=heads),
        grid_spec=grid_spec,
        out_shape=[
            jax.ShapeDtypeStruct((slot_count, 2 * window, state_rows), jnp.float32),
            jax.ShapeDtypeStruct((slot_count, state_rows, lanes), jnp.bfloat16),
        ],
    )(rows, *([received] * group), mix, weight)

MESH = pl.DeviceIdType.MESH


def scatter_sum_kernel(x_ref, out_ref, slots, send_sem, recv_sem, *, n, rows):
    me = lax.axis_index("head")
    group = lax.axis_index("req")
    barrier = pltpu.get_barrier_semaphore()
    for k in range(1, n):
        pl.semaphore_signal(
            barrier, inc=1, device_id=(group, lax.rem(me + k, n)), device_id_type=MESH
        )
    pl.semaphore_wait(barrier, n - 1)
    copies = []
    for k in range(1, n):
        peer = lax.rem(me + k, n)
        start = pl.multiple_of(peer * rows, rows)
        copy = pltpu.make_async_remote_copy(
            src_ref=x_ref.at[pl.ds(start, rows)],
            dst_ref=slots.at[k - 1],
            send_sem=send_sem.at[k - 1],
            recv_sem=recv_sem.at[k - 1],
            device_id=(group, peer),
            device_id_type=MESH,
        )
        copy.start()
        copies.append(copy)
    own = pl.multiple_of(me * rows, rows)
    total = x_ref[pl.ds(own, rows)].astype(jnp.float32)
    for k, copy in enumerate(copies):
        copy.wait()
        total = total + slots[k].astype(jnp.float32)
    out_ref[...] = total


def scatter_sum(x, n):
    rows = x.shape[0] // n
    return pl.pallas_call(
        functools.partial(scatter_sum_kernel, n=n, rows=rows),
        out_shape=jax.ShapeDtypeStruct((rows, x.shape[1]), jnp.float32),
        in_specs=[pl.BlockSpec(memory_space=pltpu.VMEM)],
        out_specs=pl.BlockSpec(memory_space=pltpu.VMEM),
        scratch_shapes=[
            pltpu.VMEM((n - 1, rows, x.shape[1]), x.dtype),
            pltpu.SemaphoreType.DMA((n - 1,)),
            pltpu.SemaphoreType.DMA((n - 1,)),
        ],
        compiler_params=pltpu.CompilerParams(collective_id=0, has_side_effects=True),
    )(x)


def exchange_kernel(x_ref, out_ref, send_sem, recv_sem, local_sem, *, n):
    me = lax.axis_index("req")
    head = lax.axis_index("head")
    barrier = pltpu.get_barrier_semaphore()
    for k in range(1, n):
        pl.semaphore_signal(
            barrier, inc=1, device_id=(lax.rem(me + k, n), head), device_id_type=MESH
        )
    pl.semaphore_wait(barrier, n - 1)
    own = pltpu.make_async_copy(x_ref.at[me], out_ref.at[me], local_sem.at[0])
    own.start()
    copies = []
    for k in range(1, n):
        peer = lax.rem(me + k, n)
        copy = pltpu.make_async_remote_copy(
            src_ref=x_ref.at[peer],
            dst_ref=out_ref.at[me],
            send_sem=send_sem.at[k - 1],
            recv_sem=recv_sem.at[k - 1],
            device_id=(peer, head),
            device_id_type=MESH,
        )
        copy.start()
        copies.append(copy)
    own.wait()
    for copy in copies:
        copy.wait()


def exchange(x, tag):
    n = x.shape[0]
    return pl.pallas_call(
        functools.partial(exchange_kernel, n=n),
        out_shape=jax.ShapeDtypeStruct(x.shape, x.dtype),
        in_specs=[pl.BlockSpec(memory_space=pl.ANY)],
        out_specs=pl.BlockSpec(memory_space=pl.ANY),
        scratch_shapes=[
            pltpu.SemaphoreType.DMA((n - 1,)),
            pltpu.SemaphoreType.DMA((n - 1,)),
            pltpu.SemaphoreType.DMA((1,)),
        ],
        compiler_params=pltpu.CompilerParams(collective_id=tag, has_side_effects=True),
    )(x)


def exchange_pack_kernel(
    idx_ref, x_ref, states_ref, edges_ref, out_ref, send_ref, send_sem, recv_sem, local_sem, *, n
):
    me = lax.axis_index("req")
    head = lax.axis_index("head")
    barrier = pltpu.get_barrier_semaphore()
    for k in range(1, n):
        pl.semaphore_signal(
            barrier, inc=1, device_id=(lax.rem(me + k, n), head), device_id_type=MESH
        )
    pl.semaphore_wait(barrier, n - 1)
    own = pltpu.make_async_copy(x_ref.at[me], out_ref.at[me], local_sem.at[0])
    own.start()
    copies = []
    for k in range(1, n):
        peer = lax.rem(me + k, n)
        copy = pltpu.make_async_remote_copy(
            src_ref=x_ref.at[peer],
            dst_ref=out_ref.at[me],
            send_sem=send_sem.at[k - 1],
            recv_sem=recv_sem.at[k - 1],
            device_id=(peer, head),
            device_id_type=MESH,
        )
        copy.start()
        copies.append(copy)
    state_rows = states_ref.shape[1]
    for r in range(send_ref.shape[0]):
        row = idx_ref[r]
        send_ref[r, :state_rows] = states_ref[row]
        send_ref[r, state_rows:] = edges_ref[row]
    own.wait()
    for copy in copies:
        copy.wait()


def exchange_pack(x, idx, states_block, edges_block, tag):
    n = x.shape[0]
    slots, state_rows, lanes = states_block.shape
    return pl.pallas_call(
        functools.partial(exchange_pack_kernel, n=n),
        out_shape=[
            jax.ShapeDtypeStruct(x.shape, x.dtype),
            jax.ShapeDtypeStruct(
                (idx.shape[0], state_rows + edges_block.shape[1], lanes), states_block.dtype
            ),
        ],
        in_specs=[
            pl.BlockSpec(memory_space=pltpu.SMEM),
            pl.BlockSpec(memory_space=pl.ANY),
            pl.BlockSpec(memory_space=pltpu.VMEM),
            pl.BlockSpec(memory_space=pltpu.VMEM),
        ],
        out_specs=[
            pl.BlockSpec(memory_space=pl.ANY),
            pl.BlockSpec(memory_space=pltpu.VMEM),
        ],
        scratch_shapes=[
            pltpu.SemaphoreType.DMA((n - 1,)),
            pltpu.SemaphoreType.DMA((n - 1,)),
            pltpu.SemaphoreType.DMA((1,)),
        ],
        compiler_params=pltpu.CompilerParams(collective_id=tag, has_side_effects=True),
    )(idx, x, states_block, edges_block)


def migrate(item, mig_dest, slot_count, groups, device, pack):
    length = item.shape[0]
    lanes = 128
    piece = -(-length // (groups * lanes)) * lanes
    padded = jnp.pad(item, (0, piece * groups - length)).reshape(groups, piece // lanes, lanes)
    first, send_base = pack(padded)
    first = first.reshape(groups, piece)
    dest_dev = mig_dest // slot_count
    order = invert(dest_dev, groups)
    pick = (order[:, None] == jnp.arange(groups, dtype=jnp.int32)[None, :]).astype(first.dtype)
    routed = jnp.dot(pick, first, preferred_element_type=jnp.float32).astype(first.dtype)
    second = exchange(routed.reshape(groups, piece // lanes, lanes), 2)
    arrived = second.reshape(-1)[:length]
    target_local = jnp.sum(jnp.where(dest_dev == device, mig_dest, 0)) - device * slot_count
    return arrived, target_local, send_base


def local(
    tokens,
    pre_gain,
    inner_weight,
    shared_weight,
    conv_inner,
    conv_inner_bias,
    conv_shared,
    conv_shared_bias,
    step_bias,
    decay_log,
    skip_gain,
    gate_gain,
    out_weight,
    states,
    edge_inner,
    edge_shared,
    counts,
    mig_ids,
    mig_dest,
    reorder,
):
    slot_count, heads_here, head_dim, state_dim = states.shape
    inner_here = heads_here * head_dim
    lanes = state_dim
    groups = lax.axis_size("req")
    device = lax.axis_index("req")
    first_slot = device * slot_count
    stride = (slot_count + groups - 1) // groups
    all_slots = jnp.arange(slot_count * groups, dtype=jnp.int32)

    rows_in = tokens.astype(jnp.float32)
    normed = (
        rows_in * lax.rsqrt(jnp.mean(rows_in * rows_in, axis=-1, keepdims=True) + EPS) * pre_gain
    ).astype(jnp.bfloat16)
    inner_flat = inner_weight.reshape(inner_weight.shape[0], 2 * inner_here)
    piece_rows = lax.all_gather(normed, "head", axis=0, tiled=True)
    inner_rows = jnp.dot(piece_rows, inner_flat, preferred_element_type=jnp.float32).astype(
        jnp.bfloat16
    )
    shared_rows = jnp.dot(piece_rows, shared_weight, preferred_element_type=jnp.float32).astype(
        jnp.bfloat16
    )

    state_rows = heads_here * head_dim * state_dim // lanes
    inner_edge_rows = edge_inner.shape[1] * edge_inner.shape[2] // lanes
    shared_edge_rows = edge_shared.shape[1] * edge_shared.shape[2] // lanes
    state_block = states.reshape(slot_count, state_rows, lanes)
    edge_block = jnp.concatenate(
        [
            edge_inner.reshape(slot_count, inner_edge_rows, lanes),
            edge_shared.reshape(slot_count, shared_edge_rows, lanes),
        ],
        axis=1,
    )
    row_total = state_rows + edge_block.shape[1]
    send_rows, recv_rows = route_rows(reorder, first_slot, slot_count, all_slots, stride)
    buffer_rows = groups * stride
    send_idx = invert(send_rows, buffer_rows)

    moving = mig_ids.shape[0] // groups
    own_id = jnp.sum(jnp.where(jnp.arange(mig_ids.shape[0]) == device * moving, mig_ids, 0))
    mig_local = own_id - first_slot
    item = jnp.concatenate(
        [
            lax.dynamic_index_in_dim(part, mig_local, 0, keepdims=False).reshape(-1)
            for part in (states, edge_inner, edge_shared)
        ]
    )
    arrived, target_local, send_base = migrate(
        item,
        mig_dest,
        slot_count,
        groups,
        device,
        lambda x: exchange_pack(x, send_idx, state_block, edge_block, 1),
    )
    arrived = arrived.reshape(row_total, lanes)

    target_row = jnp.sum(jnp.where(jnp.arange(slot_count) == target_local, send_rows, 0))
    send_buf = lax.dynamic_update_slice(send_base, arrived[None], (target_row, 0, 0))
    received = lax.all_to_all(send_buf, "req", 0, 0, tiled=True)
    moved = received[:, state_rows:][recv_rows]
    moved_inner = moved[:, :inner_edge_rows].reshape(edge_inner.shape)
    moved_shared = moved[:, inner_edge_rows:].reshape(edge_shared.shape)

    window = inner_rows.shape[0] // slot_count
    inner_rows = inner_rows.reshape(slot_count, window, 2 * inner_here)
    shared_rows = shared_rows.reshape(slot_count, window, shared_rows.shape[1])
    gate_part = inner_rows[:, :, :inner_here]
    value_part = inner_rows[:, :, inner_here:]
    fresh_shared = shared_rows[:, :, : 2 * state_dim]
    head_index = lax.axis_index("head")
    step_raw = lax.dynamic_slice_in_dim(
        shared_rows[:, :, 2 * state_dim :], head_index * heads_here, heads_here, axis=2
    )
    edge_inner_out = new_edge(moved_inner, value_part, counts)
    edge_shared_out = new_edge(moved_shared, fresh_shared, counts)
    mixed_inner = depthwise(moved_inner, value_part, conv_inner, conv_inner_bias)
    mixed_shared = depthwise(moved_shared, fresh_shared, conv_shared, conv_shared_bias)
    valid = jnp.arange(window)[None, :] < counts[:, None]
    step_size = jax.nn.softplus(step_raw.astype(jnp.float32) + step_bias)
    step_size = jnp.where(valid[:, :, None], step_size, 0.0)
    decay = -jnp.exp(decay_log)
    entries = mixed_shared[:, :, :state_dim]
    readouts = mixed_shared[:, :, state_dim:]

    factor = jnp.exp(step_size * decay)
    cum = [factor[:, 0]]
    for t in range(1, window):
        cum.append(cum[-1] * factor[:, t])
    span = {}
    for t in range(window):
        span[(t, t)] = jnp.ones_like(factor[:, 0])
        for s in range(t - 1, -1, -1):
            span[(t, s)] = span[(t, s + 1)] * factor[:, s + 1]

    def per_head(v):
        return jnp.repeat(v, head_dim, axis=-1)

    flat_inputs = mixed_inner.reshape(slot_count, window, inner_here)
    weighted = per_head(step_size) * flat_inputs
    last = window - 1
    pushed = jnp.stack([per_head(span[(last, s)]) * weighted[:, s] for s in range(window)], axis=1)
    weight = jnp.concatenate([pushed, jnp.zeros_like(pushed)], axis=1)
    carry = jnp.pad(cum[last], ((0, 0), (0, state_dim - heads_here)))[:, None, :]
    mix = jnp.concatenate(
        [readouts, entries, carry, jnp.zeros((slot_count, 2 * window - 1, state_dim), jnp.float32)],
        axis=1,
    )
    read, states_out = recurrence(received, recv_rows, mix, weight, state_rows, heads_here)
    states_out = states_out.reshape(states.shape)
    overlap = jnp.einsum("rtn,rsn->rts", readouts, entries, precision=HIGH)
    skip_wide = jnp.repeat(skip_gain, head_dim)
    produced = []
    for t in range(window):
        acc = per_head(cum[t]) * read[:, t]
        for s in range(t + 1):
            acc = acc + per_head(span[(t, s)] * overlap[:, t, s, None]) * weighted[:, s]
        produced.append(acc + skip_wide * flat_inputs[:, t])
    outputs = jnp.stack(produced, axis=1)

    gated = outputs * jax.nn.silu(gate_part.astype(jnp.float32))
    square_part = jnp.sum(gated * gated, axis=-1).reshape(slot_count * window, 1)
    pre_scaled = (
        jnp.where(valid[:, :, None], gated * gate_gain, 0.0)
        .astype(jnp.bfloat16)
        .reshape(slot_count * window, inner_here)
    )
    partial = jnp.dot(pre_scaled, out_weight, preferred_element_type=jnp.float32)
    square_hi = square_part.astype(jnp.bfloat16)
    square_lo = (square_part - square_hi.astype(jnp.float32)).astype(jnp.bfloat16)
    extra = jnp.pad(
        jnp.concatenate([square_hi, square_lo], axis=1), ((0, 0), (0, 126))
    )
    combined = jnp.concatenate([partial.astype(jnp.bfloat16), extra], axis=1)
    reduced = scatter_sum(combined, lax.axis_size("head"))
    full_inner = inner_here * lax.axis_size("head")
    width = partial.shape[1]
    square_sum = reduced[:, width : width + 1] + reduced[:, width + 1 : width + 2]
    scale = lax.rsqrt(square_sum / full_inner + EPS)
    hidden_out = (rows_in + reduced[:, :width] * scale).astype(jnp.bfloat16)
    return (hidden_out, states_out, edge_inner_out, edge_shared_out)


def solution(mesh):
    placed = (
        P(("req", "head"), None),
        P(),
        P(None, None, "head"),
        P(),
        P(None, "head"),
        P("head"),
        P(),
        P(),
        P("head"),
        P("head"),
        P("head"),
        P("head"),
        P("head", None),
        P("req", "head", None, None),
        P("req", None, "head"),
        P("req", None, None),
        P("req"),
        P(),
        P(),
        P(),
    )
    return jax.shard_map(
        local,
        mesh=mesh,
        in_specs=placed,
        out_specs=(
            P(("req", "head"), None),
            P("req", "head", None, None),
            P("req", None, "head"),
            P("req", None, None),
        ),
        check_vma=False,
    )
```

```python
import functools

import jax
import jax.numpy as jnp
from jax import lax
from jax.sharding import PartitionSpec as P
from jax.experimental import pallas as pl
from jax.experimental.pallas import tpu as pltpu

EPS = 1e-05
HIGH = lax.Precision.HIGHEST


def depthwise(edge, fresh, weight, offset_bias):
    sequence = jnp.concatenate([edge, fresh], axis=1).astype(jnp.float32)
    window = fresh.shape[1]
    summed = sequence[:, 0:window] * weight[0]
    for offset in range(1, weight.shape[0]):
        summed = summed + sequence[:, offset : offset + window] * weight[offset]
    return jax.nn.silu(summed + offset_bias)


def new_edge(edge, fresh, counts):
    sequence = jnp.concatenate([edge, fresh], axis=1)
    keep_rows = edge.shape[1]
    result = edge
    for length in range(1, fresh.shape[1] + 1):
        result = jnp.where(
            (counts == length)[:, None, None], sequence[:, length : length + keep_rows], result
        )
    return result


def rank_rows(partner, position, capacity):
    matching = partner[:, None] == partner[None, :]
    earlier = position[None, :] < position[:, None]
    ranking = jnp.sum(jnp.logical_and(matching, earlier), axis=1)
    return partner * capacity + ranking


def invert(values, size):
    hits = values[None, :] == jnp.arange(size, dtype=jnp.int32)[:, None]
    return jnp.sum(jnp.where(hits, jnp.arange(values.shape[0], dtype=jnp.int32)[None, :], 0), axis=1)


def route_rows(anchor, first_slot, slot_count, all_slots, capacity):
    mine = first_slot + jnp.arange(slot_count, dtype=jnp.int32)
    hits = anchor[None, :] == mine[:, None]
    targets = jnp.sum(jnp.where(hits, all_slots[None, :], 0), axis=1)
    send_rows = rank_rows(targets // slot_count, targets % slot_count, capacity)
    sources = lax.dynamic_slice_in_dim(anchor, first_slot, slot_count)
    recv_rows = rank_rows(sources // slot_count, jnp.arange(slot_count, dtype=jnp.int32), capacity)
    return (send_rows, recv_rows)


def recurrence_kernel(rows_ref, *refs, group, window, heads):
    held_refs = refs[:group]
    mix_ref, weight_ref, read_ref, out_ref = refs[group:]
    nt = (((1,), (1,)), ((), ()))
    tn = (((0,), (0,)), ((), ()))
    for q in range(group):
        held_low = held_refs[q][0]
        mix = mix_ref[q]
        read = None
        rest = mix[: 2 * window]
        for _ in range(3):
            part = rest.astype(jnp.bfloat16)
            rest = rest - part.astype(jnp.float32)
            term = lax.dot_general(part, held_low, nt, preferred_element_type=jnp.float32)
            read = term if read is None else read + term
        read_ref[q] = read
        weight = weight_ref[q]
        entry = mix[window : 3 * window]
        w_hi = weight.astype(jnp.bfloat16)
        w_lo = (weight - w_hi.astype(jnp.float32)).astype(jnp.bfloat16)
        e_hi = entry.astype(jnp.bfloat16)
        e_lo = (entry - e_hi.astype(jnp.float32)).astype(jnp.bfloat16)
        pushed = (
            lax.dot_general(w_hi, e_hi, tn, preferred_element_type=jnp.float32)
            + lax.dot_general(w_hi, e_lo, tn, preferred_element_type=jnp.float32)
            + lax.dot_general(w_lo, e_hi, tn, preferred_element_type=jnp.float32)
        )
        held = held_low.astype(jnp.float32)
        rows = held.shape[0] // heads
        carry = mix[2 * window : 2 * window + 1]
        for h in range(heads):
            part = slice(h * rows, (h + 1) * rows)
            out_ref[q, part] = (carry[:, h : h + 1] * held[part] + pushed[part]).astype(
                out_ref.dtype
            )


def recurrence(received, rows, mix, weight, state_rows, heads, group=8):
    slot_count, _, lanes = received.shape
    window = mix.shape[1] // 4
    held_specs = [
        pl.BlockSpec((1, state_rows, lanes), lambda i, r, q=q: (r[i * group + q], 0, 0))
        for q in range(group)
    ]
    grid_spec = pltpu.PrefetchScalarGridSpec(
        num_scalar_prefetch=1,
        grid=(slot_count // group,),
        in_specs=held_specs
        + [
            pl.BlockSpec((group, 4 * window, lanes), lambda i, r: (i, 0, 0)),
            pl.BlockSpec((group, 2 * window, state_rows), lambda i, r: (i, 0, 0)),
        ],
        out_specs=[
            pl.BlockSpec((group, 2 * window, state_rows), lambda i, r: (i, 0, 0)),
            pl.BlockSpec((group, state_rows, lanes), lambda i, r: (i, 0, 0)),
        ],
    )
    return pl.pallas_call(
        functools.partial(recurrence_kernel, group=group, window=window, heads=heads),
        grid_spec=grid_spec,
        out_shape=[
            jax.ShapeDtypeStruct((slot_count, 2 * window, state_rows), jnp.float32),
            jax.ShapeDtypeStruct((slot_count, state_rows, lanes), jnp.bfloat16),
        ],
    )(rows, *([received] * group), mix, weight)

MESH = pl.DeviceIdType.MESH


def scatter_sum_kernel(x_ref, out_ref, slots, send_sem, recv_sem, *, n, rows):
    me = lax.axis_index("head")
    group = lax.axis_index("req")
    barrier = pltpu.get_barrier_semaphore()
    for k in range(1, n):
        pl.semaphore_signal(
            barrier, inc=1, device_id=(group, lax.rem(me + k, n)), device_id_type=MESH
        )
    pl.semaphore_wait(barrier, n - 1)
    copies = []
    for k in range(1, n):
        peer = lax.rem(me + k, n)
        start = pl.multiple_of(peer * rows, rows)
        copy = pltpu.make_async_remote_copy(
            src_ref=x_ref.at[pl.ds(start, rows)],
            dst_ref=slots.at[k - 1],
            send_sem=send_sem.at[k - 1],
            recv_sem=recv_sem.at[k - 1],
            device_id=(group, peer),
            device_id_type=MESH,
        )
        copy.start()
        copies.append(copy)
    own = pl.multiple_of(me * rows, rows)
    total = x_ref[pl.ds(own, rows)].astype(jnp.float32)
    for k, copy in enumerate(copies):
        copy.wait()
        total = total + slots[k].astype(jnp.float32)
    out_ref[...] = total


def scatter_sum(x, n):
    rows = x.shape[0] // n
    return pl.pallas_call(
        functools.partial(scatter_sum_kernel, n=n, rows=rows),
        out_shape=jax.ShapeDtypeStruct((rows, x.shape[1]), jnp.float32),
        in_specs=[pl.BlockSpec(memory_space=pltpu.VMEM)],
        out_specs=pl.BlockSpec(memory_space=pltpu.VMEM),
        scratch_shapes=[
            pltpu.VMEM((n - 1, rows, x.shape[1]), x.dtype),
            pltpu.SemaphoreType.DMA((n - 1,)),
            pltpu.SemaphoreType.DMA((n - 1,)),
        ],
        compiler_params=pltpu.CompilerParams(collective_id=0, has_side_effects=True),
    )(x)


def exchange_kernel(x_ref, out_ref, send_sem, recv_sem, local_sem, *, n):
    me = lax.axis_index("req")
    head = lax.axis_index("head")
    barrier = pltpu.get_barrier_semaphore()
    for k in range(1, n):
        pl.semaphore_signal(
            barrier, inc=1, device_id=(lax.rem(me + k, n), head), device_id_type=MESH
        )
    pl.semaphore_wait(barrier, n - 1)
    own = pltpu.make_async_copy(x_ref.at[me], out_ref.at[me], local_sem.at[0])
    own.start()
    copies = []
    for k in range(1, n):
        peer = lax.rem(me + k, n)
        copy = pltpu.make_async_remote_copy(
            src_ref=x_ref.at[peer],
            dst_ref=out_ref.at[me],
            send_sem=send_sem.at[k - 1],
            recv_sem=recv_sem.at[k - 1],
            device_id=(peer, head),
            device_id_type=MESH,
        )
        copy.start()
        copies.append(copy)
    own.wait()
    for copy in copies:
        copy.wait()


def exchange(x, tag):
    n = x.shape[0]
    return pl.pallas_call(
        functools.partial(exchange_kernel, n=n),
        out_shape=jax.ShapeDtypeStruct(x.shape, x.dtype),
        in_specs=[pl.BlockSpec(memory_space=pl.ANY)],
        out_specs=pl.BlockSpec(memory_space=pl.ANY),
        scratch_shapes=[
            pltpu.SemaphoreType.DMA((n - 1,)),
            pltpu.SemaphoreType.DMA((n - 1,)),
            pltpu.SemaphoreType.DMA((1,)),
        ],
        compiler_params=pltpu.CompilerParams(collective_id=tag, has_side_effects=True),
    )(x)


def exchange_pack_kernel(
    idx_ref, x_ref, states_ref, edges_ref, out_ref, send_ref, send_sem, recv_sem, local_sem, *, n
):
    me = lax.axis_index("req")
    head = lax.axis_index("head")
    barrier = pltpu.get_barrier_semaphore()
    for k in range(1, n):
        pl.semaphore_signal(
            barrier, inc=1, device_id=(lax.rem(me + k, n), head), device_id_type=MESH
        )
    pl.semaphore_wait(barrier, n - 1)
    own = pltpu.make_async_copy(x_ref.at[me], out_ref.at[me], local_sem.at[0])
    own.start()
    copies = []
    for k in range(1, n):
        peer = lax.rem(me + k, n)
        copy = pltpu.make_async_remote_copy(
            src_ref=x_ref.at[peer],
            dst_ref=out_ref.at[me],
            send_sem=send_sem.at[k - 1],
            recv_sem=recv_sem.at[k - 1],
            device_id=(peer, head),
            device_id_type=MESH,
        )
        copy.start()
        copies.append(copy)
    state_rows = states_ref.shape[1]
    for r in range(send_ref.shape[0]):
        row = idx_ref[r]
        send_ref[r, :state_rows] = states_ref[row]
        send_ref[r, state_rows:] = edges_ref[row]
    own.wait()
    for copy in copies:
        copy.wait()


def exchange_pack(x, idx, states_block, edges_block, tag):
    n = x.shape[0]
    slots, state_rows, lanes = states_block.shape
    return pl.pallas_call(
        functools.partial(exchange_pack_kernel, n=n),
        out_shape=[
            jax.ShapeDtypeStruct(x.shape, x.dtype),
            jax.ShapeDtypeStruct(
                (idx.shape[0], state_rows + edges_block.shape[1], lanes), states_block.dtype
            ),
        ],
        in_specs=[
            pl.BlockSpec(memory_space=pltpu.SMEM),
            pl.BlockSpec(memory_space=pl.ANY),
            pl.BlockSpec(memory_space=pltpu.VMEM),
            pl.BlockSpec(memory_space=pltpu.VMEM),
        ],
        out_specs=[
            pl.BlockSpec(memory_space=pl.ANY),
            pl.BlockSpec(memory_space=pltpu.VMEM),
        ],
        scratch_shapes=[
            pltpu.SemaphoreType.DMA((n - 1,)),
            pltpu.SemaphoreType.DMA((n - 1,)),
            pltpu.SemaphoreType.DMA((1,)),
        ],
        compiler_params=pltpu.CompilerParams(collective_id=tag, has_side_effects=True),
    )(idx, x, states_block, edges_block)


def migrate(item, mig_dest, slot_count, groups, device, pack):
    length = item.shape[0]
    lanes = 128
    piece = -(-length // (groups * lanes)) * lanes
    padded = jnp.pad(item, (0, piece * groups - length)).reshape(groups, piece // lanes, lanes)
    first, send_base = pack(padded)
    first = first.reshape(groups, piece)
    dest_dev = mig_dest // slot_count
    order = invert(dest_dev, groups)
    pick = (order[:, None] == jnp.arange(groups, dtype=jnp.int32)[None, :]).astype(first.dtype)
    routed = jnp.dot(pick, first, preferred_element_type=jnp.float32).astype(first.dtype)
    second = exchange(routed.reshape(groups, piece // lanes, lanes), 2)
    arrived = second.reshape(-1)[:length]
    target_local = jnp.sum(jnp.where(dest_dev == device, mig_dest, 0)) - device * slot_count
    return arrived, target_local, send_base


def local(
    tokens,
    pre_gain,
    inner_weight,
    shared_weight,
    conv_inner,
    conv_inner_bias,
    conv_shared,
    conv_shared_bias,
    step_bias,
    decay_log,
    skip_gain,
    gate_gain,
    out_weight,
    states,
    edge_inner,
    edge_shared,
    counts,
    mig_ids,
    mig_dest,
    reorder,
):
    slot_count, heads_here, head_dim, state_dim = states.shape
    inner_here = heads_here * head_dim
    lanes = state_dim
    groups = lax.axis_size("req")
    device = lax.axis_index("req")
    first_slot = device * slot_count
    stride = (slot_count + groups - 1) // groups
    all_slots = jnp.arange(slot_count * groups, dtype=jnp.int32)

    rows_in = tokens.astype(jnp.float32)
    normed = (
        rows_in * lax.rsqrt(jnp.mean(rows_in * rows_in, axis=-1, keepdims=True) + EPS) * pre_gain
    ).astype(jnp.bfloat16)
    inner_flat = inner_weight.reshape(inner_weight.shape[0], 2 * inner_here)
    piece_rows = lax.all_gather(normed, "head", axis=0, tiled=True)
    inner_rows = jnp.dot(piece_rows, inner_flat, preferred_element_type=jnp.float32).astype(
        jnp.bfloat16
    )
    shared_rows = jnp.dot(piece_rows, shared_weight, preferred_element_type=jnp.float32).astype(
        jnp.bfloat16
    )

    state_rows = heads_here * head_dim * state_dim // lanes
    inner_edge_rows = edge_inner.shape[1] * edge_inner.shape[2] // lanes
    shared_edge_rows = edge_shared.shape[1] * edge_shared.shape[2] // lanes
    state_block = states.reshape(slot_count, state_rows, lanes)
    edge_block = jnp.concatenate(
        [
            edge_inner.reshape(slot_count, inner_edge_rows, lanes),
            edge_shared.reshape(slot_count, shared_edge_rows, lanes),
        ],
        axis=1,
    )
    row_total = state_rows + edge_block.shape[1]
    send_rows, recv_rows = route_rows(reorder, first_slot, slot_count, all_slots, stride)
    buffer_rows = groups * stride
    send_idx = invert(send_rows, buffer_rows)

    moving = mig_ids.shape[0] // groups
    own_id = jnp.sum(jnp.where(jnp.arange(mig_ids.shape[0]) == device * moving, mig_ids, 0))
    mig_local = own_id - first_slot
    item = jnp.concatenate(
        [
            lax.dynamic_index_in_dim(part, mig_local, 0, keepdims=False).reshape(-1)
            for part in (states, edge_block)
        ]
    )
    arrived, target_local, send_base = migrate(
        item,
        mig_dest,
        slot_count,
        groups,
        device,
        lambda x: exchange_pack(x, send_idx, state_block, edge_block, 1),
    )
    arrived = arrived.reshape(row_total, lanes)

    target_row = jnp.sum(jnp.where(jnp.arange(slot_count) == target_local, send_rows, 0))
    send_buf = lax.dynamic_update_slice(send_base, arrived[None], (target_row, 0, 0))
    received = lax.all_to_all(send_buf, "req", 0, 0, tiled=True)
    moved = received[:, state_rows:][recv_rows]
    moved_inner = moved[:, :inner_edge_rows].reshape(edge_inner.shape)
    moved_shared = moved[:, inner_edge_rows:].reshape(edge_shared.shape)

    window = inner_rows.shape[0] // slot_count
    inner_rows = inner_rows.reshape(slot_count, window, 2 * inner_here)
    shared_rows = shared_rows.reshape(slot_count, window, shared_rows.shape[1])
    gate_part = inner_rows[:, :, :inner_here]
    value_part = inner_rows[:, :, inner_here:]
    fresh_shared = shared_rows[:, :, : 2 * state_dim]
    head_index = lax.axis_index("head")
    step_raw = lax.dynamic_slice_in_dim(
        shared_rows[:, :, 2 * state_dim :], head_index * heads_here, heads_here, axis=2
    )
    edge_inner_out = new_edge(moved_inner, value_part, counts)
    edge_shared_out = new_edge(moved_shared, fresh_shared, counts)
    mixed_inner = depthwise(moved_inner, value_part, conv_inner, conv_inner_bias)
    mixed_shared = depthwise(moved_shared, fresh_shared, conv_shared, conv_shared_bias)
    valid = jnp.arange(window)[None, :] < counts[:, None]
    step_size = jax.nn.softplus(step_raw.astype(jnp.float32) + step_bias)
    step_size = jnp.where(valid[:, :, None], step_size, 0.0)
    decay = -jnp.exp(decay_log)
    entries = mixed_shared[:, :, :state_dim]
    readouts = mixed_shared[:, :, state_dim:]

    factor = jnp.exp(step_size * decay)
    cum = [factor[:, 0]]
    for t in range(1, window):
        cum.append(cum[-1] * factor[:, t])
    span = {}
    for t in range(window):
        span[(t, t)] = jnp.ones_like(factor[:, 0])
        for s in range(t - 1, -1, -1):
            span[(t, s)] = span[(t, s + 1)] * factor[:, s + 1]

    def per_head(v):
        return jnp.repeat(v, head_dim, axis=-1)

    flat_inputs = mixed_inner.reshape(slot_count, window, inner_here)
    weighted = per_head(step_size) * flat_inputs
    last = window - 1
    pushed = jnp.stack([per_head(span[(last, s)]) * weighted[:, s] for s in range(window)], axis=1)
    weight = jnp.concatenate([pushed, jnp.zeros_like(pushed)], axis=1)
    carry = jnp.pad(cum[last], ((0, 0), (0, state_dim - heads_here)))[:, None, :]
    mix = jnp.concatenate(
        [readouts, entries, carry, jnp.zeros((slot_count, 2 * window - 1, state_dim), jnp.float32)],
        axis=1,
    )
    read, states_out = recurrence(received, recv_rows, mix, weight, state_rows, heads_here)
    states_out = states_out.reshape(states.shape)
    overlap = jnp.einsum("rtn,rsn->rts", readouts, entries, precision=HIGH)
    skip_wide = jnp.repeat(skip_gain, head_dim)
    produced = []
    for t in range(window):
        acc = per_head(cum[t]) * read[:, t]
        for s in range(t + 1):
            acc = acc + per_head(span[(t, s)] * overlap[:, t, s, None]) * weighted[:, s]
        produced.append(acc + skip_wide * flat_inputs[:, t])
    outputs = jnp.stack(produced, axis=1)

    gated = outputs * jax.nn.silu(gate_part.astype(jnp.float32))
    square_part = jnp.sum(gated * gated, axis=-1).reshape(slot_count * window, 1)
    pre_scaled = (
        jnp.where(valid[:, :, None], gated * gate_gain, 0.0)
        .astype(jnp.bfloat16)
        .reshape(slot_count * window, inner_here)
    )
    partial = jnp.dot(pre_scaled, out_weight, preferred_element_type=jnp.float32)
    square_hi = square_part.astype(jnp.bfloat16)
    square_lo = (square_part - square_hi.astype(jnp.float32)).astype(jnp.bfloat16)
    extra = jnp.pad(
        jnp.concatenate([square_hi, square_lo], axis=1), ((0, 0), (0, 126))
    )
    combined = jnp.concatenate([partial.astype(jnp.bfloat16), extra], axis=1)
    reduced = scatter_sum(combined, lax.axis_size("head"))
    full_inner = inner_here * lax.axis_size("head")
    width = partial.shape[1]
    square_sum = reduced[:, width : width + 1] + reduced[:, width + 1 : width + 2]
    scale = lax.rsqrt(square_sum / full_inner + EPS)
    hidden_out = (rows_in + reduced[:, :width] * scale).astype(jnp.bfloat16)
    return (hidden_out, states_out, edge_inner_out, edge_shared_out)


def solution(mesh):
    placed = (
        P(("req", "head"), None),
        P(),
        P(None, None, "head"),
        P(),
        P(None, "head"),
        P("head"),
        P(),
        P(),
        P("head"),
        P("head"),
        P("head"),
        P("head"),
        P("head", None),
        P("req", "head", None, None),
        P("req", None, "head"),
        P("req", None, None),
        P("req"),
        P(),
        P(),
        P(),
    )
    return jax.shard_map(
        local,
        mesh=mesh,
        in_specs=placed,
        out_specs=(
            P(("req", "head"), None),
            P("req", "head", None, None),
            P("req", None, "head"),
            P("req", None, None),
        ),
        check_vma=False,
    )
```

```python
import functools

import jax
import jax.numpy as jnp
from jax import lax
from jax.sharding import PartitionSpec as P
from jax.experimental import pallas as pl
from jax.experimental.pallas import tpu as pltpu

EPS = 1e-05
HIGH = lax.Precision.HIGHEST


def depthwise(edge, fresh, weight, offset_bias):
    sequence = jnp.concatenate([edge, fresh], axis=1).astype(jnp.float32)
    window = fresh.shape[1]
    summed = sequence[:, 0:window] * weight[0]
    for offset in range(1, weight.shape[0]):
        summed = summed + sequence[:, offset : offset + window] * weight[offset]
    return jax.nn.silu(summed + offset_bias)


def new_edge(edge, fresh, counts):
    sequence = jnp.concatenate([edge, fresh], axis=1)
    keep_rows = edge.shape[1]
    result = edge
    for length in range(1, fresh.shape[1] + 1):
        result = jnp.where(
            (counts == length)[:, None, None], sequence[:, length : length + keep_rows], result
        )
    return result


def rank_rows(partner, position, capacity):
    matching = partner[:, None] == partner[None, :]
    earlier = position[None, :] < position[:, None]
    ranking = jnp.sum(jnp.logical_and(matching, earlier), axis=1)
    return partner * capacity + ranking


def invert(values, size):
    hits = values[None, :] == jnp.arange(size, dtype=jnp.int32)[:, None]
    return jnp.sum(jnp.where(hits, jnp.arange(values.shape[0], dtype=jnp.int32)[None, :], 0), axis=1)


def route_rows(anchor, first_slot, slot_count, all_slots, capacity):
    mine = first_slot + jnp.arange(slot_count, dtype=jnp.int32)
    hits = anchor[None, :] == mine[:, None]
    targets = jnp.sum(jnp.where(hits, all_slots[None, :], 0), axis=1)
    send_rows = rank_rows(targets // slot_count, targets % slot_count, capacity)
    sources = lax.dynamic_slice_in_dim(anchor, first_slot, slot_count)
    recv_rows = rank_rows(sources // slot_count, jnp.arange(slot_count, dtype=jnp.int32), capacity)
    return (send_rows, recv_rows)


def recurrence_kernel(rows_ref, *refs, group, window, heads):
    held_refs = refs[:group]
    mix_ref, weight_ref, read_ref, out_ref = refs[group:]
    nt = (((1,), (1,)), ((), ()))
    tn = (((0,), (0,)), ((), ()))
    for q in range(group):
        held_low = held_refs[q][0]
        mix = mix_ref[q]
        read = None
        rest = mix[: 2 * window]
        for _ in range(3):
            part = rest.astype(jnp.bfloat16)
            rest = rest - part.astype(jnp.float32)
            term = lax.dot_general(part, held_low, nt, preferred_element_type=jnp.float32)
            read = term if read is None else read + term
        read_ref[q] = read
        weight = weight_ref[q]
        entry = mix[window : 3 * window]
        w_hi = weight.astype(jnp.bfloat16)
        w_lo = (weight - w_hi.astype(jnp.float32)).astype(jnp.bfloat16)
        e_hi = entry.astype(jnp.bfloat16)
        e_lo = (entry - e_hi.astype(jnp.float32)).astype(jnp.bfloat16)
        pushed = (
            lax.dot_general(w_hi, e_hi, tn, preferred_element_type=jnp.float32)
            + lax.dot_general(w_hi, e_lo, tn, preferred_element_type=jnp.float32)
            + lax.dot_general(w_lo, e_hi, tn, preferred_element_type=jnp.float32)
        )
        held = held_low.astype(jnp.float32)
        rows = held.shape[0] // heads
        carry = mix[2 * window : 2 * window + 1]
        for h in range(heads):
            part = slice(h * rows, (h + 1) * rows)
            out_ref[q, part] = (carry[:, h : h + 1] * held[part] + pushed[part]).astype(
                out_ref.dtype
            )


def recurrence(received, rows, mix, weight, state_rows, heads, group=8):
    slot_count, _, lanes = received.shape
    window = mix.shape[1] // 4
    held_specs = [
        pl.BlockSpec((1, state_rows, lanes), lambda i, r, q=q: (r[i * group + q], 0, 0))
        for q in range(group)
    ]
    grid_spec = pltpu.PrefetchScalarGridSpec(
        num_scalar_prefetch=1,
        grid=(slot_count // group,),
        in_specs=held_specs
        + [
            pl.BlockSpec((group, 4 * window, lanes), lambda i, r: (i, 0, 0)),
            pl.BlockSpec((group, 2 * window, state_rows), lambda i, r: (i, 0, 0)),
        ],
        out_specs=[
            pl.BlockSpec((group, 2 * window, state_rows), lambda i, r: (i, 0, 0)),
            pl.BlockSpec((group, state_rows, lanes), lambda i, r: (i, 0, 0)),
        ],
    )
    return pl.pallas_call(
        functools.partial(recurrence_kernel, group=group, window=window, heads=heads),
        grid_spec=grid_spec,
        out_shape=[
            jax.ShapeDtypeStruct((slot_count, 2 * window, state_rows), jnp.float32),
            jax.ShapeDtypeStruct((slot_count, state_rows, lanes), jnp.bfloat16),
        ],
    )(rows, *([received] * group), mix, weight)

MESH = pl.DeviceIdType.MESH


def scatter_sum_kernel(x_ref, out_ref, slots, send_sem, recv_sem, *, n, rows):
    me = lax.axis_index("head")
    group = lax.axis_index("req")
    barrier = pltpu.get_barrier_semaphore()
    for k in range(1, n):
        pl.semaphore_signal(
            barrier, inc=1, device_id=(group, lax.rem(me + k, n)), device_id_type=MESH
        )
    pl.semaphore_wait(barrier, n - 1)
    copies = []
    for k in range(1, n):
        peer = lax.rem(me + k, n)
        start = pl.multiple_of(peer * rows, rows)
        copy = pltpu.make_async_remote_copy(
            src_ref=x_ref.at[pl.ds(start, rows)],
            dst_ref=slots.at[k - 1],
            send_sem=send_sem.at[k - 1],
            recv_sem=recv_sem.at[k - 1],
            device_id=(group, peer),
            device_id_type=MESH,
        )
        copy.start()
        copies.append(copy)
    own = pl.multiple_of(me * rows, rows)
    total = x_ref[pl.ds(own, rows)].astype(jnp.float32)
    for k, copy in enumerate(copies):
        copy.wait()
        total = total + slots[k].astype(jnp.float32)
    out_ref[...] = total


def scatter_sum(x, n):
    rows = x.shape[0] // n
    return pl.pallas_call(
        functools.partial(scatter_sum_kernel, n=n, rows=rows),
        out_shape=jax.ShapeDtypeStruct((rows, x.shape[1]), jnp.float32),
        in_specs=[pl.BlockSpec(memory_space=pltpu.VMEM)],
        out_specs=pl.BlockSpec(memory_space=pltpu.VMEM),
        scratch_shapes=[
            pltpu.VMEM((n - 1, rows, x.shape[1]), x.dtype),
            pltpu.SemaphoreType.DMA((n - 1,)),
            pltpu.SemaphoreType.DMA((n - 1,)),
        ],
        compiler_params=pltpu.CompilerParams(collective_id=0, has_side_effects=True),
    )(x)


def exchange_kernel(x_ref, out_ref, send_sem, recv_sem, local_sem, *, n):
    me = lax.axis_index("req")
    head = lax.axis_index("head")
    barrier = pltpu.get_barrier_semaphore()
    for k in range(1, n):
        pl.semaphore_signal(
            barrier, inc=1, device_id=(lax.rem(me + k, n), head), device_id_type=MESH
        )
    pl.semaphore_wait(barrier, n - 1)
    own = pltpu.make_async_copy(x_ref.at[me], out_ref.at[me], local_sem.at[0])
    own.start()
    copies = []
    for k in range(1, n):
        peer = lax.rem(me + k, n)
        copy = pltpu.make_async_remote_copy(
            src_ref=x_ref.at[peer],
            dst_ref=out_ref.at[me],
            send_sem=send_sem.at[k - 1],
            recv_sem=recv_sem.at[k - 1],
            device_id=(peer, head),
            device_id_type=MESH,
        )
        copy.start()
        copies.append(copy)
    own.wait()
    for copy in copies:
        copy.wait()


def exchange(x, tag):
    n = x.shape[0]
    return pl.pallas_call(
        functools.partial(exchange_kernel, n=n),
        out_shape=jax.ShapeDtypeStruct(x.shape, x.dtype),
        in_specs=[pl.BlockSpec(memory_space=pl.ANY)],
        out_specs=pl.BlockSpec(memory_space=pl.ANY),
        scratch_shapes=[
            pltpu.SemaphoreType.DMA((n - 1,)),
            pltpu.SemaphoreType.DMA((n - 1,)),
            pltpu.SemaphoreType.DMA((1,)),
        ],
        compiler_params=pltpu.CompilerParams(collective_id=tag, has_side_effects=True),
    )(x)


def exchange_pack_kernel(
    idx_ref, x_ref, states_ref, edges_ref, out_ref, send_ref, send_sem, recv_sem, local_sem, *, n
):
    me = lax.axis_index("req")
    head = lax.axis_index("head")
    barrier = pltpu.get_barrier_semaphore()
    for k in range(1, n):
        pl.semaphore_signal(
            barrier, inc=1, device_id=(lax.rem(me + k, n), head), device_id_type=MESH
        )
    pl.semaphore_wait(barrier, n - 1)
    own = pltpu.make_async_copy(x_ref.at[me], out_ref.at[me], local_sem.at[0])
    own.start()
    copies = []
    for k in range(1, n):
        peer = lax.rem(me + k, n)
        copy = pltpu.make_async_remote_copy(
            src_ref=x_ref.at[peer],
            dst_ref=out_ref.at[me],
            send_sem=send_sem.at[k - 1],
            recv_sem=recv_sem.at[k - 1],
            device_id=(peer, head),
            device_id_type=MESH,
        )
        copy.start()
        copies.append(copy)
    state_rows = states_ref.shape[1]
    for r in range(send_ref.shape[0]):
        row = idx_ref[r]
        send_ref[r, :state_rows] = states_ref[row]
        send_ref[r, state_rows:] = edges_ref[row]
    own.wait()
    for copy in copies:
        copy.wait()


def exchange_pack(x, idx, states_block, edges_block, tag):
    n = x.shape[0]
    slots, state_rows, lanes = states_block.shape
    return pl.pallas_call(
        functools.partial(exchange_pack_kernel, n=n),
        out_shape=[
            jax.ShapeDtypeStruct(x.shape, x.dtype),
            jax.ShapeDtypeStruct(
                (idx.shape[0], state_rows + edges_block.shape[1], lanes), states_block.dtype
            ),
        ],
        in_specs=[
            pl.BlockSpec(memory_space=pltpu.SMEM),
            pl.BlockSpec(memory_space=pl.ANY),
            pl.BlockSpec(memory_space=pltpu.VMEM),
            pl.BlockSpec(memory_space=pltpu.VMEM),
        ],
        out_specs=[
            pl.BlockSpec(memory_space=pl.ANY),
            pl.BlockSpec(memory_space=pltpu.VMEM),
        ],
        scratch_shapes=[
            pltpu.SemaphoreType.DMA((n - 1,)),
            pltpu.SemaphoreType.DMA((n - 1,)),
            pltpu.SemaphoreType.DMA((1,)),
        ],
        compiler_params=pltpu.CompilerParams(collective_id=tag, has_side_effects=True),
    )(idx, x, states_block, edges_block)


def migrate(item, mig_dest, slot_count, groups, device, pack):
    length = item.shape[0]
    lanes = 128
    piece = -(-length // (groups * lanes)) * lanes
    padded = jnp.pad(item, (0, piece * groups - length)).reshape(groups, piece // lanes, lanes)
    first, send_base = pack(padded)
    first = first.reshape(groups, piece)
    dest_dev = mig_dest // slot_count
    order = invert(dest_dev, groups)
    pick = (order[:, None] == jnp.arange(groups, dtype=jnp.int32)[None, :]).astype(first.dtype)
    routed = jnp.dot(pick, first, preferred_element_type=jnp.float32).astype(first.dtype)
    second = exchange(routed.reshape(groups, piece // lanes, lanes), 2)
    arrived = second.reshape(-1)[:length]
    target_local = jnp.sum(jnp.where(dest_dev == device, mig_dest, 0)) - device * slot_count
    return arrived, target_local, send_base


def local(
    tokens,
    pre_gain,
    inner_weight,
    shared_weight,
    conv_inner,
    conv_inner_bias,
    conv_shared,
    conv_shared_bias,
    step_bias,
    decay_log,
    skip_gain,
    gate_gain,
    out_weight,
    states,
    edge_inner,
    edge_shared,
    counts,
    mig_ids,
    mig_dest,
    reorder,
):
    slot_count, heads_here, head_dim, state_dim = states.shape
    inner_here = heads_here * head_dim
    lanes = state_dim
    groups = lax.axis_size("req")
    device = lax.axis_index("req")
    first_slot = device * slot_count
    stride = (slot_count + groups - 1) // groups
    all_slots = jnp.arange(slot_count * groups, dtype=jnp.int32)

    rows_in = tokens.astype(jnp.float32)
    normed = (
        rows_in * lax.rsqrt(jnp.mean(rows_in * rows_in, axis=-1, keepdims=True) + EPS) * pre_gain
    ).astype(jnp.bfloat16)
    inner_flat = inner_weight.reshape(inner_weight.shape[0], 2 * inner_here)
    piece_rows = lax.all_gather(normed, "head", axis=0, tiled=True)
    inner_rows = jnp.dot(piece_rows, inner_flat, preferred_element_type=jnp.float32).astype(
        jnp.bfloat16
    )
    shared_rows = jnp.dot(piece_rows, shared_weight, preferred_element_type=jnp.float32).astype(
        jnp.bfloat16
    )

    state_rows = heads_here * head_dim * state_dim // lanes
    inner_edge_rows = edge_inner.shape[1] * edge_inner.shape[2] // lanes
    shared_edge_rows = edge_shared.shape[1] * edge_shared.shape[2] // lanes
    state_block = states.reshape(slot_count, state_rows, lanes)
    edge_block = jnp.concatenate(
        [
            edge_inner.reshape(slot_count, inner_edge_rows, lanes),
            edge_shared.reshape(slot_count, shared_edge_rows, lanes),
        ],
        axis=1,
    )
    row_total = state_rows + edge_block.shape[1]
    send_rows, recv_rows = route_rows(reorder, first_slot, slot_count, all_slots, stride)
    buffer_rows = groups * stride
    send_idx = invert(send_rows, buffer_rows)

    moving = mig_ids.shape[0] // groups
    own_id = jnp.sum(jnp.where(jnp.arange(mig_ids.shape[0]) == device * moving, mig_ids, 0))
    mig_local = own_id - first_slot
    item = jnp.concatenate(
        [
            lax.dynamic_index_in_dim(part, mig_local, 0, keepdims=False).reshape(-1)
            for part in (states, edge_block)
        ]
    )
    arrived, target_local, send_base = migrate(
        item,
        mig_dest,
        slot_count,
        groups,
        device,
        lambda x: exchange_pack(x, send_idx, state_block, edge_block, 1),
    )
    arrived = arrived.reshape(row_total, lanes)

    target_row = jnp.sum(jnp.where(jnp.arange(slot_count) == target_local, send_rows, 0))
    send_buf = lax.dynamic_update_slice(send_base, arrived[None], (target_row, 0, 0))
    received = lax.all_to_all(send_buf, "req", 0, 0, tiled=True)
    moved = received[:, state_rows:][recv_rows]
    moved_inner = moved[:, :inner_edge_rows].reshape(edge_inner.shape)
    moved_shared = moved[:, inner_edge_rows:].reshape(edge_shared.shape)

    window = inner_rows.shape[0] // slot_count
    inner_rows = inner_rows.reshape(slot_count, window, 2 * inner_here)
    shared_rows = shared_rows.reshape(slot_count, window, shared_rows.shape[1])
    gate_part = inner_rows[:, :, :inner_here]
    value_part = inner_rows[:, :, inner_here:]
    fresh_shared = shared_rows[:, :, : 2 * state_dim]
    head_index = lax.axis_index("head")
    step_raw = lax.dynamic_slice_in_dim(
        shared_rows[:, :, 2 * state_dim :], head_index * heads_here, heads_here, axis=2
    )
    edge_inner_out = new_edge(moved_inner, value_part, counts)
    edge_shared_out = new_edge(moved_shared, fresh_shared, counts)
    mixed_inner = depthwise(moved_inner, value_part, conv_inner, conv_inner_bias)
    mixed_shared = depthwise(moved_shared, fresh_shared, conv_shared, conv_shared_bias)
    valid = jnp.arange(window)[None, :] < counts[:, None]
    step_size = jax.nn.softplus(step_raw.astype(jnp.float32) + step_bias)
    step_size = jnp.where(valid[:, :, None], step_size, 0.0)
    decay = -jnp.exp(decay_log)
    entries = mixed_shared[:, :, :state_dim]
    readouts = mixed_shared[:, :, state_dim:]

    factor = jnp.exp(step_size * decay)
    cum = [factor[:, 0]]
    for t in range(1, window):
        cum.append(cum[-1] * factor[:, t])
    span = {}
    for t in range(window):
        span[(t, t)] = jnp.ones_like(factor[:, 0])
        for s in range(t - 1, -1, -1):
            span[(t, s)] = span[(t, s + 1)] * factor[:, s + 1]

    last = window - 1
    overlap = jnp.einsum("rtn,rsn->rts", readouts, entries, precision=HIGH)
    names = (
        [("step", t) for t in range(window)]
        + [("push", s) for s in range(window)]
        + [("cum", t) for t in range(window)]
        + [("pair", t, s) for t in range(window) for s in range(t + 1)]
    )
    rows = []
    for name in names:
        if name[0] == "step":
            rows.append(step_size[:, name[1]])
        elif name[0] == "push":
            rows.append(span[(last, name[1])])
        elif name[0] == "cum":
            rows.append(cum[name[1]])
        else:
            rows.append(span[(name[1], name[2])] * overlap[:, name[1], name[2], None])
    wide = jnp.repeat(jnp.stack(rows, axis=1), head_dim, axis=-1)
    at = {name: k for k, name in enumerate(names)}

    flat_inputs = mixed_inner.reshape(slot_count, window, inner_here)
    weighted = jnp.stack(
        [wide[:, at[("step", t)]] * flat_inputs[:, t] for t in range(window)], axis=1
    )
    pushed = jnp.stack([wide[:, at[("push", s)]] * weighted[:, s] for s in range(window)], axis=1)
    weight = jnp.concatenate([pushed, jnp.zeros_like(pushed)], axis=1)
    carry = jnp.pad(cum[last], ((0, 0), (0, state_dim - heads_here)))[:, None, :]
    mix = jnp.concatenate(
        [readouts, entries, carry, jnp.zeros((slot_count, 2 * window - 1, state_dim), jnp.float32)],
        axis=1,
    )
    read, states_out = recurrence(received, recv_rows, mix, weight, state_rows, heads_here)
    states_out = states_out.reshape(states.shape)
    skip_wide = jnp.repeat(skip_gain, head_dim)
    produced = []
    for t in range(window):
        acc = wide[:, at[("cum", t)]] * read[:, t]
        for s in range(t + 1):
            acc = acc + wide[:, at[("pair", t, s)]] * weighted[:, s]
        produced.append(acc + skip_wide * flat_inputs[:, t])
    outputs = jnp.stack(produced, axis=1)

    gated = outputs * jax.nn.silu(gate_part.astype(jnp.float32))
    square_part = jnp.sum(gated * gated, axis=-1).reshape(slot_count * window, 1)
    pre_scaled = (
        jnp.where(valid[:, :, None], gated * gate_gain, 0.0)
        .astype(jnp.bfloat16)
        .reshape(slot_count * window, inner_here)
    )
    partial = jnp.dot(pre_scaled, out_weight, preferred_element_type=jnp.float32)
    square_hi = square_part.astype(jnp.bfloat16)
    square_lo = (square_part - square_hi.astype(jnp.float32)).astype(jnp.bfloat16)
    extra = jnp.pad(
        jnp.concatenate([square_hi, square_lo], axis=1), ((0, 0), (0, 126))
    )
    combined = jnp.concatenate([partial.astype(jnp.bfloat16), extra], axis=1)
    reduced = scatter_sum(combined, lax.axis_size("head"))
    full_inner = inner_here * lax.axis_size("head")
    width = partial.shape[1]
    square_sum = reduced[:, width : width + 1] + reduced[:, width + 1 : width + 2]
    scale = lax.rsqrt(square_sum / full_inner + EPS)
    hidden_out = (rows_in + reduced[:, :width] * scale).astype(jnp.bfloat16)
    return (hidden_out, states_out, edge_inner_out, edge_shared_out)


def solution(mesh):
    placed = (
        P(("req", "head"), None),
        P(),
        P(None, None, "head"),
        P(),
        P(None, "head"),
        P("head"),
        P(),
        P(),
        P("head"),
        P("head"),
        P("head"),
        P("head"),
        P("head", None),
        P("req", "head", None, None),
        P("req", None, "head"),
        P("req", None, None),
        P("req"),
        P(),
        P(),
        P(),
    )
    return jax.shard_map(
        local,
        mesh=mesh,
        in_specs=placed,
        out_specs=(
            P(("req", "head"), None),
            P("req", "head", None, None),
            P("req", None, "head"),
            P("req", None, None),
        ),
        check_vma=False,
    )
```

```python
import functools

import jax
import jax.numpy as jnp
from jax import lax
from jax.sharding import PartitionSpec as P
from jax.experimental import pallas as pl
from jax.experimental.pallas import tpu as pltpu

EPS = 1e-05
HIGH = lax.Precision.HIGHEST


def depthwise(edge, fresh, weight, offset_bias):
    sequence = jnp.concatenate([edge, fresh], axis=1).astype(jnp.float32)
    window = fresh.shape[1]
    summed = sequence[:, 0:window] * weight[0]
    for offset in range(1, weight.shape[0]):
        summed = summed + sequence[:, offset : offset + window] * weight[offset]
    return jax.nn.silu(summed + offset_bias)


def new_edge(edge, fresh, counts):
    sequence = jnp.concatenate([edge, fresh], axis=1)
    keep_rows = edge.shape[1]
    result = edge
    for length in range(1, fresh.shape[1] + 1):
        result = jnp.where(
            (counts == length)[:, None, None], sequence[:, length : length + keep_rows], result
        )
    return result


def rank_rows(partner, position, capacity):
    matching = partner[:, None] == partner[None, :]
    earlier = position[None, :] < position[:, None]
    ranking = jnp.sum(jnp.logical_and(matching, earlier), axis=1)
    return partner * capacity + ranking


def invert(values, size):
    hits = values[None, :] == jnp.arange(size, dtype=jnp.int32)[:, None]
    return jnp.sum(jnp.where(hits, jnp.arange(values.shape[0], dtype=jnp.int32)[None, :], 0), axis=1)


def route_rows(anchor, first_slot, slot_count, all_slots, capacity):
    mine = first_slot + jnp.arange(slot_count, dtype=jnp.int32)
    hits = anchor[None, :] == mine[:, None]
    targets = jnp.sum(jnp.where(hits, all_slots[None, :], 0), axis=1)
    send_rows = rank_rows(targets // slot_count, targets % slot_count, capacity)
    sources = lax.dynamic_slice_in_dim(anchor, first_slot, slot_count)
    recv_rows = rank_rows(sources // slot_count, jnp.arange(slot_count, dtype=jnp.int32), capacity)
    return (send_rows, recv_rows)


def recurrence_kernel(rows_ref, *refs, group, window, heads):
    held_refs = refs[:group]
    mix_ref, weight_ref, read_ref, out_ref = refs[group:]
    nt = (((1,), (1,)), ((), ()))
    tn = (((0,), (0,)), ((), ()))
    for q in range(group):
        held_low = held_refs[q][0]
        mix = mix_ref[q]
        read = None
        rest = mix[: 2 * window]
        for _ in range(3):
            part = rest.astype(jnp.bfloat16)
            rest = rest - part.astype(jnp.float32)
            term = lax.dot_general(part, held_low, nt, preferred_element_type=jnp.float32)
            read = term if read is None else read + term
        read_ref[q] = read
        weight = weight_ref[q]
        entry = mix[window : 3 * window]
        w_hi = weight.astype(jnp.bfloat16)
        w_lo = (weight - w_hi.astype(jnp.float32)).astype(jnp.bfloat16)
        e_hi = entry.astype(jnp.bfloat16)
        e_lo = (entry - e_hi.astype(jnp.float32)).astype(jnp.bfloat16)
        pushed = (
            lax.dot_general(w_hi, e_hi, tn, preferred_element_type=jnp.float32)
            + lax.dot_general(w_hi, e_lo, tn, preferred_element_type=jnp.float32)
            + lax.dot_general(w_lo, e_hi, tn, preferred_element_type=jnp.float32)
        )
        held = held_low.astype(jnp.float32)
        rows = held.shape[0] // heads
        carry = mix[2 * window : 2 * window + 1]
        for h in range(heads):
            part = slice(h * rows, (h + 1) * rows)
            out_ref[q, part] = (carry[:, h : h + 1] * held[part] + pushed[part]).astype(
                out_ref.dtype
            )


def recurrence(received, rows, mix, weight, state_rows, heads, group=16):
    slot_count, _, lanes = received.shape
    window = mix.shape[1] // 4
    held_specs = [
        pl.BlockSpec((1, state_rows, lanes), lambda i, r, q=q: (r[i * group + q], 0, 0))
        for q in range(group)
    ]
    grid_spec = pltpu.PrefetchScalarGridSpec(
        num_scalar_prefetch=1,
        grid=(slot_count // group,),
        in_specs=held_specs
        + [
            pl.BlockSpec((group, 4 * window, lanes), lambda i, r: (i, 0, 0)),
            pl.BlockSpec((group, 2 * window, state_rows), lambda i, r: (i, 0, 0)),
        ],
        out_specs=[
            pl.BlockSpec((group, 2 * window, state_rows), lambda i, r: (i, 0, 0)),
            pl.BlockSpec((group, state_rows, lanes), lambda i, r: (i, 0, 0)),
        ],
    )
    return pl.pallas_call(
        functools.partial(recurrence_kernel, group=group, window=window, heads=heads),
        grid_spec=grid_spec,
        out_shape=[
            jax.ShapeDtypeStruct((slot_count, 2 * window, state_rows), jnp.float32),
            jax.ShapeDtypeStruct((slot_count, state_rows, lanes), jnp.bfloat16),
        ],
    )(rows, *([received] * group), mix, weight)

MESH = pl.DeviceIdType.MESH


def scatter_sum_kernel(x_ref, out_ref, slots, send_sem, recv_sem, *, n, rows):
    me = lax.axis_index("head")
    group = lax.axis_index("req")
    barrier = pltpu.get_barrier_semaphore()
    for k in range(1, n):
        pl.semaphore_signal(
            barrier, inc=1, device_id=(group, lax.rem(me + k, n)), device_id_type=MESH
        )
    pl.semaphore_wait(barrier, n - 1)
    copies = []
    for k in range(1, n):
        peer = lax.rem(me + k, n)
        start = pl.multiple_of(peer * rows, rows)
        copy = pltpu.make_async_remote_copy(
            src_ref=x_ref.at[pl.ds(start, rows)],
            dst_ref=slots.at[k - 1],
            send_sem=send_sem.at[k - 1],
            recv_sem=recv_sem.at[k - 1],
            device_id=(group, peer),
            device_id_type=MESH,
        )
        copy.start()
        copies.append(copy)
    own = pl.multiple_of(me * rows, rows)
    total = x_ref[pl.ds(own, rows)].astype(jnp.float32)
    for k, copy in enumerate(copies):
        copy.wait()
        total = total + slots[k].astype(jnp.float32)
    out_ref[...] = total


def scatter_sum(x, n):
    rows = x.shape[0] // n
    return pl.pallas_call(
        functools.partial(scatter_sum_kernel, n=n, rows=rows),
        out_shape=jax.ShapeDtypeStruct((rows, x.shape[1]), jnp.float32),
        in_specs=[pl.BlockSpec(memory_space=pltpu.VMEM)],
        out_specs=pl.BlockSpec(memory_space=pltpu.VMEM),
        scratch_shapes=[
            pltpu.VMEM((n - 1, rows, x.shape[1]), x.dtype),
            pltpu.SemaphoreType.DMA((n - 1,)),
            pltpu.SemaphoreType.DMA((n - 1,)),
        ],
        compiler_params=pltpu.CompilerParams(collective_id=0, has_side_effects=True),
    )(x)


def exchange_kernel(x_ref, out_ref, send_sem, recv_sem, local_sem, *, n):
    me = lax.axis_index("req")
    head = lax.axis_index("head")
    barrier = pltpu.get_barrier_semaphore()
    for k in range(1, n):
        pl.semaphore_signal(
            barrier, inc=1, device_id=(lax.rem(me + k, n), head), device_id_type=MESH
        )
    pl.semaphore_wait(barrier, n - 1)
    own = pltpu.make_async_copy(x_ref.at[me], out_ref.at[me], local_sem.at[0])
    own.start()
    copies = []
    for k in range(1, n):
        peer = lax.rem(me + k, n)
        copy = pltpu.make_async_remote_copy(
            src_ref=x_ref.at[peer],
            dst_ref=out_ref.at[me],
            send_sem=send_sem.at[k - 1],
            recv_sem=recv_sem.at[k - 1],
            device_id=(peer, head),
            device_id_type=MESH,
        )
        copy.start()
        copies.append(copy)
    own.wait()
    for copy in copies:
        copy.wait()


def exchange(x, tag):
    n = x.shape[0]
    return pl.pallas_call(
        functools.partial(exchange_kernel, n=n),
        out_shape=jax.ShapeDtypeStruct(x.shape, x.dtype),
        in_specs=[pl.BlockSpec(memory_space=pl.ANY)],
        out_specs=pl.BlockSpec(memory_space=pl.ANY),
        scratch_shapes=[
            pltpu.SemaphoreType.DMA((n - 1,)),
            pltpu.SemaphoreType.DMA((n - 1,)),
            pltpu.SemaphoreType.DMA((1,)),
        ],
        compiler_params=pltpu.CompilerParams(collective_id=tag, has_side_effects=True),
    )(x)


def exchange_pack_kernel(
    idx_ref, x_ref, states_ref, edges_ref, out_ref, send_ref, send_sem, recv_sem, local_sem, *, n
):
    me = lax.axis_index("req")
    head = lax.axis_index("head")
    barrier = pltpu.get_barrier_semaphore()
    for k in range(1, n):
        pl.semaphore_signal(
            barrier, inc=1, device_id=(lax.rem(me + k, n), head), device_id_type=MESH
        )
    pl.semaphore_wait(barrier, n - 1)
    own = pltpu.make_async_copy(x_ref.at[me], out_ref.at[me], local_sem.at[0])
    own.start()
    copies = []
    for k in range(1, n):
        peer = lax.rem(me + k, n)
        copy = pltpu.make_async_remote_copy(
            src_ref=x_ref.at[peer],
            dst_ref=out_ref.at[me],
            send_sem=send_sem.at[k - 1],
            recv_sem=recv_sem.at[k - 1],
            device_id=(peer, head),
            device_id_type=MESH,
        )
        copy.start()
        copies.append(copy)
    state_rows = states_ref.shape[1]
    for r in range(send_ref.shape[0]):
        row = idx_ref[r]
        send_ref[r, :state_rows] = states_ref[row]
        send_ref[r, state_rows:] = edges_ref[row]
    own.wait()
    for copy in copies:
        copy.wait()


def exchange_pack(x, idx, states_block, edges_block, tag):
    n = x.shape[0]
    slots, state_rows, lanes = states_block.shape
    return pl.pallas_call(
        functools.partial(exchange_pack_kernel, n=n),
        out_shape=[
            jax.ShapeDtypeStruct(x.shape, x.dtype),
            jax.ShapeDtypeStruct(
                (idx.shape[0], state_rows + edges_block.shape[1], lanes), states_block.dtype
            ),
        ],
        in_specs=[
            pl.BlockSpec(memory_space=pltpu.SMEM),
            pl.BlockSpec(memory_space=pl.ANY),
            pl.BlockSpec(memory_space=pltpu.VMEM),
            pl.BlockSpec(memory_space=pltpu.VMEM),
        ],
        out_specs=[
            pl.BlockSpec(memory_space=pl.ANY),
            pl.BlockSpec(memory_space=pltpu.VMEM),
        ],
        scratch_shapes=[
            pltpu.SemaphoreType.DMA((n - 1,)),
            pltpu.SemaphoreType.DMA((n - 1,)),
            pltpu.SemaphoreType.DMA((1,)),
        ],
        compiler_params=pltpu.CompilerParams(collective_id=tag, has_side_effects=True),
    )(idx, x, states_block, edges_block)


def migrate(item, mig_dest, slot_count, groups, device, pack):
    length = item.shape[0]
    lanes = 128
    piece = -(-length // (groups * lanes)) * lanes
    padded = jnp.pad(item, (0, piece * groups - length)).reshape(groups, piece // lanes, lanes)
    first, send_base = pack(padded)
    first = first.reshape(groups, piece)
    dest_dev = mig_dest // slot_count
    order = invert(dest_dev, groups)
    pick = (order[:, None] == jnp.arange(groups, dtype=jnp.int32)[None, :]).astype(first.dtype)
    routed = jnp.dot(pick, first, preferred_element_type=jnp.float32).astype(first.dtype)
    second = exchange(routed.reshape(groups, piece // lanes, lanes), 2)
    arrived = second.reshape(-1)[:length]
    target_local = jnp.sum(jnp.where(dest_dev == device, mig_dest, 0)) - device * slot_count
    return arrived, target_local, send_base


def local(
    tokens,
    pre_gain,
    inner_weight,
    shared_weight,
    conv_inner,
    conv_inner_bias,
    conv_shared,
    conv_shared_bias,
    step_bias,
    decay_log,
    skip_gain,
    gate_gain,
    out_weight,
    states,
    edge_inner,
    edge_shared,
    counts,
    mig_ids,
    mig_dest,
    reorder,
):
    slot_count, heads_here, head_dim, state_dim = states.shape
    inner_here = heads_here * head_dim
    lanes = state_dim
    groups = lax.axis_size("req")
    device = lax.axis_index("req")
    first_slot = device * slot_count
    stride = (slot_count + groups - 1) // groups
    all_slots = jnp.arange(slot_count * groups, dtype=jnp.int32)

    rows_in = tokens.astype(jnp.float32)
    normed = (
        rows_in * lax.rsqrt(jnp.mean(rows_in * rows_in, axis=-1, keepdims=True) + EPS) * pre_gain
    ).astype(jnp.bfloat16)
    inner_flat = inner_weight.reshape(inner_weight.shape[0], 2 * inner_here)
    piece_rows = lax.all_gather(normed, "head", axis=0, tiled=True)
    inner_rows = jnp.dot(piece_rows, inner_flat, preferred_element_type=jnp.float32).astype(
        jnp.bfloat16
    )
    shared_rows = jnp.dot(piece_rows, shared_weight, preferred_element_type=jnp.float32).astype(
        jnp.bfloat16
    )

    state_rows = heads_here * head_dim * state_dim // lanes
    inner_edge_rows = edge_inner.shape[1] * edge_inner.shape[2] // lanes
    shared_edge_rows = edge_shared.shape[1] * edge_shared.shape[2] // lanes
    state_block = states.reshape(slot_count, state_rows, lanes)
    edge_block = jnp.concatenate(
        [
            edge_inner.reshape(slot_count, inner_edge_rows, lanes),
            edge_shared.reshape(slot_count, shared_edge_rows, lanes),
        ],
        axis=1,
    )
    row_total = state_rows + edge_block.shape[1]
    send_rows, recv_rows = route_rows(reorder, first_slot, slot_count, all_slots, stride)
    buffer_rows = groups * stride
    send_idx = invert(send_rows, buffer_rows)

    moving = mig_ids.shape[0] // groups
    own_id = jnp.sum(jnp.where(jnp.arange(mig_ids.shape[0]) == device * moving, mig_ids, 0))
    mig_local = own_id - first_slot
    item = jnp.concatenate(
        [
            lax.dynamic_index_in_dim(part, mig_local, 0, keepdims=False).reshape(-1)
            for part in (states, edge_block)
        ]
    )
    arrived, target_local, send_base = migrate(
        item,
        mig_dest,
        slot_count,
        groups,
        device,
        lambda x: exchange_pack(x, send_idx, state_block, edge_block, 1),
    )
    arrived = arrived.reshape(row_total, lanes)

    target_row = jnp.sum(jnp.where(jnp.arange(slot_count) == target_local, send_rows, 0))
    send_buf = lax.dynamic_update_slice(send_base, arrived[None], (target_row, 0, 0))
    received = lax.all_to_all(send_buf, "req", 0, 0, tiled=True)
    moved = received[:, state_rows:][recv_rows]
    moved_inner = moved[:, :inner_edge_rows].reshape(edge_inner.shape)
    moved_shared = moved[:, inner_edge_rows:].reshape(edge_shared.shape)

    window = inner_rows.shape[0] // slot_count
    inner_rows = inner_rows.reshape(slot_count, window, 2 * inner_here)
    shared_rows = shared_rows.reshape(slot_count, window, shared_rows.shape[1])
    gate_part = inner_rows[:, :, :inner_here]
    value_part = inner_rows[:, :, inner_here:]
    fresh_shared = shared_rows[:, :, : 2 * state_dim]
    head_index = lax.axis_index("head")
    step_raw = lax.dynamic_slice_in_dim(
        shared_rows[:, :, 2 * state_dim :], head_index * heads_here, heads_here, axis=2
    )
    edge_inner_out = new_edge(moved_inner, value_part, counts)
    edge_shared_out = new_edge(moved_shared, fresh_shared, counts)
    mixed_inner = depthwise(moved_inner, value_part, conv_inner, conv_inner_bias)
    mixed_shared = depthwise(moved_shared, fresh_shared, conv_shared, conv_shared_bias)
    valid = jnp.arange(window)[None, :] < counts[:, None]
    step_size = jax.nn.softplus(step_raw.astype(jnp.float32) + step_bias)
    step_size = jnp.where(valid[:, :, None], step_size, 0.0)
    decay = -jnp.exp(decay_log)
    entries = mixed_shared[:, :, :state_dim]
    readouts = mixed_shared[:, :, state_dim:]

    factor = jnp.exp(step_size * decay)
    cum = [factor[:, 0]]
    for t in range(1, window):
        cum.append(cum[-1] * factor[:, t])
    span = {}
    for t in range(window):
        span[(t, t)] = jnp.ones_like(factor[:, 0])
        for s in range(t - 1, -1, -1):
            span[(t, s)] = span[(t, s + 1)] * factor[:, s + 1]

    def per_head(v):
        return jnp.repeat(v, head_dim, axis=-1)

    flat_inputs = mixed_inner.reshape(slot_count, window, inner_here)
    weighted = per_head(step_size) * flat_inputs
    last = window - 1
    pushed = jnp.stack([per_head(span[(last, s)]) * weighted[:, s] for s in range(window)], axis=1)
    weight = jnp.concatenate([pushed, jnp.zeros_like(pushed)], axis=1)
    carry = jnp.pad(cum[last], ((0, 0), (0, state_dim - heads_here)))[:, None, :]
    mix = jnp.concatenate(
        [readouts, entries, carry, jnp.zeros((slot_count, 2 * window - 1, state_dim), jnp.float32)],
        axis=1,
    )
    read, states_out = recurrence(received, recv_rows, mix, weight, state_rows, heads_here)
    states_out = states_out.reshape(states.shape)
    overlap = jnp.einsum("rtn,rsn->rts", readouts, entries, precision=HIGH)
    skip_wide = jnp.repeat(skip_gain, head_dim)
    produced = []
    for t in range(window):
        acc = per_head(cum[t]) * read[:, t]
        for s in range(t + 1):
            acc = acc + per_head(span[(t, s)] * overlap[:, t, s, None]) * weighted[:, s]
        produced.append(acc + skip_wide * flat_inputs[:, t])
    outputs = jnp.stack(produced, axis=1)

    gated = outputs * jax.nn.silu(gate_part.astype(jnp.float32))
    square_part = jnp.sum(gated * gated, axis=-1).reshape(slot_count * window, 1)
    pre_scaled = (
        jnp.where(valid[:, :, None], gated * gate_gain, 0.0)
        .astype(jnp.bfloat16)
        .reshape(slot_count * window, inner_here)
    )
    partial = jnp.dot(pre_scaled, out_weight, preferred_element_type=jnp.float32)
    square_hi = square_part.astype(jnp.bfloat16)
    square_lo = (square_part - square_hi.astype(jnp.float32)).astype(jnp.bfloat16)
    extra = jnp.pad(
        jnp.concatenate([square_hi, square_lo], axis=1), ((0, 0), (0, 126))
    )
    combined = jnp.concatenate([partial.astype(jnp.bfloat16), extra], axis=1)
    reduced = scatter_sum(combined, lax.axis_size("head"))
    full_inner = inner_here * lax.axis_size("head")
    width = partial.shape[1]
    square_sum = reduced[:, width : width + 1] + reduced[:, width + 1 : width + 2]
    scale = lax.rsqrt(square_sum / full_inner + EPS)
    hidden_out = (rows_in + reduced[:, :width] * scale).astype(jnp.bfloat16)
    return (hidden_out, states_out, edge_inner_out, edge_shared_out)


def solution(mesh):
    placed = (
        P(("req", "head"), None),
        P(),
        P(None, None, "head"),
        P(),
        P(None, "head"),
        P("head"),
        P(),
        P(),
        P("head"),
        P("head"),
        P("head"),
        P("head"),
        P("head", None),
        P("req", "head", None, None),
        P("req", None, "head"),
        P("req", None, None),
        P("req"),
        P(),
        P(),
        P(),
    )
    return jax.shard_map(
        local,
        mesh=mesh,
        in_specs=placed,
        out_specs=(
            P(("req", "head"), None),
            P("req", "head", None, None),
            P("req", None, "head"),
            P("req", None, None),
        ),
        check_vma=False,
    )
```

```python
import functools

import jax
import jax.numpy as jnp
from jax import lax
from jax.sharding import PartitionSpec as P
from jax.experimental import pallas as pl
from jax.experimental.pallas import tpu as pltpu

EPS = 1e-05
HIGH = lax.Precision.HIGHEST


def depthwise(edge, fresh, weight, offset_bias):
    sequence = jnp.concatenate([edge, fresh], axis=1).astype(jnp.float32)
    window = fresh.shape[1]
    summed = sequence[:, 0:window] * weight[0]
    for offset in range(1, weight.shape[0]):
        summed = summed + sequence[:, offset : offset + window] * weight[offset]
    return jax.nn.silu(summed + offset_bias)


def new_edge(edge, fresh, counts):
    sequence = jnp.concatenate([edge, fresh], axis=1)
    keep_rows = edge.shape[1]
    result = edge
    for length in range(1, fresh.shape[1] + 1):
        result = jnp.where(
            (counts == length)[:, None, None], sequence[:, length : length + keep_rows], result
        )
    return result


def rank_rows(partner, position, capacity):
    matching = partner[:, None] == partner[None, :]
    earlier = position[None, :] < position[:, None]
    ranking = jnp.sum(jnp.logical_and(matching, earlier), axis=1)
    return partner * capacity + ranking


def invert(values, size):
    hits = values[None, :] == jnp.arange(size, dtype=jnp.int32)[:, None]
    return jnp.sum(jnp.where(hits, jnp.arange(values.shape[0], dtype=jnp.int32)[None, :], 0), axis=1)


def route_rows(anchor, first_slot, slot_count, all_slots, capacity):
    mine = first_slot + jnp.arange(slot_count, dtype=jnp.int32)
    hits = anchor[None, :] == mine[:, None]
    targets = jnp.sum(jnp.where(hits, all_slots[None, :], 0), axis=1)
    send_rows = rank_rows(targets // slot_count, targets % slot_count, capacity)
    sources = lax.dynamic_slice_in_dim(anchor, first_slot, slot_count)
    recv_rows = rank_rows(sources // slot_count, jnp.arange(slot_count, dtype=jnp.int32), capacity)
    return (send_rows, recv_rows)


def recurrence_kernel(rows_ref, *refs, group, window, heads):
    held_refs = refs[:group]
    mix_ref, weight_ref, read_ref, out_ref = refs[group:]
    nt = (((1,), (1,)), ((), ()))
    tn = (((0,), (0,)), ((), ()))
    for q in range(group):
        held_low = held_refs[q][0]
        mix = mix_ref[q]
        read = None
        rest = mix[: 2 * window]
        for _ in range(3):
            part = rest.astype(jnp.bfloat16)
            rest = rest - part.astype(jnp.float32)
            term = lax.dot_general(part, held_low, nt, preferred_element_type=jnp.float32)
            read = term if read is None else read + term
        read_ref[q] = read
        weight = weight_ref[q]
        entry = mix[window : 3 * window]
        w_hi = weight.astype(jnp.bfloat16)
        w_lo = (weight - w_hi.astype(jnp.float32)).astype(jnp.bfloat16)
        e_hi = entry.astype(jnp.bfloat16)
        e_lo = (entry - e_hi.astype(jnp.float32)).astype(jnp.bfloat16)
        pushed = (
            lax.dot_general(w_hi, e_hi, tn, preferred_element_type=jnp.float32)
            + lax.dot_general(w_hi, e_lo, tn, preferred_element_type=jnp.float32)
            + lax.dot_general(w_lo, e_hi, tn, preferred_element_type=jnp.float32)
        )
        held = held_low.astype(jnp.float32)
        rows = held.shape[0] // heads
        carry = mix[2 * window : 2 * window + 1]
        for h in range(heads):
            part = slice(h * rows, (h + 1) * rows)
            out_ref[q, part] = (carry[:, h : h + 1] * held[part] + pushed[part]).astype(
                out_ref.dtype
            )


def recurrence(received, rows, mix, weight, state_rows, heads, group=8):
    slot_count, _, lanes = received.shape
    window = mix.shape[1] // 4
    held_specs = [
        pl.BlockSpec((1, state_rows, lanes), lambda i, r, q=q: (r[i * group + q], 0, 0))
        for q in range(group)
    ]
    grid_spec = pltpu.PrefetchScalarGridSpec(
        num_scalar_prefetch=1,
        grid=(slot_count // group,),
        in_specs=held_specs
        + [
            pl.BlockSpec((group, 4 * window, lanes), lambda i, r: (i, 0, 0)),
            pl.BlockSpec((group, 2 * window, state_rows), lambda i, r: (i, 0, 0)),
        ],
        out_specs=[
            pl.BlockSpec((group, 2 * window, state_rows), lambda i, r: (i, 0, 0)),
            pl.BlockSpec((group, state_rows, lanes), lambda i, r: (i, 0, 0)),
        ],
    )
    return pl.pallas_call(
        functools.partial(recurrence_kernel, group=group, window=window, heads=heads),
        grid_spec=grid_spec,
        out_shape=[
            jax.ShapeDtypeStruct((slot_count, 2 * window, state_rows), jnp.float32),
            jax.ShapeDtypeStruct((slot_count, state_rows, lanes), jnp.bfloat16),
        ],
    )(rows, *([received] * group), mix, weight)

MESH = pl.DeviceIdType.MESH


def scatter_sum_kernel(*refs, n, rows, parts):
    x_refs = refs[:parts]
    out_refs = refs[parts : 2 * parts]
    slots = refs[2 * parts : 3 * parts]
    send_sem, recv_sem = refs[3 * parts :]
    me = lax.axis_index("head")
    group = lax.axis_index("req")
    barrier = pltpu.get_barrier_semaphore()
    for k in range(1, n):
        pl.semaphore_signal(
            barrier, inc=1, device_id=(group, lax.rem(me + k, n)), device_id_type=MESH
        )
    pl.semaphore_wait(barrier, n - 1)
    copies = []
    for k in range(1, n):
        peer = lax.rem(me + k, n)
        start = pl.multiple_of(peer * rows, rows)
        for p in range(parts):
            copy = pltpu.make_async_remote_copy(
                src_ref=x_refs[p].at[pl.ds(start, rows)],
                dst_ref=slots[p].at[k - 1],
                send_sem=send_sem.at[p, k - 1],
                recv_sem=recv_sem.at[p, k - 1],
                device_id=(group, peer),
                device_id_type=MESH,
            )
            copy.start()
            copies.append((p, k, copy))
    own = pl.multiple_of(me * rows, rows)
    totals = [x_refs[p][pl.ds(own, rows)].astype(jnp.float32) for p in range(parts)]
    for p, k, copy in copies:
        copy.wait()
        totals[p] = totals[p] + slots[p][k - 1].astype(jnp.float32)
    for p in range(parts):
        out_refs[p][...] = totals[p]


def scatter_sum(xs, n):
    rows = xs[0].shape[0] // n
    parts = len(xs)
    return pl.pallas_call(
        functools.partial(scatter_sum_kernel, n=n, rows=rows, parts=parts),
        out_shape=[jax.ShapeDtypeStruct((rows, x.shape[1]), jnp.float32) for x in xs],
        in_specs=[pl.BlockSpec(memory_space=pltpu.VMEM)] * parts,
        out_specs=[pl.BlockSpec(memory_space=pltpu.VMEM)] * parts,
        scratch_shapes=[pltpu.VMEM((n - 1, rows, x.shape[1]), x.dtype) for x in xs]
        + [
            pltpu.SemaphoreType.DMA((parts, n - 1)),
            pltpu.SemaphoreType.DMA((parts, n - 1)),
        ],
        compiler_params=pltpu.CompilerParams(collective_id=0, has_side_effects=True),
    )(*xs)


def exchange_kernel(x_ref, out_ref, send_sem, recv_sem, local_sem, *, n):
    me = lax.axis_index("req")
    head = lax.axis_index("head")
    barrier = pltpu.get_barrier_semaphore()
    for k in range(1, n):
        pl.semaphore_signal(
            barrier, inc=1, device_id=(lax.rem(me + k, n), head), device_id_type=MESH
        )
    pl.semaphore_wait(barrier, n - 1)
    own = pltpu.make_async_copy(x_ref.at[me], out_ref.at[me], local_sem.at[0])
    own.start()
    copies = []
    for k in range(1, n):
        peer = lax.rem(me + k, n)
        copy = pltpu.make_async_remote_copy(
            src_ref=x_ref.at[peer],
            dst_ref=out_ref.at[me],
            send_sem=send_sem.at[k - 1],
            recv_sem=recv_sem.at[k - 1],
            device_id=(peer, head),
            device_id_type=MESH,
        )
        copy.start()
        copies.append(copy)
    own.wait()
    for copy in copies:
        copy.wait()


def exchange(x, tag):
    n = x.shape[0]
    return pl.pallas_call(
        functools.partial(exchange_kernel, n=n),
        out_shape=jax.ShapeDtypeStruct(x.shape, x.dtype),
        in_specs=[pl.BlockSpec(memory_space=pl.ANY)],
        out_specs=pl.BlockSpec(memory_space=pl.ANY),
        scratch_shapes=[
            pltpu.SemaphoreType.DMA((n - 1,)),
            pltpu.SemaphoreType.DMA((n - 1,)),
            pltpu.SemaphoreType.DMA((1,)),
        ],
        compiler_params=pltpu.CompilerParams(collective_id=tag, has_side_effects=True),
    )(x)


def exchange_pack_kernel(
    idx_ref, x_ref, states_ref, edges_ref, out_ref, send_ref, send_sem, recv_sem, local_sem, *, n
):
    me = lax.axis_index("req")
    head = lax.axis_index("head")
    barrier = pltpu.get_barrier_semaphore()
    for k in range(1, n):
        pl.semaphore_signal(
            barrier, inc=1, device_id=(lax.rem(me + k, n), head), device_id_type=MESH
        )
    pl.semaphore_wait(barrier, n - 1)
    own = pltpu.make_async_copy(x_ref.at[me], out_ref.at[me], local_sem.at[0])
    own.start()
    copies = []
    for k in range(1, n):
        peer = lax.rem(me + k, n)
        copy = pltpu.make_async_remote_copy(
            src_ref=x_ref.at[peer],
            dst_ref=out_ref.at[me],
            send_sem=send_sem.at[k - 1],
            recv_sem=recv_sem.at[k - 1],
            device_id=(peer, head),
            device_id_type=MESH,
        )
        copy.start()
        copies.append(copy)
    state_rows = states_ref.shape[1]
    for r in range(send_ref.shape[0]):
        row = idx_ref[r]
        send_ref[r, :state_rows] = states_ref[row]
        send_ref[r, state_rows:] = edges_ref[row]
    own.wait()
    for copy in copies:
        copy.wait()


def exchange_pack(x, idx, states_block, edges_block, tag):
    n = x.shape[0]
    slots, state_rows, lanes = states_block.shape
    return pl.pallas_call(
        functools.partial(exchange_pack_kernel, n=n),
        out_shape=[
            jax.ShapeDtypeStruct(x.shape, x.dtype),
            jax.ShapeDtypeStruct(
                (idx.shape[0], state_rows + edges_block.shape[1], lanes), states_block.dtype
            ),
        ],
        in_specs=[
            pl.BlockSpec(memory_space=pltpu.SMEM),
            pl.BlockSpec(memory_space=pl.ANY),
            pl.BlockSpec(memory_space=pltpu.VMEM),
            pl.BlockSpec(memory_space=pltpu.VMEM),
        ],
        out_specs=[
            pl.BlockSpec(memory_space=pl.ANY),
            pl.BlockSpec(memory_space=pltpu.VMEM),
        ],
        scratch_shapes=[
            pltpu.SemaphoreType.DMA((n - 1,)),
            pltpu.SemaphoreType.DMA((n - 1,)),
            pltpu.SemaphoreType.DMA((1,)),
        ],
        compiler_params=pltpu.CompilerParams(collective_id=tag, has_side_effects=True),
    )(idx, x, states_block, edges_block)


def migrate(item, mig_dest, slot_count, groups, device, pack):
    length = item.shape[0]
    lanes = 128
    piece = -(-length // (groups * lanes)) * lanes
    padded = jnp.pad(item, (0, piece * groups - length)).reshape(groups, piece // lanes, lanes)
    first, send_base = pack(padded)
    first = first.reshape(groups, piece)
    dest_dev = mig_dest // slot_count
    order = invert(dest_dev, groups)
    pick = (order[:, None] == jnp.arange(groups, dtype=jnp.int32)[None, :]).astype(first.dtype)
    routed = jnp.dot(pick, first, preferred_element_type=jnp.float32).astype(first.dtype)
    second = exchange(routed.reshape(groups, piece // lanes, lanes), 2)
    arrived = second.reshape(-1)[:length]
    target_local = jnp.sum(jnp.where(dest_dev == device, mig_dest, 0)) - device * slot_count
    return arrived, target_local, send_base


def local(
    tokens,
    pre_gain,
    inner_weight,
    shared_weight,
    conv_inner,
    conv_inner_bias,
    conv_shared,
    conv_shared_bias,
    step_bias,
    decay_log,
    skip_gain,
    gate_gain,
    out_weight,
    states,
    edge_inner,
    edge_shared,
    counts,
    mig_ids,
    mig_dest,
    reorder,
):
    slot_count, heads_here, head_dim, state_dim = states.shape
    inner_here = heads_here * head_dim
    lanes = state_dim
    groups = lax.axis_size("req")
    device = lax.axis_index("req")
    first_slot = device * slot_count
    stride = (slot_count + groups - 1) // groups
    all_slots = jnp.arange(slot_count * groups, dtype=jnp.int32)

    rows_in = tokens.astype(jnp.float32)
    normed = (
        rows_in * lax.rsqrt(jnp.mean(rows_in * rows_in, axis=-1, keepdims=True) + EPS) * pre_gain
    ).astype(jnp.bfloat16)
    inner_flat = inner_weight.reshape(inner_weight.shape[0], 2 * inner_here)
    piece_rows = lax.all_gather(normed, "head", axis=0, tiled=True)
    inner_rows = jnp.dot(piece_rows, inner_flat, preferred_element_type=jnp.float32).astype(
        jnp.bfloat16
    )
    shared_rows = jnp.dot(piece_rows, shared_weight, preferred_element_type=jnp.float32).astype(
        jnp.bfloat16
    )

    state_rows = heads_here * head_dim * state_dim // lanes
    inner_edge_rows = edge_inner.shape[1] * edge_inner.shape[2] // lanes
    shared_edge_rows = edge_shared.shape[1] * edge_shared.shape[2] // lanes
    state_block = states.reshape(slot_count, state_rows, lanes)
    edge_block = jnp.concatenate(
        [
            edge_inner.reshape(slot_count, inner_edge_rows, lanes),
            edge_shared.reshape(slot_count, shared_edge_rows, lanes),
        ],
        axis=1,
    )
    row_total = state_rows + edge_block.shape[1]
    send_rows, recv_rows = route_rows(reorder, first_slot, slot_count, all_slots, stride)
    buffer_rows = groups * stride
    send_idx = invert(send_rows, buffer_rows)

    moving = mig_ids.shape[0] // groups
    own_id = jnp.sum(jnp.where(jnp.arange(mig_ids.shape[0]) == device * moving, mig_ids, 0))
    mig_local = own_id - first_slot
    item = jnp.concatenate(
        [
            lax.dynamic_index_in_dim(part, mig_local, 0, keepdims=False).reshape(-1)
            for part in (states, edge_block)
        ]
    )
    arrived, target_local, send_base = migrate(
        item,
        mig_dest,
        slot_count,
        groups,
        device,
        lambda x: exchange_pack(x, send_idx, state_block, edge_block, 1),
    )
    arrived = arrived.reshape(row_total, lanes)

    target_row = jnp.sum(jnp.where(jnp.arange(slot_count) == target_local, send_rows, 0))
    send_buf = lax.dynamic_update_slice(send_base, arrived[None], (target_row, 0, 0))
    received = lax.all_to_all(send_buf, "req", 0, 0, tiled=True)
    moved = received[:, state_rows:][recv_rows]
    moved_inner = moved[:, :inner_edge_rows].reshape(edge_inner.shape)
    moved_shared = moved[:, inner_edge_rows:].reshape(edge_shared.shape)

    window = inner_rows.shape[0] // slot_count
    inner_rows = inner_rows.reshape(slot_count, window, 2 * inner_here)
    shared_rows = shared_rows.reshape(slot_count, window, shared_rows.shape[1])
    gate_part = inner_rows[:, :, :inner_here]
    value_part = inner_rows[:, :, inner_here:]
    fresh_shared = shared_rows[:, :, : 2 * state_dim]
    head_index = lax.axis_index("head")
    step_raw = lax.dynamic_slice_in_dim(
        shared_rows[:, :, 2 * state_dim :], head_index * heads_here, heads_here, axis=2
    )
    edge_inner_out = new_edge(moved_inner, value_part, counts)
    edge_shared_out = new_edge(moved_shared, fresh_shared, counts)
    mixed_inner = depthwise(moved_inner, value_part, conv_inner, conv_inner_bias)
    mixed_shared = depthwise(moved_shared, fresh_shared, conv_shared, conv_shared_bias)
    valid = jnp.arange(window)[None, :] < counts[:, None]
    step_size = jax.nn.softplus(step_raw.astype(jnp.float32) + step_bias)
    step_size = jnp.where(valid[:, :, None], step_size, 0.0)
    decay = -jnp.exp(decay_log)
    entries = mixed_shared[:, :, :state_dim]
    readouts = mixed_shared[:, :, state_dim:]

    factor = jnp.exp(step_size * decay)
    cum = [factor[:, 0]]
    for t in range(1, window):
        cum.append(cum[-1] * factor[:, t])
    span = {}
    for t in range(window):
        span[(t, t)] = jnp.ones_like(factor[:, 0])
        for s in range(t - 1, -1, -1):
            span[(t, s)] = span[(t, s + 1)] * factor[:, s + 1]

    def per_head(v):
        return jnp.repeat(v, head_dim, axis=-1)

    flat_inputs = mixed_inner.reshape(slot_count, window, inner_here)
    weighted = per_head(step_size) * flat_inputs
    last = window - 1
    pushed = jnp.stack([per_head(span[(last, s)]) * weighted[:, s] for s in range(window)], axis=1)
    weight = jnp.concatenate([pushed, jnp.zeros_like(pushed)], axis=1)
    carry = jnp.pad(cum[last], ((0, 0), (0, state_dim - heads_here)))[:, None, :]
    mix = jnp.concatenate(
        [readouts, entries, carry, jnp.zeros((slot_count, 2 * window - 1, state_dim), jnp.float32)],
        axis=1,
    )
    read, states_out = recurrence(received, recv_rows, mix, weight, state_rows, heads_here)
    states_out = states_out.reshape(states.shape)
    overlap = jnp.einsum("rtn,rsn->rts", readouts, entries, precision=HIGH)
    skip_wide = jnp.repeat(skip_gain, head_dim)
    produced = []
    for t in range(window):
        acc = per_head(cum[t]) * read[:, t]
        for s in range(t + 1):
            acc = acc + per_head(span[(t, s)] * overlap[:, t, s, None]) * weighted[:, s]
        produced.append(acc + skip_wide * flat_inputs[:, t])
    outputs = jnp.stack(produced, axis=1)

    gated = outputs * jax.nn.silu(gate_part.astype(jnp.float32))
    square_part = jnp.sum(gated * gated, axis=-1).reshape(slot_count * window, 1)
    pre_scaled = (
        jnp.where(valid[:, :, None], gated * gate_gain, 0.0)
        .astype(jnp.bfloat16)
        .reshape(slot_count * window, inner_here)
    )
    partial = jnp.dot(pre_scaled, out_weight, preferred_element_type=jnp.float32)
    square_hi = square_part.astype(jnp.bfloat16)
    square_lo = (square_part - square_hi.astype(jnp.float32)).astype(jnp.bfloat16)
    extra = jnp.pad(
        jnp.concatenate([square_hi, square_lo], axis=1), ((0, 0), (0, 126))
    )
    reduced, squares = scatter_sum(
        [partial.astype(jnp.bfloat16), extra.astype(jnp.bfloat16)], lax.axis_size("head")
    )
    full_inner = inner_here * lax.axis_size("head")
    square_sum = squares[:, 0:1] + squares[:, 1:2]
    scale = lax.rsqrt(square_sum / full_inner + EPS)
    hidden_out = (rows_in + reduced * scale).astype(jnp.bfloat16)
    return (hidden_out, states_out, edge_inner_out, edge_shared_out)


def solution(mesh):
    placed = (
        P(("req", "head"), None),
        P(),
        P(None, None, "head"),
        P(),
        P(None, "head"),
        P("head"),
        P(),
        P(),
        P("head"),
        P("head"),
        P("head"),
        P("head"),
        P("head", None),
        P("req", "head", None, None),
        P("req", None, "head"),
        P("req", None, None),
        P("req"),
        P(),
        P(),
        P(),
    )
    return jax.shard_map(
        local,
        mesh=mesh,
        in_specs=placed,
        out_specs=(
            P(("req", "head"), None),
            P("req", "head", None, None),
            P("req", None, "head"),
            P("req", None, None),
        ),
        check_vma=False,
    )
```
